32 devices in a mesh: section: 2 (over x), shard: 4 (over y, core), replica: 4 (over z).
Axes of the slice: x: 2, y: 2, z: 4, core: 2. Of those that a mesh axis runs over, the one named last changes fastest.
Arguments:
- block_input: bfloat16 [2, 16, 218, 1536], P(None, ('shard', 'replica')), may hold values from -6 to 6
- modulation: float32 [2, 2, 16, 2, 6, 1536], P('section', None, ('shard', 'replica')), may hold values from -4 to 4
- w_qkv: bfloat16 [2, 2, 1536, 4608], P('section', None, 'shard'), may hold values from -0.15625 to 0.15625
- b_qkv: bfloat16 [2, 2, 4608], P('section', None, 'shard'), may hold values from -3 to 3
- qk_gain: bfloat16 [2, 2, 2, 64], P('section', None, None, 'shard'), may hold values from 0.099609375 to 1.8984375
- w_out: bfloat16 [2, 2, 1536, 1536], P('section', None, 'shard'), may hold values from -1.25 to 1.25
- b_out: bfloat16 [2, 2, 1536], P('section', None, 'shard'), may hold values from -3 to 3
- w_fc1: bfloat16 [2, 2, 1536, 6144], P('section', None, 'shard'), may hold values from -0.15625 to 0.15625
- b_fc1: bfloat16 [2, 2, 6144], P('section', None, 'shard'), may hold values from -3 to 3
- w_fc2: bfloat16 [2, 2, 6144, 1536], P('section', None, 'shard'), may hold values from -0.078125 to 0.078125
- b_fc2: bfloat16 [2, 2, 1536], P('section', None, 'shard'), may hold values from -3 to 3
- cotangent: bfloat16 [2, 16, 218, 1536], P(None, ('shard', 'replica')), may hold values from -6 to 6
Outputs:
- activations: bfloat16 [2, 2, 16, 218, 1536], P('section', None, ('shard', 'replica'))
- input_grads: float32 [2, 2, 16, 218, 1536], P('section', None, ('shard', 'replica'))
- modulation_grad: float32 [2, 2, 16, 2, 6, 1536], P('section', None, ('shard', 'replica'))
- w_qkv_grad: float32 [2, 2, 1536, 4608], P('section', None, ('shard', 'replica'))
- b_qkv_grad: float32 [2, 2, 4608], P('section', None, ('shard', 'replica'))
- qk_gain_grad: float32 [2, 2, 2, 64], P('section', None, None, ('shard', 'replica'))
- w_out_grad: float32 [2, 2, 1536, 1536], P('section', None, ('shard', 'replica'))
- b_out_grad: float32 [2, 2, 1536], P('section', None, ('shard', 'replica'))
- w_fc1_grad: float32 [2, 2, 1536, 6144], P('section', None, ('shard', 'replica'))
- b_fc1_grad: float32 [2, 2, 6144], P('section', None, ('shard', 'replica'))
- w_fc2_grad: float32 [2, 2, 6144, 1536], P('section', None, ('shard', 'replica'))
- b_fc2_grad: float32 [2, 2, 1536], P('section', None, ('shard', 'replica'))
The draws below stay inside these ranges and needn't reach their ends.
All inputs are finite; a program needn't handle non-finite values.
Results may differ from the reference program's by a relative error of at most 0.017.
Values may be sent and summed in bfloat16 or wider, within the bound.
No kernel may reach another device: no remote copies, remote signals or barrier semaphores. Data moves between devices by JAX's collectives and lax.ppermute only.
A program may use at most 704 MiB of HBM per device.

```python
import jax
import jax.numpy as jnp
from jax import lax

D = 1536
HEADS = 24
HD = 64
FF = 6144
IMG = 64
MB = 2
LEN = 218
SEQS = 16
N_SECTION = 2


def shard_levels(own_key, shape, shards, smallest, top_value):
    loudness = 1.0
    for position, blocks in shards:
        draws = jax.random.uniform(jax.random.fold_in(jax.random.fold_in(own_key, 6), position), (blocks,), jnp.float32, smallest / len(shards), top_value / len(shards))
        loudness = loudness * jnp.repeat(jnp.exp(draws), shape[position] // blocks).reshape((-1,) + (1,) * (len(shape) - 1 - position))
    return loudness


def gaussian(key, dims, width, reach, cuts=(), dtype=jnp.bfloat16):
    entries = width * jax.random.normal(key, dims, jnp.float32)
    if cuts:
        entries = entries * shard_levels(key, dims, cuts, -0.22, 0.18)
    return jnp.clip(entries, -reach, reach).astype(dtype)


def setup_inputs(seed: int = 0) -> dict:
    seeds = jax.random.split(jax.random.key(seed), 13)
    block_input = gaussian(seeds[0], (MB, SEQS, LEN, D), 1.0, 6.0, ((1, 16),))
    modulation = gaussian(seeds[1], (N_SECTION, MB, SEQS, 2, 6, D), 1.0, 4.0, ((0, 2), (2, 16)), jnp.float32)
    w_qkv = gaussian(seeds[2], (N_SECTION, 2, D, 3 * D), D ** -0.5, 0.15625, ((0, 2), (2, 4)))
    b_qkv = gaussian(seeds[3], (N_SECTION, 2, 3 * D), 0.5, 3.0, ((0, 2), (2, 4)))
    qk_gain = jnp.clip(1.0 + 0.18 * jax.random.normal(seeds[4], (N_SECTION, 2, 2, HD), jnp.float32), 0.099609375, 1.8984375).astype(jnp.bfloat16)
    w_out = gaussian(seeds[5], (N_SECTION, 2, D, D), (D // 64) ** -0.5, 1.25, ((0, 2), (2, 4)))
    b_out = gaussian(seeds[6], (N_SECTION, 2, D), 0.5, 3.0, ((0, 2), (2, 4)))
    w_fc1 = gaussian(seeds[7], (N_SECTION, 2, D, FF), D ** -0.5, 0.15625, ((0, 2), (2, 4)))
    b_fc1 = gaussian(seeds[8], (N_SECTION, 2, FF), 0.5, 3.0, ((0, 2), (2, 4)))
    w_fc2 = gaussian(seeds[9], (N_SECTION, 2, FF, D), FF ** -0.5, 0.078125, ((0, 2), (2, 4)))
    b_fc2 = gaussian(seeds[10], (N_SECTION, 2, D), 0.5, 3.0, ((0, 2), (2, 4)))
    cotangent = gaussian(seeds[11], (MB, SEQS, LEN, D), 1.0, 6.0, ((1, 16),))
    return {"block_input": block_input, "modulation": modulation, "w_qkv": w_qkv, "b_qkv": b_qkv, "qk_gain": qk_gain, "w_out": w_out, "b_out": b_out, "w_fc1": w_fc1, "b_fc1": b_fc1, "w_fc2": w_fc2, "b_fc2": b_fc2, "cotangent": cotangent}


@jax.custom_vjp
def low(v):
    return lax.optimization_barrier(v.astype(jnp.bfloat16)).astype(jnp.float32)

@jax.custom_vjp
def low_back(v):
    return v

def low_keep(v):
    return (low(v), None)

def low_pass(kept, grad):
    return (grad,)

def back_keep(v):
    return (v, None)

def back_low(kept, grad):
    return (low(grad),)
low.defvjp(low_keep, low_pass)
low_back.defvjp(back_keep, back_low)
norm_eps = 1e-06
highest = lax.Precision.HIGHEST

def head_norm(values, head_gain):
    return values * lax.rsqrt(lax.optimization_barrier(jnp.mean(values * values, -1, keepdims=True)) + norm_eps) * head_gain

def layer_norm_mod(segment, shift_row, scale_row):
    centred = segment - lax.optimization_barrier(jnp.mean(segment, -1, keepdims=True))
    normed = centred * lax.rsqrt(lax.optimization_barrier(jnp.mean(centred * centred, -1, keepdims=True)) + norm_eps)
    return normed * (1.0 + scale_row) + shift_row

def one_layer(section_in, modul_seq, layer_params):
    projection_weight, b_proj, gain_set, backward_weight, b_back, w_up, b_up, w_down, b_down = layer_params
    stream_bounds = ((0, IMG), (IMG, LEN))
    query_list, key_list, value_list = ([], [], [])
    for token_stream in range(2):
        row_start, row_stop = stream_bounds[token_stream]
        segment = section_in[row_start:row_stop]
        hidden_state = low(layer_norm_mod(segment, modul_seq[token_stream, 0], modul_seq[token_stream, 1]))
        projected = low_back(jnp.dot(hidden_state, projection_weight[token_stream], precision=highest) + b_proj[token_stream])
        shaped = projected.reshape(row_stop - row_start, 3, HEADS, HD)
        query_list.append(low(head_norm(shaped[:, 0], gain_set[token_stream, 0])))
        key_list.append(low(head_norm(shaped[:, 1], gain_set[token_stream, 1])))
        value_list.append(low(shaped[:, 2]))
    query_all = jnp.concatenate(query_list, 0)
    key_all = jnp.concatenate(key_list, 0)
    value_all = jnp.concatenate(value_list, 0)
    scores = low_back(jnp.einsum('qhd,khd->hqk', query_all, key_all, precision=highest) * HD ** (-0.5))
    exponent = jnp.exp(scores)
    soft_weights = low(exponent / lax.optimization_barrier(jnp.sum(exponent, -1, keepdims=True)))
    attended = jnp.einsum('hqk,khd->qhd', soft_weights, value_all, precision=highest).reshape(LEN, D)
    attended = low(low_back(attended))
    mixed_list = []
    for token_stream in range(2):
        row_start, row_stop = stream_bounds[token_stream]
        branch = low_back(jnp.dot(attended[row_start:row_stop], backward_weight[token_stream], precision=highest) + b_back[token_stream])
        mixed_list.append(section_in[row_start:row_stop] + modul_seq[token_stream, 2] * branch)
    mixed = jnp.concatenate(mixed_list, 0)
    final_list = []
    for token_stream in range(2):
        row_start, row_stop = stream_bounds[token_stream]
        segment = mixed[row_start:row_stop]
        hidden_mlp = low(layer_norm_mod(segment, modul_seq[token_stream, 3], modul_seq[token_stream, 4]))
        pre_act = low_back(jnp.dot(hidden_mlp, w_up[token_stream], precision=highest) + b_up[token_stream])
        activated = low(jax.nn.gelu(pre_act, approximate=True))
        mlp_out = low_back(jnp.dot(activated, w_down[token_stream], precision=highest) + b_down[token_stream])
        final_list.append(segment + modul_seq[token_stream, 5] * mlp_out)
    return jnp.concatenate(final_list, 0)

def reference(block_input, modulation, w_qkv, b_qkv, qk_gain, w_out, b_out, w_fc1, b_fc1, w_fc2, b_fc2, cotangent):
    seq_total = MB * SEQS
    inputs = block_input.astype(jnp.float32).reshape(seq_total, LEN, D)
    modul_all = modulation.reshape(N_SECTION, seq_total, 2, 6, D)
    params = (w_qkv.astype(jnp.float32), b_qkv.astype(jnp.float32), qk_gain.astype(jnp.float32), w_out.astype(jnp.float32), b_out.astype(jnp.float32), w_fc1.astype(jnp.float32), b_fc1.astype(jnp.float32), w_fc2.astype(jnp.float32), b_fc2.astype(jnp.float32))
    middle = jnp.zeros_like(inputs)

    def whole_model(inputs, middle, modul_all, params):

        def run_section(section_id, section_rows):
            layer_params = tuple((member[section_id] for member in params))

            def one_seq(carried, element):
                seq_in, seq_mod = element
                layer_out = jax.checkpoint(one_layer)(seq_in, seq_mod, layer_params)
                return (carried, layer_out)
            _, results = lax.scan(one_seq, jnp.float32(0.0), (section_rows, modul_all[section_id]))
            return results
        first_out = run_section(0, inputs)
        second_out = run_section(1, low(low_back(first_out)) + middle)
        return (first_out, second_out)
    (first_out, second_out), pullback = jax.vjp(whole_model, inputs, middle, modul_all, params)
    seed_grad = cotangent.astype(jnp.float32).reshape(seq_total, LEN, D)
    input_grad, middle_grad, modul_grad, param_grads = pullback((jnp.zeros_like(first_out), seed_grad))
    shape_out = (N_SECTION, MB, SEQS, LEN, D)
    activations = jnp.stack([first_out, second_out]).astype(jnp.bfloat16).reshape(shape_out)
    input_grads = jnp.stack([input_grad, middle_grad]).reshape(shape_out)
    return (activations, input_grads, modul_grad.reshape(modulation.shape), param_grads[0], param_grads[1], param_grads[2], param_grads[3], param_grads[4], param_grads[5], param_grads[6], param_grads[7], param_grads[8])
```

```python
import jax
import jax.numpy as jnp
from jax import lax
from jax.sharding import PartitionSpec as P

IMG = 64
norm_eps = 1e-06
BF = jnp.bfloat16
F32 = jnp.float32


def dot(spec, a, b):
    return jnp.einsum(spec, a, b, preferred_element_type=F32)


def near(x):
    return lax.ppermute(x, "shard", [(i, i ^ 1) for i in range(4)])


def far(x):
    return lax.ppermute(x, "shard", [(i, i ^ 2) for i in range(4)])


def across(x):
    return lax.ppermute(x, "shard", [(i, i ^ 3) for i in range(4)])


def mate(x):
    count = lax.axis_size("replica")
    return lax.ppermute(x, "replica", [(i, i ^ 1) for i in range(count)])


def gather_two(x):
    return jnp.concatenate([x, near(x)], 0)


def gather_four(x):
    other = far(x)
    return jnp.concatenate([x, near(x), other, near(other)], 0)


def scatter_two(parts):
    own = parts.shape[0] // 2
    return parts[:own] + near(parts[own:].astype(BF)).astype(F32)


def scatter_four(parts):
    own = parts.shape[0] // 4
    away = parts[2 * own : 3 * own] + near(parts[3 * own :].astype(BF)).astype(F32)
    away = far(away.astype(BF))
    here = parts[:own] + near(parts[own : 2 * own].astype(BF)).astype(F32)
    return here + away.astype(F32)


def normalise(x):
    centred = x - jnp.mean(x, -1, keepdims=True)
    inverse = lax.rsqrt(jnp.mean(centred * centred, -1, keepdims=True) + norm_eps)
    return centred * inverse, inverse


def normalise_back(f, normed, inverse):
    return inverse * (
        f - jnp.mean(f, -1, keepdims=True) - normed * jnp.mean(f * normed, -1, keepdims=True)
    )


gelu_a = (2.0 / jnp.pi) ** 0.5
gelu_b = 0.044715


def gelu(v):
    return 0.5 * v * (1.0 + jnp.tanh(gelu_a * (v + gelu_b * v * v * v)))


def gelu_slope(v):
    t = jnp.tanh(gelu_a * (v + gelu_b * v * v * v))
    return 0.5 * (1.0 + t) + 0.5 * v * (1.0 - t * t) * gelu_a * (1.0 + 3.0 * gelu_b * v * v)


def split_rows(x):
    return (x[:, :IMG], x[:, IMG:])


def key_mask(length, padded):
    return jnp.where(jnp.arange(padded) < length, 0.0, -1e30).astype(F32)


def attention(u, gains, length):
    queries, keys, values = [], [], []
    for st in range(2):
        pair = u[st][:, :, :2]
        normed = pair * lax.rsqrt(jnp.mean(pair * pair, -1, keepdims=True) + norm_eps)
        normed = (normed * gains[st][:, None, :]).astype(BF)
        queries.append(normed[:, :, 0])
        keys.append(normed[:, :, 1])
        values.append(u[st][:, :, 2].astype(BF))
    q, k, v = (jnp.concatenate(t, 1) for t in (queries, keys, values))
    n, padded, heads, hd = q.shape
    scores = dot("sqhd,skhd->shqk", q, k) * hd**-0.5 + key_mask(length, padded)
    exponent = jnp.exp(scores)
    total = jnp.sum(exponent, -1, keepdims=True)
    probs = (exponent / total).astype(BF)
    attended = dot("shqk,skhd->sqhd", probs, v).astype(BF)
    return attended.reshape(n, padded, heads * hd), (q, k, v, jnp.log(total))


def attention_back(attended_grad, u, gains, saved, length):
    q, k, v, log_total = saved
    n, padded, heads, hd = q.shape
    scale = hd**-0.5
    scores = dot("sqhd,skhd->shqk", q, k) * scale + key_mask(length, padded)
    exact = jnp.exp(scores - log_total)
    grad = attended_grad.reshape(n, padded, heads, hd)
    value_grad = dot("shqk,sqhd->skhd", exact.astype(BF), grad)
    prob_grad = dot("sqhd,skhd->shqk", grad, v)
    delta = jnp.sum(prob_grad * exact, -1, keepdims=True)
    score_grad = (exact * (prob_grad - delta)).astype(BF)
    query_grad = dot("shqk,skhd->sqhd", score_grad, k) * scale
    key_grad = dot("shqk,sqhd->skhd", score_grad, q) * scale
    projected_grad, gain_grad = [], []
    for st, part in enumerate(zip(split_rows(query_grad), split_rows(key_grad), split_rows(value_grad))):
        pair = u[st][:, :, :2]
        t = jnp.stack(part[:2], 2)
        r = lax.rsqrt(jnp.mean(pair * pair, -1, keepdims=True) + norm_eps)
        g = gains[st][:, None, :]
        back = r * g * t - pair * (r * r * r) * jnp.mean(pair * g * t, -1, keepdims=True)
        gain_grad.append(jnp.sum(t * pair * r, (0, 1, 3)))
        whole = jnp.concatenate([back, part[2][:, :, None]], 2).astype(BF)
        projected_grad.append(whole.reshape(n, whole.shape[1], 3 * heads * hd))
    return projected_grad, gain_grad


def forward(x, mod, w, length):
    us, mixeds, saved = [], [], {}
    keep = {"x": x, "mod": mod}
    hidden = []
    hd = w["gain"].shape[-1]
    for st in range(2):
        normed, _ = normalise(x[st].astype(F32))
        h = (normed * (1.0 + mod[:, st, 1][:, None]) + mod[:, st, 0][:, None]).astype(BF)
        h = gather_two(h)
        hidden.append(h)
        p = dot("nrd,dk->nrk", h, w["qkv"][st]) + w["b_qkv"][st]
        us.append(p.reshape(p.shape[0], p.shape[1], 3, -1, hd))
    keep["hidden"], keep["u"] = hidden, us
    attended, keep["att"] = attention(us, w["gain"], length)
    attended = split_rows(attended)
    keep["attended"] = attended
    keep["branch"], keep["mixed"], keep["hidden_mlp"], keep["pre"], keep["act"], keep["mlp"] = [], [], [], [], [], []
    outs = []
    for st in range(2):
        branch = scatter_two(dot("nrk,kd->nrd", attended[st], w["out"][st])) + w["b_out"][st]
        mixed = x[st].astype(F32) + mod[:, st, 2][:, None] * branch
        normed, _ = normalise(mixed)
        h = (normed * (1.0 + mod[:, st, 4][:, None]) + mod[:, st, 3][:, None]).astype(BF)
        h = gather_four(h)
        pre = dot("nrd,df->nrf", h, w["fc1"][st]) + w["b_fc1"][st]
        act = gelu(pre).astype(BF)
        mlp = scatter_four(dot("nrf,fd->nrd", act, w["fc2"][st])) + w["b_fc2"][st]
        outs.append(mixed + mod[:, st, 5][:, None] * mlp)
        for name, value in (("branch", branch), ("mixed", mixed), ("hidden_mlp", h), ("pre", pre), ("act", act), ("mlp", mlp)):
            keep[name].append(value)
    return outs, keep


def backward(up, keep, w, length):
    mod = keep["mod"]
    mixed_grads, late, right, small = [], [], {}, {}
    right["mlp"], right["pre"], right["branch"] = [], [], []
    attended_grads, gates = [], []
    small["fc2"], small["fc1"], small["out"] = [], [], []
    for st in range(2):
        mlp_grad = (mod[:, st, 5][:, None] * up[st]).astype(BF)
        small["fc2"].append(jnp.sum(mlp_grad.astype(F32), (0, 1)))
        gate = jnp.sum(keep["mlp"][st] * up[st], 1)
        mlp_grad = gather_four(mlp_grad)
        act_grad = dot("nrd,fd->nrf", mlp_grad, w["fc2"][st])
        pre_grad = (act_grad * gelu_slope(keep["pre"][st])).astype(BF)
        small["fc1"].append(jnp.sum(pre_grad.astype(F32), (0, 1)))
        h_grad = scatter_four(dot("nrf,df->nrd", pre_grad, w["fc1"][st]))
        normed, inverse = normalise(keep["mixed"][st])
        mixed_grad = up[st] + normalise_back(h_grad * (1.0 + mod[:, st, 4][:, None]), normed, inverse)
        late.append((jnp.sum(h_grad, 1), jnp.sum(h_grad * normed, 1), gate))
        mixed_grads.append(mixed_grad)
        right["mlp"].append(mlp_grad)
        right["pre"].append(pre_grad)
        branch_grad = (mod[:, st, 2][:, None] * mixed_grad).astype(BF)
        gates.append(jnp.sum(keep["branch"][st] * mixed_grad, 1))
        small["out"].append(jnp.sum(branch_grad.astype(F32), (0, 1)))
        branch_grad = gather_two(branch_grad)
        right["branch"].append(branch_grad)
        attended_grads.append(dot("nrd,kd->nrk", branch_grad, w["out"][st]).astype(BF))
    attended_grad = jnp.concatenate(attended_grads, 1)
    right["qkv"], small["gain"] = attention_back(attended_grad, keep["u"], w["gain"], keep["att"], length)
    small["qkv"] = [jnp.sum(t.astype(F32), (0, 1)) for t in right["qkv"]]
    input_grads, mod_grads = [], []
    for st in range(2):
        h_grad = scatter_two(dot("nrk,dk->nrd", right["qkv"][st], w["qkv"][st]))
        normed, inverse = normalise(keep["x"][st].astype(F32))
        input_grads.append(mixed_grads[st] + normalise_back(h_grad * (1.0 + mod[:, st, 1][:, None]), normed, inverse))
        mod_grads.append(jnp.stack([jnp.sum(h_grad, 1), jnp.sum(h_grad * normed, 1), gates[st], *late[st]], 1))
    return input_grads, jnp.stack(mod_grads, 1), small, right


def place(pieces, slots, count):
    whole = jnp.zeros((count,) + pieces[0].shape, pieces[0].dtype)
    for piece, slot in zip(pieces, slots):
        whole = lax.dynamic_update_index_in_dim(whole, piece, slot, 0)
    return whole


def take(x, index, axis):
    return lax.dynamic_index_in_dim(x, index, axis, keepdims=False)


def halves(mine, parity):
    direct = far(take(mine, parity, 0))
    relayed = mate(direct)
    return tuple(jnp.where(parity == st, direct, relayed) for st in range(2))


def prepare(w_qkv, b_qkv, gain, w_out, b_out, w_fc1, b_fc1, w_fc2, b_fc2):
    sid = lax.axis_index("shard")
    core = sid % 2
    parity = lax.axis_index("replica") % 2
    rows, width = w_qkv.shape[1], w_qkv.shape[2]
    part = width // 12
    vectors = (b_qkv, b_out, b_fc1, b_fc2, gain.reshape(2, -1))
    packed = lax.all_gather(jnp.concatenate(vectors, 1), "shard", axis=0)
    unpacked, at = [], 0
    for vector in vectors:
        piece = packed[:, :, at : at + vector.shape[1]].astype(F32)
        at += vector.shape[1]
        unpacked.append(piece)
    flat = [jnp.swapaxes(piece, 0, 1).reshape(2, -1) for piece in unpacked[:4]]
    hd = gain.shape[2] * 4
    gains = jnp.transpose(unpacked[4].reshape(4, 2, 2, -1), (1, 2, 0, 3)).reshape(2, 2, hd)
    w = {"gain": gains, "b_out": flat[1], "b_fc2": flat[3], "b_fc1": b_fc1.astype(F32)}
    w["b_qkv"] = take(flat[0].reshape(2, 3, 2, 2, part), core, 3).reshape(2, 3 * 2 * part)
    heads = w_qkv.reshape(2, rows, 3, 2, 2, part)
    own = take(heads, core, 4)
    beside = near(take(heads, 1 - core, 4))
    qkv_parts = []
    for j in range(3):
        far_own = halves(own[:, :, j], parity)
        far_beside = halves(beside[:, :, j], parity)
        qkv_parts.append((far_own, far_beside))
    slots = (sid, sid ^ 1, sid ^ 2, sid ^ 3)
    w["qkv"] = []
    for st in range(2):
        far_own = jnp.stack([qkv_parts[j][0][st] for j in range(3)], 1)
        far_beside = jnp.stack([qkv_parts[j][1][st] for j in range(3)], 1)
        whole = place((own[st], beside[st], far_own, far_beside), slots, 4)
        w["qkv"].append(whole.reshape(4 * rows, 3 * 2 * part))
    far_out = halves(w_out, parity)
    row_pair = sid // 2
    w["out"] = [
        place((w_out[st], far_out[st]), (row_pair, 1 - row_pair), 2).reshape(2 * rows, -1) for st in range(2)
    ]
    columns = w_fc1.reshape(2, rows, 4, -1)
    blocks = [take(columns, slots[j], 2) for j in range(4)]
    beside = near(blocks[1])
    behind = [blocks[2], blocks[3]]
    behind, far_out = lax.optimization_barrier((behind, far_out))
    direct = [far(take(behind[0], parity, 0)), across(take(behind[1], parity, 0))]
    relayed = [mate(t) for t in direct]
    w["fc1"] = []
    for st in range(2):
        away = [jnp.where(parity == st, d, m) for d, m in zip(direct, relayed)]
        w["fc1"].append(place((blocks[0][st], beside[st], *away), slots, 4).reshape(4 * rows, -1))
    w["fc2"] = [w_fc2[0], w_fc2[1]]
    return w


def weight_terms(left, right):
    total = None
    for a, b in zip(left, right):
        term = dot("nrd,nre->de", a, b)
        total = term if total is None else total + term
    return total


def over_replicas(x):
    return lax.psum_scatter(x, "replica", scatter_dimension=0, tiled=True)


def per_device(block_input, modulation, w_qkv, b_qkv, qk_gain, w_out, b_out, w_fc1, b_fc1, w_fc2, b_fc2, cotangent):
    section = lax.axis_index("section")
    first = section == 0
    sid = lax.axis_index("shard")
    core, row_pair = sid % 2, sid // 2
    count = lax.axis_size("replica")
    rid = lax.axis_index("replica")
    length = block_input.shape[2]
    padded = (length + 15) // 16 * 16
    w = prepare(w_qkv[0], b_qkv[0], qk_gain[0], w_out[0], b_out[0], w_fc1[0], b_fc1[0], w_fc2[0], b_fc2[0])

    def padding(x):
        return jnp.pad(x, ((0, 0), (0, 0), (0, padded - length), (0, 0)))

    def streams(x):
        return list(split_rows(x))

    def choose(a, b):
        return jax.tree.map(lambda p, q: jnp.where(first, p, q), a, b)

    def relay(x, pairs):
        return [lax.ppermute(t.astype(BF), "section", pairs) for t in x]

    block_input = padding(block_input)
    cotangent = padding(cotangent)
    mod = modulation[0]
    middle_mod = jnp.where(first, mod[1], mod[0])
    up_pair, down_pair = [(0, 1)], [(1, 0)]

    out0, keep0 = forward(streams(block_input[0]), mod[0], w, length)
    got = relay(out0, up_pair)
    out1, keep1 = forward(choose(streams(block_input[1]), got), middle_mod, w, length)
    got = relay(out1, up_pair)
    out2, keep2 = forward(got, mod[1], w, length)

    def zero_unless(cond, x):
        return [jnp.where(cond, t.astype(F32), 0.0) for t in x]

    grad0, mod_grad0, small0, right0 = backward(zero_unless(~first, streams(cotangent[0])), keep1, w, length)
    got = relay(grad0, down_pair)
    up = choose([t.astype(F32) for t in got], [t.astype(F32) for t in streams(cotangent[1])])
    keep_mid = choose(keep0, keep2)
    grad1, mod_grad1, small1, right1 = backward(up, keep_mid, w, length)
    got = relay(grad1, down_pair)
    grad2, mod_grad2, small2, right2 = backward(zero_unless(first, got), keep1, w, length)

    ends = choose(right2, right0)

    def terms(left, right, st):
        return weight_terms((keep_mid[left][st], keep1[left][st]), (right1[right][st], ends[right][st])).astype(BF)

    fc2 = jnp.stack([over_replicas(terms("act", "mlp", st)) for st in range(2)]).astype(F32)
    fc1 = []
    for st in range(2):
        t = terms("hidden_mlp", "pre", st)
        d, cols = t.shape
        t = jnp.swapaxes(t.reshape(4, count, -1, cols), 0, 1).reshape(d, cols)
        fc1.append(over_replicas(t).reshape(4, -1, cols))
    fc1 = jnp.stack(fc1, 1)
    own = take(fc1, sid, 0)
    moved = [own] + [send(take(fc1, sid ^ j, 0)) for j, send in ((1, near), (2, far), (3, across))]
    fc1 = place(moved, [sid ^ j for j in range(4)], 4)
    fc1 = jnp.transpose(fc1, (1, 2, 0, 3)).reshape(2, fc1.shape[2], -1).astype(F32)

    out, qkv = [], []
    for st in range(2):
        t = terms("attended", "branch", st)
        t = t.reshape(2, -1, t.shape[1])
        t = take(t, row_pair, 0).astype(F32) + far(take(t, 1 - row_pair, 0)).astype(F32)
        out.append(over_replicas(t.astype(BF)))
    out = jnp.stack(out).astype(F32)
    for st in range(2):
        t = terms("hidden", "qkv", st)
        cols = t.shape[1]
        t = t.reshape(2, -1, cols)
        t = take(t, row_pair, 0).astype(F32) + far(take(t, 1 - row_pair, 0)).astype(F32)
        t = jnp.swapaxes(t.astype(BF).reshape(2, count, -1, cols), 0, 1).reshape(-1, cols)
        qkv.append(over_replicas(t).reshape(2, -1, cols))
    qkv = jnp.stack(qkv, 1)
    own = take(qkv, core, 0)
    other = near(take(qkv, 1 - core, 0))
    qkv = place((own, other), (core, 1 - core), 2)
    rows = qkv.shape[2]
    qkv = qkv.reshape(2, 2, rows, 6, -1)
    qkv = jnp.transpose(qkv, (1, 2, 3, 0, 4)).reshape(2, rows, -1).astype(F32)

    small = jax.tree.map(lambda a, b, c: a + b + c, small0, small1, small2)
    pieces = []
    for st in range(2):
        cores = small["qkv"][st].reshape(6, 1, -1)
        cores = jnp.where(jnp.arange(2).reshape(1, 2, 1) == core, cores, 0.0).reshape(-1)
        quarter = small["fc1"][st].reshape(1, -1)
        quarter = jnp.where(jnp.arange(4).reshape(4, 1) == sid, quarter, 0.0).reshape(-1)
        pieces.append(jnp.concatenate([cores, small["out"][st], quarter, small["fc2"][st], small["gain"][st].reshape(-1)]))
    sizes = [w_qkv.shape[3], w_out.shape[3], w_fc1.shape[3], w_fc2.shape[3], 2 * w["gain"].shape[-1]]
    summed = lax.psum(jnp.stack(pieces), ("shard", "replica"))
    place_id = sid * count + rid
    vectors, at = [], 0
    for size in sizes:
        vectors.append(summed[:, at : at + size])
        at += size

    def own_block(x, axis):
        size = x.shape[axis] // (4 * count)
        return lax.dynamic_slice_in_dim(x, place_id * size, size, axis)

    blocks = [own_block(v, 1)[None] for v in vectors[:4]]
    gain = own_block(vectors[4].reshape(2, 2, -1), 2)[None]

    def joined(x):
        return jnp.concatenate(x, 1)[:, :length]

    activations = jnp.stack([joined(choose(out0, out1)), joined(choose(out1, out2))]).astype(BF)
    input_grads = jnp.stack([joined(choose(grad1, grad0)), joined(choose(grad2, grad1))])
    modulation_grad = jnp.stack([choose(mod_grad1, mod_grad0), choose(mod_grad2, mod_grad1)])
    return (
        activations[None],
        input_grads[None],
        modulation_grad[None],
        qkv[None],
        blocks[0],
        gain,
        out[None],
        blocks[1],
        fc1[None],
        blocks[2],
        fc2[None],
        blocks[3],
    )


def solution(mesh):
    every = ("shard", "replica")
    return jax.shard_map(
        per_device,
        mesh=mesh,
        in_specs=(
            P(None, every, None, None),
            P("section", None, every, None, None, None),
            P("section", None, "shard", None),
            P("section", None, "shard"),
            P("section", None, None, "shard"),
            P("section", None, "shard", None),
            P("section", None, "shard"),
            P("section", None, "shard", None),
            P("section", None, "shard"),
            P("section", None, "shard", None),
            P("section", None, "shard"),
            P(None, every, None, None),
        ),
        out_specs=(
            P("section", None, every, None, None),
            P("section", None, every, None, None),
            P("section", None, every, None, None, None),
            P("section", None, every, None),
            P("section", None, every),
            P("section", None, None, every),
            P("section", None, every, None),
            P("section", None, every),
            P("section", None, every, None),
            P("section", None, every),
            P("section", None, every, None),
            P("section", None, every),
        ),
        check_vma=False,
    )
```

```python
import functools

import jax
import jax.numpy as jnp
from jax import lax
from jax.experimental import pallas as pl
from jax.experimental.pallas import tpu as pltpu
from jax.sharding import PartitionSpec as P

IMG = 64
norm_eps = 1e-06
BF = jnp.bfloat16
F32 = jnp.float32


def dot(spec, a, b):
    return jnp.einsum(spec, a, b, preferred_element_type=F32)


def near(x):
    return lax.ppermute(x, "shard", [(i, i ^ 1) for i in range(4)])


def far(x):
    return lax.ppermute(x, "shard", [(i, i ^ 2) for i in range(4)])


def across(x):
    return lax.ppermute(x, "shard", [(i, i ^ 3) for i in range(4)])


def mate(x):
    count = lax.axis_size("replica")
    return lax.ppermute(x, "replica", [(i, i ^ 1) for i in range(count)])


def gather_two(x):
    return jnp.concatenate([x, near(x)], 0)


def gather_four(x):
    other = far(x)
    return jnp.concatenate([x, near(x), other, near(other)], 0)


def scatter_two(parts):
    own = parts.shape[0] // 2
    return parts[:own] + near(parts[own:].astype(BF)).astype(F32)


def scatter_four(parts):
    own = parts.shape[0] // 4
    away = parts[2 * own : 3 * own] + near(parts[3 * own :].astype(BF)).astype(F32)
    away = far(away.astype(BF))
    here = parts[:own] + near(parts[own : 2 * own].astype(BF)).astype(F32)
    return here + away.astype(F32)


def normalise(x):
    centred = x - jnp.mean(x, -1, keepdims=True)
    inverse = lax.rsqrt(jnp.mean(centred * centred, -1, keepdims=True) + norm_eps)
    return centred * inverse, inverse


def normalise_back(f, normed, inverse):
    return inverse * (
        f - jnp.mean(f, -1, keepdims=True) - normed * jnp.mean(f * normed, -1, keepdims=True)
    )


gelu_a = (2.0 / jnp.pi) ** 0.5
gelu_b = 0.044715


def gelu(v):
    return 0.5 * v * (1.0 + jnp.tanh(gelu_a * (v + gelu_b * v * v * v)))


def gelu_slope(v):
    t = jnp.tanh(gelu_a * (v + gelu_b * v * v * v))
    return 0.5 * (1.0 + t) + 0.5 * v * (1.0 - t * t) * gelu_a * (1.0 + 3.0 * gelu_b * v * v)


def split_rows(x):
    return (x[:, :IMG], x[:, IMG:])


def lanes_of(hd):
    return lax.broadcasted_iota(jnp.int32, (1, 2 * hd), 1) < hd


def head_sums(x, low):
    a = jnp.sum(jnp.where(low, x, 0.0), -1, keepdims=True)
    b = jnp.sum(jnp.where(low, 0.0, x), -1, keepdims=True)
    return jnp.where(low, a, b)


def rows_of(first, second, at, width):
    return jnp.concatenate([first[0, :, pl.ds(at, width)], second[0, :, pl.ds(at, width)]], 0)


def dot_rows(a, b):
    return lax.dot_general(a, b, (((1,), (1,)), ((), ())), preferred_element_type=F32)


def dot_plain(a, b):
    return lax.dot_general(a, b, (((1,), (0,)), ((), ())), preferred_element_type=F32)


def dot_turned(a, b):
    return lax.dot_general(a, b, (((0,), (0,)), ((), ())), preferred_element_type=F32)


def pair_state(ui, ut, gains, at, model, hd, low, first_rows):
    wide = 2 * hd
    q_u, k_u, v_u = (rows_of(ui, ut, j * model + at, wide) for j in range(3))
    state = []
    for j, u in enumerate((q_u, k_u)):
        g = jnp.where(first_rows, gains[j : j + 1, :], gains[j + 2 : j + 3, :])
        r = lax.rsqrt(head_sums(u * u, low) / hd + norm_eps)
        state.append((u, g, r, (u * r * g).astype(BF)))
    return state[0], state[1], v_u.astype(BF)


def head_probs(q, k, low, bias, scale):
    scores = dot_rows(jnp.where(low, q, jnp.zeros_like(q)), k) * scale + bias
    exponent = jnp.exp(scores)
    return exponent / jnp.sum(exponent, -1, keepdims=True)


def row_kinds(image, padded, length):
    first_rows = lax.broadcasted_iota(jnp.int32, (padded, 1), 0) < image
    keys = lax.broadcasted_iota(jnp.int32, (1, padded), 1)
    return first_rows, jnp.where(keys < length, 0.0, -1e30).astype(F32)


def attention_kernel(ui, ut, gains, oi, ot, *, length, hd, pairs):
    image = ui.shape[1]
    padded = image + ut.shape[1]
    model = pairs * 2 * hd
    low = lanes_of(hd)
    first_rows, bias = row_kinds(image, padded, length)
    scale = hd**-0.5

    def one(at):
        (_, _, _, q), (_, _, _, k), v = pair_state(ui, ut, gains, at, model, hd, low, first_rows)
        both = []
        for mask in (low, jnp.logical_not(low)):
            probs = head_probs(q, k, mask, bias, scale).astype(BF)
            both.append(dot_plain(probs, v))
        out = jnp.where(low, both[0], both[1]).astype(BF)
        oi[0, :, pl.ds(at, 2 * hd)] = out[:image]
        ot[0, :, pl.ds(at, 2 * hd)] = out[image:]

    def step(i, carry):
        for j in range(2):
            one(pl.multiple_of((2 * i + j) * 2 * hd, 2 * hd))
        return carry

    lax.fori_loop(0, pairs // 2, step, 0)


def attention_back_kernel(ui, ut, gi, gt, gains, pi, pt, sums, gain_sums, *, length, hd, pairs):
    image = ui.shape[1]
    padded = image + ut.shape[1]
    wide = 2 * hd
    model = pairs * wide
    low = lanes_of(hd)
    first_rows, bias = row_kinds(image, padded, length)
    scale = hd**-0.5

    def one(at):
        (q_u, q_g, q_r, q), (k_u, k_g, k_r, k), v = pair_state(ui, ut, gains, at, model, hd, low, first_rows)
        grad = rows_of(gi, gt, at, wide)
        dqs, dks, dvs = [], [], []
        for mask in (low, jnp.logical_not(low)):
            probs = head_probs(q, k, mask, bias, scale)
            prob_grad = dot_rows(jnp.where(mask, grad, jnp.zeros_like(grad)), v)
            delta = jnp.sum(prob_grad * probs, -1, keepdims=True)
            score_grad = (probs * (prob_grad - delta)).astype(BF)
            dvs.append(dot_turned(probs.astype(BF), grad))
            dqs.append(dot_plain(score_grad, k))
            dks.append(dot_turned(score_grad, q))
        gain_rows = []
        for j, (u, g, r, pair) in enumerate(((q_u, q_g, q_r, dqs), (k_u, k_g, k_r, dks), (None, None, None, dvs))):
            t = jnp.where(low, pair[0], pair[1])
            if j < 2:
                t = t * scale
                grown = t * u * r
                gain_rows.append((jnp.sum(grown[:image], 0, keepdims=True), jnp.sum(grown[image:], 0, keepdims=True)))
                gt_ = g * t
                t = r * gt_ - u * (r * r * r) * (head_sums(u * gt_, low) / hd)
            t = t.astype(BF)
            pi[0, :, pl.ds(j * model + at, wide)] = t[:image]
            pt[0, :, pl.ds(j * model + at, wide)] = t[image:]
            wide_t = t.astype(F32)
            sums[0, 0:1, pl.ds(j * model + at, wide)] = jnp.sum(wide_t[:image], 0, keepdims=True)
            sums[0, 1:2, pl.ds(j * model + at, wide)] = jnp.sum(wide_t[image:], 0, keepdims=True)
        return jnp.concatenate([gain_rows[0][0], gain_rows[1][0], gain_rows[0][1], gain_rows[1][1]], 0)

    def step(i, total):
        for j in range(2):
            total = total + one(pl.multiple_of((2 * i + j) * wide, wide))
        return total

    gain_sums[0] = lax.fori_loop(0, pairs // 2, step, jnp.zeros((4, wide), F32))


def whole_block(x):
    return pl.BlockSpec((1,) + x.shape[1:], lambda i: (i, 0, 0))


def attention(u, gains, length):
    n, image, width = u[0].shape
    text = u[1].shape[1]
    hd = gains.shape[1] // 2
    model = width // 3
    outs = [jax.ShapeDtypeStruct((n, rows, model), BF) for rows in (image, text)]
    return pl.pallas_call(
        functools.partial(attention_kernel, length=length, hd=hd, pairs=model // (2 * hd)),
        grid=(n,),
        in_specs=[whole_block(u[0]), whole_block(u[1]), pl.BlockSpec(gains.shape, lambda i: (0, 0))],
        out_specs=[whole_block(t) for t in outs],
        out_shape=outs,
        name="attention",
    )(u[0], u[1], gains)


def attention_back(grads, u, gains, length):
    n, image, width = u[0].shape
    text = u[1].shape[1]
    hd = gains.shape[1] // 2
    model = width // 3
    outs = [jax.ShapeDtypeStruct((n, rows, width), BF) for rows in (image, text)]
    outs += [jax.ShapeDtypeStruct((n, 2, width), F32), jax.ShapeDtypeStruct((n, 4, 2 * hd), F32)]
    ins = [u[0], u[1], grads[0], grads[1]]
    pi, pt, sums, gain_sums = pl.pallas_call(
        functools.partial(attention_back_kernel, length=length, hd=hd, pairs=model // (2 * hd)),
        grid=(n,),
        in_specs=[whole_block(t) for t in ins] + [pl.BlockSpec(gains.shape, lambda i: (0, 0))],
        out_specs=[whole_block(t) for t in outs],
        out_shape=outs,
        name="attention_back",
    )(*ins, gains)
    gain = jnp.sum(gain_sums, 0)
    gain = (gain[:, :hd] + gain[:, hd:]).reshape(2, 2, hd)
    sums = jnp.sum(sums, 0)
    return [pi, pt], [sums[0], sums[1]], [gain[0], gain[1]]


def forward(x, mod, w, length):
    us, mixeds, saved = [], [], {}
    keep = {"x": x, "mod": mod}
    hidden = []
    for st in range(2):
        normed, _ = normalise(x[st].astype(F32))
        h = (normed * (1.0 + mod[:, st, 1][:, None]) + mod[:, st, 0][:, None]).astype(BF)
        h = gather_two(h)
        hidden.append(h)
        p = dot("nrd,dk->nrk", h, w["qkv"][st]) + w["b_qkv"][st]
        us.append(p)
    keep["hidden"], keep["u"] = hidden, us
    attended = attention(us, w["gain"], length)
    keep["attended"] = attended
    keep["branch"], keep["mixed"], keep["hidden_mlp"], keep["pre"], keep["act"], keep["mlp"] = [], [], [], [], [], []
    outs = []
    for st in range(2):
        branch = scatter_two(dot("nrk,kd->nrd", attended[st], w["out"][st])) + w["b_out"][st]
        mixed = x[st].astype(F32) + mod[:, st, 2][:, None] * branch
        normed, _ = normalise(mixed)
        h = (normed * (1.0 + mod[:, st, 4][:, None]) + mod[:, st, 3][:, None]).astype(BF)
        h = gather_four(h)
        pre = dot("nrd,df->nrf", h, w["fc1"][st]) + w["b_fc1"][st]
        act = gelu(pre).astype(BF)
        mlp = scatter_four(dot("nrf,fd->nrd", act, w["fc2"][st])) + w["b_fc2"][st]
        outs.append(mixed + mod[:, st, 5][:, None] * mlp)
        for name, value in (("branch", branch), ("mixed", mixed), ("hidden_mlp", h), ("pre", pre), ("act", act), ("mlp", mlp)):
            keep[name].append(value)
    return outs, keep


def backward_mlp(up, keep, w):
    mod = keep["mod"]
    state = {"mixed_grad": [], "late": [], "mlp": [], "pre": [], "fc2": [], "fc1": []}
    for st in range(2):
        mlp_grad = (mod[:, st, 5][:, None] * up[st]).astype(BF)
        state["fc2"].append(jnp.sum(mlp_grad.astype(F32), (0, 1)))
        gate = jnp.sum(keep["mlp"][st] * up[st], 1)
        mlp_grad = gather_four(mlp_grad)
        act_grad = dot("nrd,fd->nrf", mlp_grad, w["fc2"][st])
        pre_grad = (act_grad * gelu_slope(keep["pre"][st])).astype(BF)
        state["fc1"].append(jnp.sum(pre_grad.astype(F32), (0, 1)))
        h_grad = scatter_four(dot("nrf,df->nrd", pre_grad, w["fc1"][st]))
        normed, inverse = normalise(keep["mixed"][st])
        mixed_grad = up[st] + normalise_back(h_grad * (1.0 + mod[:, st, 4][:, None]), normed, inverse)
        state["late"].append((jnp.sum(h_grad, 1), jnp.sum(h_grad * normed, 1), gate))
        state["mixed_grad"].append(mixed_grad)
        state["mlp"].append(mlp_grad)
        state["pre"].append(pre_grad)
    return state


def backward_attention(state, keep, w, length):
    mod = keep["mod"]
    small = {"fc2": state["fc2"], "fc1": state["fc1"], "out": []}
    right = {"mlp": state["mlp"], "pre": state["pre"], "branch": []}
    attended_grads, gates = [], []
    for st in range(2):
        mixed_grad = state["mixed_grad"][st]
        branch_grad = (mod[:, st, 2][:, None] * mixed_grad).astype(BF)
        gates.append(jnp.sum(keep["branch"][st] * mixed_grad, 1))
        small["out"].append(jnp.sum(branch_grad.astype(F32), (0, 1)))
        branch_grad = gather_two(branch_grad)
        right["branch"].append(branch_grad)
        attended_grads.append(dot("nrd,kd->nrk", branch_grad, w["out"][st]).astype(BF))
    right["qkv"], small["qkv"], small["gain"] = attention_back(attended_grads, keep["u"], w["gain"], length)
    input_grads, mod_grads = [], []
    for st in range(2):
        h_grad = scatter_two(dot("nrk,dk->nrd", right["qkv"][st], w["qkv"][st]))
        normed, inverse = normalise(keep["x"][st].astype(F32))
        input_grads.append(
            state["mixed_grad"][st] + normalise_back(h_grad * (1.0 + mod[:, st, 1][:, None]), normed, inverse)
        )
        mod_grads.append(jnp.stack([jnp.sum(h_grad, 1), jnp.sum(h_grad * normed, 1), gates[st], *state["late"][st]], 1))
    return input_grads, jnp.stack(mod_grads, 1), small, right


def backward(up, keep, w, length):
    return backward_attention(backward_mlp(up, keep, w), keep, w, length)


def place(pieces, slots, count):
    whole = jnp.zeros((count,) + pieces[0].shape, pieces[0].dtype)
    for piece, slot in zip(pieces, slots):
        whole = lax.dynamic_update_index_in_dim(whole, piece, slot, 0)
    return whole


def take(x, index, axis):
    return lax.dynamic_index_in_dim(x, index, axis, keepdims=False)


def column_blocks(x, blocks, groups, width):
    streams, rows, _ = x.shape
    per = len(blocks) // groups

    def body(blocks_ref, x_ref, out_ref):
        out_ref[0] = x_ref[...]

    grid_spec = pltpu.PrefetchScalarGridSpec(
        num_scalar_prefetch=1,
        grid=(groups, streams, per),
        in_specs=[pl.BlockSpec((1, rows, width), lambda g, s, b, blocks: (s, 0, blocks[g * per + b]))],
        out_specs=pl.BlockSpec((1, 1, rows, width), lambda g, s, b, blocks: (g, s, 0, b)),
    )
    out = jax.ShapeDtypeStruct((groups, streams, rows, per * width), x.dtype)
    table = jnp.stack(blocks).astype(jnp.int32)
    return pl.pallas_call(body, grid_spec=grid_spec, out_shape=out, name="column_blocks")(table, x)


def columns_back(x, numbers):
    groups, streams, rows, columns = x.shape
    per = len(numbers) // groups
    width = columns // per

    def body(numbers_ref, x_ref, out_ref):
        out_ref[...] = x_ref[0].astype(F32)

    grid_spec = pltpu.PrefetchScalarGridSpec(
        num_scalar_prefetch=1,
        grid=(groups, per),
        in_specs=[pl.BlockSpec((1, streams, rows, width), lambda g, b, numbers: (g, 0, 0, b))],
        out_specs=pl.BlockSpec((streams, rows, width), lambda g, b, numbers: (0, 0, numbers[g * per + b])),
    )
    out = jax.ShapeDtypeStruct((streams, rows, groups * columns), F32)
    table = jnp.stack(numbers).astype(jnp.int32)
    return pl.pallas_call(body, grid_spec=grid_spec, out_shape=out, name="columns_back")(table, x)


def assemble(pieces, count, rows, parity):
    arrays = []
    for st in range(2):
        whole = None
        for piece, relayed, slot, at in pieces:
            if relayed is None:
                block = piece[st]
            else:
                block = jnp.where(parity == st, piece, relayed)
            if whole is None:
                whole = jnp.zeros((count * rows, block.shape[1]), block.dtype)
            whole = lax.dynamic_update_slice_in_dim(whole, block, slot * rows + at, 0)
        arrays.append(whole)
    return arrays


def prepare(w_qkv, b_qkv, gain, w_out, b_out, w_fc1, b_fc1, w_fc2, b_fc2):
    sid = lax.axis_index("shard")
    core = sid % 2
    parity = lax.axis_index("replica") % 2
    rows, width = w_qkv.shape[1], w_qkv.shape[2]
    part = width // 12
    slots = (sid, sid ^ 1, sid ^ 2, sid ^ 3)

    def of_parity(x):
        return jnp.where(parity == 0, x[0], x[1])

    numbers = [j * 4 + h * 2 + (core if g == 0 else 1 - core) for g in range(2) for j in range(3) for h in range(2)]
    mine, theirs = (t for t in column_blocks(w_qkv, numbers, 2, part))
    beside = near(theirs)
    pieces = [(mine, None, slots[0], 0), (beside, None, slots[1], 0)]
    last = None
    for block, slot in ((mine, slots[2]), (beside, slots[3])):
        chosen = of_parity(block)
        for h in range(2):
            direct = far(chosen[h * rows // 2 : (h + 1) * rows // 2])
            last = direct
            pieces.append((direct, mate(direct), slot, h * rows // 2))
    w = {"qkv": assemble(pieces, 4, rows, parity)}

    chosen = of_parity(w_out)
    chosen, last = lax.optimization_barrier((chosen, last))
    direct = far(chosen)
    relayed = mate(direct)
    half = sid // 2
    w["out"] = assemble([(w_out, None, half, 0), (direct, relayed, 1 - half, 0)], 2, rows, parity)

    columns = w_fc1.shape[2] // 4
    blocks = column_blocks(w_fc1, list(slots), 4, columns)
    beside = near(blocks[1])
    pieces = [(blocks[0], None, slots[0], 0), (beside, None, slots[1], 0)]
    for j, send in ((2, far), (3, across)):
        chosen, direct = lax.optimization_barrier((of_parity(blocks[j]), direct))
        direct = send(chosen)
        pieces.append((direct, mate(direct), slots[j], 0))
    w["fc1"] = assemble(pieces, 4, rows, parity)
    w["fc2"] = [w_fc2[0], w_fc2[1]]

    vectors = (b_qkv, b_out, b_fc2, gain.reshape(2, -1))
    packed = jnp.concatenate(vectors, 1)
    packed = gather_four(packed[None])
    packed = place([packed[j] for j in range(4)], slots, 4).astype(F32)
    flat, at = [], 0
    for vector in vectors:
        piece = packed[:, :, at : at + vector.shape[1]]
        at += vector.shape[1]
        flat.append(piece)
    b_qkv, b_out, b_fc2 = (jnp.concatenate([piece[j] for j in range(4)], 1) for piece in flat[:3])
    w["b_out"], w["b_fc2"], w["b_fc1"] = b_out, b_fc2, b_fc1.astype(F32)
    columns = [b_qkv[:, i * part : (i + 1) * part] for i in range(12)]
    w["b_qkv"] = jnp.where(core == 0, jnp.concatenate(columns[0::2], 1), jnp.concatenate(columns[1::2], 1))
    quarter = gain.shape[2]
    table = []
    for st in range(2):
        for j in range(2):
            row = [flat[3][i, st, j * quarter : (j + 1) * quarter] for i in range(4)]
            table.append(jnp.concatenate(row + row))
    w["gain"] = jnp.stack(table)
    return w


def weight_terms(left, right):
    total = None
    for a, b in zip(left, right):
        term = dot("nrd,nre->de", a, b)
        total = term if total is None else total + term
    return total


def over_replicas(x):
    return lax.psum_scatter(x, "replica", scatter_dimension=0, tiled=True)


def per_device(block_input, modulation, w_qkv, b_qkv, qk_gain, w_out, b_out, w_fc1, b_fc1, w_fc2, b_fc2, cotangent):
    section = lax.axis_index("section")
    first = section == 0
    sid = lax.axis_index("shard")
    core, row_pair = sid % 2, sid // 2
    count = lax.axis_size("replica")
    rid = lax.axis_index("replica")
    length = block_input.shape[2]
    padded = (length + 15) // 16 * 16
    w = prepare(w_qkv[0], b_qkv[0], qk_gain[0], w_out[0], b_out[0], w_fc1[0], b_fc1[0], w_fc2[0], b_fc2[0])

    def padding(x):
        return jnp.pad(x, ((0, 0), (0, 0), (0, padded - length), (0, 0)))

    def streams(x):
        return list(split_rows(x))

    def choose(a, b):
        return jax.tree.map(lambda p, q: jnp.where(first, p, q), a, b)

    def relay(x, pairs):
        return [lax.ppermute(t.astype(BF), "section", pairs) for t in x]

    block_input = padding(block_input)
    cotangent = padding(cotangent)
    mod = modulation[0]
    middle_mod = jnp.where(first, mod[1], mod[0])
    up_pair, down_pair = [(0, 1)], [(1, 0)]

    out0, keep0 = forward(streams(block_input[0]), mod[0], w, length)
    got = relay(out0, up_pair)
    out1, keep1 = forward(choose(streams(block_input[1]), got), middle_mod, w, length)
    got = relay(out1, up_pair)
    out2, keep2 = forward(got, mod[1], w, length)

    def zero_unless(cond, x):
        return [jnp.where(cond, t.astype(F32), 0.0) for t in x]

    grad0, mod_grad0, small0, right0 = backward(zero_unless(~first, streams(cotangent[0])), keep1, w, length)
    got = relay(grad0, down_pair)
    up = choose([t.astype(F32) for t in got], [t.astype(F32) for t in streams(cotangent[1])])
    keep_mid = choose(keep0, keep2)
    grad1, mod_grad1, small1, right1 = backward(up, keep_mid, w, length)
    got = relay(grad1, down_pair)
    last = backward_mlp(zero_unless(first, got), keep1, w)

    def terms(left, early, late, st):
        return weight_terms((keep_mid[left][st], keep1[left][st]), (early[st], late[st])).astype(BF)

    mlp_ends, pre_ends = choose(last["mlp"], right0["mlp"]), choose(last["pre"], right0["pre"])
    fc2 = [terms("act", right1["mlp"], mlp_ends, st) for st in (1, 0)]
    fc1 = []
    for st in (1, 0):
        t = terms("hidden_mlp", right1["pre"], pre_ends, st)
        d, cols = t.shape
        fc1.append(jnp.swapaxes(t.reshape(4, count, -1, cols), 0, 1).reshape(d, cols))
    last["mixed_grad"], fc2, fc1 = lax.optimization_barrier((last["mixed_grad"], fc2, fc1))
    fc2 = [over_replicas(t) for t in fc2]
    fc1 = [over_replicas(t) for t in fc1]
    reduced = (fc2, fc1)
    fc2 = jnp.stack([fc2[1], fc2[0]]).astype(F32)
    fc1 = [t.reshape(4, -1, t.shape[1]) for t in fc1]
    slots = [sid ^ j for j in range(4)]
    moved = []
    for j, send in ((0, lambda x: x), (1, near), (2, far), (3, across)):
        moved.append(send(jnp.stack([take(fc1[1], slots[j], 0), take(fc1[0], slots[j], 0)])))
    fc1 = columns_back(jnp.stack(moved), slots)

    grad2, mod_grad2, small2, right2 = backward_attention(last, keep1, w, length)

    def over_far(t):
        t = t.reshape(2, -1, t.shape[1])
        return (take(t, row_pair, 0).astype(F32) + far(take(t, 1 - row_pair, 0)).astype(F32)).astype(BF)

    branch_ends, qkv_ends = choose(right2["branch"], right0["branch"]), choose(right2["qkv"], right0["qkv"])
    qkv, out = [], []
    for st in (1, 0):
        t = over_far(terms("hidden", right1["qkv"], qkv_ends, st))
        cols = t.shape[1]
        qkv.append(jnp.swapaxes(t.reshape(2, count, -1, cols), 0, 1).reshape(-1, cols))
        out.append(over_far(terms("attended", right1["branch"], branch_ends, st)))
    qkv, out, _ = lax.optimization_barrier((qkv, out, reduced))
    qkv = [over_replicas(t).reshape(2, -1, t.shape[1]) for t in qkv][::-1]
    out = jnp.stack([over_replicas(t) for t in out][::-1]).astype(F32)
    own, other = (jnp.stack([take(t, which, 0) for t in qkv]) for which in (core, 1 - core))
    numbers = [j * 4 + h * 2 + c for c in (core, 1 - core) for j in range(3) for h in range(2)]
    qkv = columns_back(jnp.stack([own, near(other)]), numbers)

    small = jax.tree.map(lambda a, b, c: a + b + c, small0, small1, small2)
    pieces = []
    for st in range(2):
        cores = small["qkv"][st].reshape(6, 1, -1)
        cores = jnp.where(jnp.arange(2).reshape(1, 2, 1) == core, cores, 0.0).reshape(-1)
        quarter = small["fc1"][st].reshape(1, -1)
        quarter = jnp.where(jnp.arange(4).reshape(4, 1) == sid, quarter, 0.0).reshape(-1)
        pieces.append(jnp.concatenate([cores, small["out"][st], quarter, small["fc2"][st], small["gain"][st].reshape(-1)]))
    sizes = [w_qkv.shape[3], w_out.shape[3], w_fc1.shape[3], w_fc2.shape[3], w["gain"].shape[-1]]
    summed = lax.psum(jnp.stack(pieces), ("shard", "replica"))
    place_id = sid * count + rid
    vectors, at = [], 0
    for size in sizes:
        vectors.append(summed[:, at : at + size])
        at += size

    def own_block(x, axis):
        size = x.shape[axis] // (4 * count)
        return lax.dynamic_slice_in_dim(x, place_id * size, size, axis)

    blocks = [own_block(v, 1)[None] for v in vectors[:4]]
    gain = own_block(vectors[4].reshape(2, 2, -1), 2)[None]

    def joined(x):
        return jnp.concatenate(x, 1)[:, :length]

    activations = jnp.stack([joined(choose(out0, out1)), joined(choose(out1, out2))]).astype(BF)
    input_grads = jnp.stack([joined(choose(grad1, grad0)), joined(choose(grad2, grad1))])
    modulation_grad = jnp.stack([choose(mod_grad1, mod_grad0), choose(mod_grad2, mod_grad1)])
    return (
        activations[None],
        input_grads[None],
        modulation_grad[None],
        qkv[None],
        blocks[0],
        gain,
        out[None],
        blocks[1],
        fc1[None],
        blocks[2],
        fc2[None],
        blocks[3],
    )


def solution(mesh):
    every = ("shard", "replica")
    return jax.shard_map(
        per_device,
        mesh=mesh,
        in_specs=(
            P(None, every, None, None),
            P("section", None, every, None, None, None),
            P("section", None, "shard", None),
            P("section", None, "shard"),
            P("section", None, None, "shard"),
            P("section", None, "shard", None),
            P("section", None, "shard"),
            P("section", None, "shard", None),
            P("section", None, "shard"),
            P("section", None, "shard", None),
            P("section", None, "shard"),
            P(None, every, None, None),
        ),
        out_specs=(
            P("section", None, every, None, None),
            P("section", None, every, None, None),
            P("section", None, every, None, None, None),
            P("section", None, every, None),
            P("section", None, every),
            P("section", None, None, every),
            P("section", None, every, None),
            P("section", None, every),
            P("section", None, every, None),
            P("section", None, every),
            P("section", None, every, None),
            P("section", None, every),
        ),
        check_vma=False,
    )
```

```python
import functools

import jax
import jax.numpy as jnp
from jax import lax
from jax.experimental import pallas as pl
from jax.experimental.pallas import tpu as pltpu
from jax.sharding import PartitionSpec as P


IMG = 64
norm_eps = 1e-06
BF = jnp.bfloat16
F32 = jnp.float32


def times(x, w):
    n, rows, d = x.shape
    y = lax.dot_general(x.reshape(n * rows, d), w, (((1,), (0,)), ((), ())), preferred_element_type=F32)
    return y.reshape(n, rows, -1)


def times_turned(x, w):
    n, rows, k = x.shape
    y = lax.dot_general(x.reshape(n * rows, k), w, (((1,), (1,)), ((), ())), preferred_element_type=F32)
    return y.reshape(n, rows, -1)


def outer(a, b):
    a, b = (t.reshape(-1, t.shape[2]) for t in (a, b))
    return lax.dot_general(a, b, (((0,), (0,)), ((), ())), preferred_element_type=F32)


def near(x):
    return lax.ppermute(x, "shard", [(i, i ^ 1) for i in range(4)])


def far(x):
    return lax.ppermute(x, "shard", [(i, i ^ 2) for i in range(4)])


def across(x):
    return lax.ppermute(x, "shard", [(i, i ^ 3) for i in range(4)])


def mate(x):
    count = lax.axis_size("replica")
    return lax.ppermute(x, "replica", [(i, i ^ 1) for i in range(count)])


def gather_two(x):
    return jnp.concatenate([x, near(x)], 0)


def gather_four(x):
    other = far(x)
    return jnp.concatenate([x, near(x), other, near(other)], 0)


def scatter_two(parts):
    own = parts.shape[0] // 2
    return parts[:own] + near(parts[own:].astype(BF)).astype(F32)


def scatter_four(parts):
    own = parts.shape[0] // 4
    away = parts[2 * own : 3 * own] + near(parts[3 * own :].astype(BF)).astype(F32)
    away = far(away.astype(BF))
    here = parts[:own] + near(parts[own : 2 * own].astype(BF)).astype(F32)
    return here + away.astype(F32)


def normalise(x):
    centred = x - jnp.mean(x, -1, keepdims=True)
    inverse = lax.rsqrt(jnp.mean(centred * centred, -1, keepdims=True) + norm_eps)
    return centred * inverse, inverse


def normalise_back(f, normed, inverse):
    return inverse * (
        f - jnp.mean(f, -1, keepdims=True) - normed * jnp.mean(f * normed, -1, keepdims=True)
    )


gelu_a = (2.0 / jnp.pi) ** 0.5
gelu_b = 0.044715


def gelu(v):
    square = v * v
    t = jnp.tanh(gelu_a * (v + gelu_b * square * v))
    half = 0.5 * (1.0 + t)
    return v * half, half + 0.5 * v * (1.0 - t * t) * gelu_a * (1.0 + 3.0 * gelu_b * square)


def total_of(x, axes):
    for axis in axes:
        count, step = lax.axis_size(axis), 1
        while step < count:
            x = x + lax.ppermute(x, axis, [(i, i ^ step) for i in range(count)])
            step *= 2
    return x


def split_rows(x):
    return (x[:, :IMG], x[:, IMG:])


def lanes_of(hd):
    return lax.broadcasted_iota(jnp.int32, (1, 2 * hd), 1) < hd


def head_sums(x, low):
    a = jnp.sum(jnp.where(low, x, 0.0), -1, keepdims=True)
    b = jnp.sum(jnp.where(low, 0.0, x), -1, keepdims=True)
    return jnp.where(low, a, b)


def rows_of(first, second, at, width):
    return jnp.concatenate([first[0, :, pl.ds(at, width)], second[0, :, pl.ds(at, width)]], 0)


def dot_rows(a, b):
    return lax.dot_general(a, b, (((1,), (1,)), ((), ())), preferred_element_type=F32)


def dot_plain(a, b):
    return lax.dot_general(a, b, (((1,), (0,)), ((), ())), preferred_element_type=F32)


def dot_turned(a, b):
    return lax.dot_general(a, b, (((0,), (0,)), ((), ())), preferred_element_type=F32)


def pair_state(ui, ut, gains, at, model, hd, low, first_rows):
    wide = 2 * hd
    q_u, k_u, v_u = (rows_of(ui, ut, j * model + at, wide) for j in range(3))
    state = []
    for j, u in enumerate((q_u, k_u)):
        g = jnp.where(first_rows, gains[j : j + 1, :], gains[j + 2 : j + 3, :])
        r = lax.rsqrt(head_sums(u * u, low) / hd + norm_eps)
        state.append((u, g, r, (u * r * g).astype(BF)))
    return state[0], state[1], v_u.astype(BF)


def head_probs(q, k, low, bias, scale):
    scores = dot_rows(jnp.where(low, q, jnp.zeros_like(q)), k) * scale + bias
    exponent = jnp.exp(scores)
    return exponent / jnp.sum(exponent, -1, keepdims=True)


def row_kinds(image, padded, length):
    first_rows = lax.broadcasted_iota(jnp.int32, (padded, 1), 0) < image
    keys = lax.broadcasted_iota(jnp.int32, (1, padded), 1)
    return first_rows, jnp.where(keys < length, 0.0, -1e30).astype(F32)


def attention_kernel(ui, ut, gains, oi, ot, *, length, hd, pairs):
    image = ui.shape[1]
    padded = image + ut.shape[1]
    model = pairs * 2 * hd
    low = lanes_of(hd)
    first_rows, bias = row_kinds(image, padded, length)
    scale = hd**-0.5

    def one(at):
        (_, _, _, q), (_, _, _, k), v = pair_state(ui, ut, gains, at, model, hd, low, first_rows)
        both = []
        for mask in (low, jnp.logical_not(low)):
            probs = head_probs(q, k, mask, bias, scale).astype(BF)
            both.append(dot_plain(probs, v))
        out = jnp.where(low, both[0], both[1]).astype(BF)
        oi[0, :, pl.ds(at, 2 * hd)] = out[:image]
        ot[0, :, pl.ds(at, 2 * hd)] = out[image:]

    def step(i, carry):
        for j in range(2):
            one(pl.multiple_of((2 * i + j) * 2 * hd, 2 * hd))
        return carry

    lax.fori_loop(0, pairs // 2, step, 0)


def attention_back_kernel(ui, ut, gi, gt, gains, pi, pt, sums, gain_sums, *, length, hd, pairs):
    image = ui.shape[1]
    padded = image + ut.shape[1]
    wide = 2 * hd
    model = pairs * wide
    low = lanes_of(hd)
    first_rows, bias = row_kinds(image, padded, length)
    scale = hd**-0.5

    def one(at):
        (q_u, q_g, q_r, q), (k_u, k_g, k_r, k), v = pair_state(ui, ut, gains, at, model, hd, low, first_rows)
        grad = rows_of(gi, gt, at, wide)
        dqs, dks, dvs = [], [], []
        for mask in (low, jnp.logical_not(low)):
            probs = head_probs(q, k, mask, bias, scale)
            prob_grad = dot_rows(jnp.where(mask, grad, jnp.zeros_like(grad)), v)
            delta = jnp.sum(prob_grad * probs, -1, keepdims=True)
            score_grad = (probs * (prob_grad - delta)).astype(BF)
            dvs.append(dot_turned(probs.astype(BF), grad))
            dqs.append(dot_plain(score_grad, k))
            dks.append(dot_turned(score_grad, q))
        gain_rows = []
        for j, (u, g, r, pair) in enumerate(((q_u, q_g, q_r, dqs), (k_u, k_g, k_r, dks), (None, None, None, dvs))):
            t = jnp.where(low, pair[0], pair[1])
            if j < 2:
                t = t * scale
                grown = t * u * r
                gain_rows.append((jnp.sum(grown[:image], 0, keepdims=True), jnp.sum(grown[image:], 0, keepdims=True)))
                gt_ = g * t
                t = r * gt_ - u * (r * r * r) * (head_sums(u * gt_, low) / hd)
            t = t.astype(BF)
            pi[0, :, pl.ds(j * model + at, wide)] = t[:image]
            pt[0, :, pl.ds(j * model + at, wide)] = t[image:]
            wide_t = t.astype(F32)
            sums[0, 0:1, pl.ds(j * model + at, wide)] = jnp.sum(wide_t[:image], 0, keepdims=True)
            sums[0, 1:2, pl.ds(j * model + at, wide)] = jnp.sum(wide_t[image:], 0, keepdims=True)
        return jnp.concatenate([gain_rows[0][0], gain_rows[1][0], gain_rows[0][1], gain_rows[1][1]], 0)

    def step(i, total):
        for j in range(2):
            total = total + one(pl.multiple_of((2 * i + j) * wide, wide))
        return total

    gain_sums[0] = lax.fori_loop(0, pairs // 2, step, jnp.zeros((4, wide), F32))


def whole_block(x):
    return pl.BlockSpec((1,) + x.shape[1:], lambda i: (i, 0, 0))


def attention(u, gains, length):
    n, image, width = u[0].shape
    text = u[1].shape[1]
    hd = gains.shape[1] // 2
    model = width // 3
    outs = [jax.ShapeDtypeStruct((n, rows, model), BF) for rows in (image, text)]
    return pl.pallas_call(
        functools.partial(attention_kernel, length=length, hd=hd, pairs=model // (2 * hd)),
        grid=(n,),
        in_specs=[whole_block(u[0]), whole_block(u[1]), pl.BlockSpec(gains.shape, lambda i: (0, 0))],
        out_specs=[whole_block(t) for t in outs],
        out_shape=outs,
        name="attention",
    )(u[0], u[1], gains)


def attention_back(grads, u, gains, length):
    n, image, width = u[0].shape
    text = u[1].shape[1]
    hd = gains.shape[1] // 2
    model = width // 3
    outs = [jax.ShapeDtypeStruct((n, rows, width), BF) for rows in (image, text)]
    outs += [jax.ShapeDtypeStruct((n, 2, width), F32), jax.ShapeDtypeStruct((n, 4, 2 * hd), F32)]
    ins = [u[0], u[1], grads[0], grads[1]]
    pi, pt, sums, gain_sums = pl.pallas_call(
        functools.partial(attention_back_kernel, length=length, hd=hd, pairs=model // (2 * hd)),
        grid=(n,),
        in_specs=[whole_block(t) for t in ins] + [pl.BlockSpec(gains.shape, lambda i: (0, 0))],
        out_specs=[whole_block(t) for t in outs],
        out_shape=outs,
        name="attention_back",
    )(*ins, gains)
    gain = jnp.sum(gain_sums, 0)
    gain = (gain[:, :hd] + gain[:, hd:]).reshape(2, 2, hd)
    sums = jnp.sum(sums, 0)
    return [pi, pt], [sums[0], sums[1]], [gain[0], gain[1]]


def forward(x, mod, w, length):
    us, mixeds, saved = [], [], {}
    keep = {"x": x, "mod": mod}
    hidden = []
    for st in range(2):
        normed, _ = normalise(x[st].astype(F32))
        h = (normed * (1.0 + mod[:, st, 1][:, None]) + mod[:, st, 0][:, None]).astype(BF)
        h = gather_two(h)
        hidden.append(h)
        p = times(h, w["qkv"][st]) + w["b_qkv"][st]
        us.append(p)
    keep["hidden"], keep["u"] = hidden, us
    attended = attention(us, w["gain"], length)
    keep["attended"] = attended
    keep["branch"], keep["mixed"], keep["hidden_mlp"], keep["slope"], keep["act"], keep["mlp"] = [], [], [], [], [], []
    outs = []
    for st in range(2):
        branch = scatter_two(times(attended[st], w["out"][st])) + w["b_out"][st]
        mixed = x[st].astype(F32) + mod[:, st, 2][:, None] * branch
        normed, _ = normalise(mixed)
        h = (normed * (1.0 + mod[:, st, 4][:, None]) + mod[:, st, 3][:, None]).astype(BF)
        h = gather_four(h)
        pre = times(h, w["fc1"][st]) + w["b_fc1"][st]
        act, slope = gelu(pre)
        act = act.astype(BF)
        mlp = scatter_four(times(act, w["fc2"][st])) + w["b_fc2"][st]
        outs.append(mixed + mod[:, st, 5][:, None] * mlp)
        for name, value in (("branch", branch), ("mixed", mixed), ("hidden_mlp", h), ("slope", slope), ("act", act), ("mlp", mlp)):
            keep[name].append(value)
    return outs, keep


def backward_entry(up, keep):
    mod = keep["mod"]
    state = {"up": up, "mlp": [], "fc2": [], "gate": []}
    for st in range(2):
        mlp_grad = (mod[:, st, 5][:, None] * up[st]).astype(BF)
        state["fc2"].append(jnp.sum(mlp_grad.astype(F32), (0, 1)))
        state["gate"].append(jnp.sum(keep["mlp"][st] * up[st], 1))
        state["mlp"].append(gather_four(mlp_grad))
    return state


def backward_mlp(state, keep, w):
    mod = keep["mod"]
    state = dict(state, mixed_grad=[], late=[], pre=[], fc1=[])
    for st in range(2):
        act_grad = times_turned(state["mlp"][st], w["fc2"][st])
        pre_grad = (act_grad * keep["slope"][st]).astype(BF)
        state["fc1"].append(jnp.sum(pre_grad.astype(F32), (0, 1)))
        h_grad = scatter_four(times_turned(pre_grad, w["fc1"][st]))
        normed, inverse = normalise(keep["mixed"][st])
        back = normalise_back(h_grad * (1.0 + mod[:, st, 4][:, None]), normed, inverse)
        state["mixed_grad"].append(state["up"][st] + back)
        state["late"].append((jnp.sum(h_grad, 1), jnp.sum(h_grad * normed, 1), state["gate"][st]))
        state["pre"].append(pre_grad)
    return state


def backward_attention(state, keep, w, length):
    mod = keep["mod"]
    small = {"fc2": state["fc2"], "fc1": state["fc1"], "out": []}
    right = {"mlp": state["mlp"], "pre": state["pre"], "branch": []}
    attended_grads, gates = [], []
    for st in range(2):
        mixed_grad = state["mixed_grad"][st]
        branch_grad = (mod[:, st, 2][:, None] * mixed_grad).astype(BF)
        gates.append(jnp.sum(keep["branch"][st] * mixed_grad, 1))
        small["out"].append(jnp.sum(branch_grad.astype(F32), (0, 1)))
        branch_grad = gather_two(branch_grad)
        right["branch"].append(branch_grad)
        attended_grads.append(times_turned(branch_grad, w["out"][st]).astype(BF))
    right["qkv"], small["qkv"], small["gain"] = attention_back(attended_grads, keep["u"], w["gain"], length)
    input_grads, mod_grads = [], []
    for st in range(2):
        h_grad = scatter_two(times_turned(right["qkv"][st], w["qkv"][st]))
        normed, inverse = normalise(keep["x"][st].astype(F32))
        input_grads.append(
            state["mixed_grad"][st] + normalise_back(h_grad * (1.0 + mod[:, st, 1][:, None]), normed, inverse)
        )
        mod_grads.append(jnp.stack([jnp.sum(h_grad, 1), jnp.sum(h_grad * normed, 1), gates[st], *state["late"][st]], 1))
    return input_grads, jnp.stack(mod_grads, 1), small, right


def backward(up, keep, w, length):
    return backward_attention(backward_mlp(backward_entry(up, keep), keep, w), keep, w, length)


def place(pieces, slots, count):
    whole = jnp.zeros((count,) + pieces[0].shape, pieces[0].dtype)
    for piece, slot in zip(pieces, slots):
        whole = lax.dynamic_update_index_in_dim(whole, piece, slot, 0)
    return whole


def take(x, index, axis):
    return lax.dynamic_index_in_dim(x, index, axis, keepdims=False)


def column_blocks(x, blocks, groups, width, stream=None):
    streams, rows, _ = x.shape
    streams = streams if stream is None else 1
    per = len(blocks) // groups
    numbers = list(blocks) + [0 if stream is None else stream]

    def body(blocks_ref, x_ref, out_ref):
        out_ref[0] = x_ref[...]

    grid_spec = pltpu.PrefetchScalarGridSpec(
        num_scalar_prefetch=1,
        grid=(groups, per),
        in_specs=[pl.BlockSpec((streams, rows, width), lambda g, b, blocks: (blocks[len(numbers) - 1], 0, blocks[g * per + b]))],
        out_specs=pl.BlockSpec((1, streams, rows, width), lambda g, b, blocks: (g, 0, 0, b)),
    )
    out = jax.ShapeDtypeStruct((groups, streams, rows, per * width), x.dtype)
    table = jnp.stack(numbers).astype(jnp.int32)
    return pl.pallas_call(body, grid_spec=grid_spec, out_shape=out, name="column_blocks")(table, x)


def columns_back(x, numbers):
    groups, streams, rows, columns = x.shape
    per = len(numbers) // groups
    width = columns // per

    def body(numbers_ref, x_ref, out_ref):
        out_ref[...] = x_ref[0].astype(F32)

    grid_spec = pltpu.PrefetchScalarGridSpec(
        num_scalar_prefetch=1,
        grid=(groups, per),
        in_specs=[pl.BlockSpec((1, streams, rows, width), lambda g, b, numbers: (g, 0, 0, b))],
        out_specs=pl.BlockSpec((streams, rows, width), lambda g, b, numbers: (0, 0, numbers[g * per + b])),
    )
    out = jax.ShapeDtypeStruct((streams, rows, groups * columns), F32)
    table = jnp.stack(numbers).astype(jnp.int32)
    return pl.pallas_call(body, grid_spec=grid_spec, out_shape=out, name="columns_back")(table, x)


def assemble(pieces, count, rows, parity):
    arrays = []
    for st in range(2):
        whole = None
        for piece, relayed, slot, at in pieces:
            if relayed is None:
                block = piece[st]
            else:
                block = jnp.where(parity == st, piece, relayed)
            if whole is None:
                whole = jnp.zeros((count * rows, block.shape[1]), block.dtype)
            whole = lax.dynamic_update_slice_in_dim(whole, block, slot * rows + at, 0)
        arrays.append(whole)
    return arrays


def prepare(w_qkv, b_qkv, gain, w_out, b_out, w_fc1, b_fc1, w_fc2, b_fc2):
    sid = lax.axis_index("shard")
    core = sid % 2
    parity = lax.axis_index("replica") % 2
    rows, width = w_qkv.shape[1], w_qkv.shape[2]
    part = width // 12
    slots = (sid, sid ^ 1, sid ^ 2, sid ^ 3)

    def of_parity(x):
        return jnp.where(parity == 0, x[0], x[1])

    direct, relayed = [], []

    def fetch(send, x):
        x, _, _ = lax.optimization_barrier((x, direct[-1:], relayed[-2:-1]))
        direct.append(send(x))
        relayed.append(mate(direct[-1]))
        return direct[-1], relayed[-1]

    numbers = [j * 4 + h * 2 + (core if g == 0 else 1 - core) for g in range(2) for j in range(3) for h in range(2)]
    got = []
    for g, send in ((0, far), (1, across)):
        got.append(fetch(send, column_blocks(w_qkv, numbers[6 * g : 6 * g + 6], 1, part, parity)[0, 0]))
    w_qkv, w_out, _ = lax.optimization_barrier((w_qkv, w_out, got[0][0]))
    w_fc1, _ = lax.optimization_barrier((w_fc1, got[1][0]))
    mine = column_blocks(w_qkv, numbers[:6], 1, part)[0]
    theirs = column_blocks(w_qkv, numbers[6:], 1, part)[0]
    pieces = [(mine, None, slots[0], 0), (near(theirs), None, slots[1], 0)]
    pieces += [(*t, slots[2 + i], 0) for i, t in enumerate(got)]
    w = {"qkv": assemble(pieces, 4, rows, parity)}

    got = fetch(far, of_parity(w_out))
    pair = sid // 2
    w["out"] = assemble([(w_out, None, pair, 0), (*got, 1 - pair, 0)], 2, rows, parity)

    columns = w_fc1.shape[2] // 4
    blocks = [column_blocks(w_fc1, [slot], 1, columns)[0] for slot in slots[:2]]
    pieces = [(blocks[0], None, slots[0], 0), (near(blocks[1]), None, slots[1], 0)]
    for j, send in ((2, far), (3, across)):
        block = column_blocks(w_fc1, [slots[j]], 1, columns, parity)[0, 0]
        pieces.append((*fetch(send, block), slots[j], 0))
    w["fc1"] = assemble(pieces, 4, rows, parity)
    w["fc2"] = [w_fc2[0], w_fc2[1]]

    vectors = (b_qkv, b_out, b_fc2, gain.reshape(2, -1))
    packed = jnp.concatenate(vectors, 1)
    packed = gather_four(packed[None])
    packed = place([packed[j] for j in range(4)], slots, 4).astype(F32)
    flat, at = [], 0
    for vector in vectors:
        piece = packed[:, :, at : at + vector.shape[1]]
        at += vector.shape[1]
        flat.append(piece)
    b_qkv, b_out, b_fc2 = (jnp.concatenate([piece[j] for j in range(4)], 1) for piece in flat[:3])
    w["b_out"], w["b_fc2"], w["b_fc1"] = b_out, b_fc2, b_fc1.astype(F32)
    columns = [b_qkv[:, i * part : (i + 1) * part] for i in range(12)]
    w["b_qkv"] = jnp.where(core == 0, jnp.concatenate(columns[0::2], 1), jnp.concatenate(columns[1::2], 1))
    quarter = gain.shape[2]
    table = []
    for st in range(2):
        for j in range(2):
            row = [flat[3][i, st, j * quarter : (j + 1) * quarter] for i in range(4)]
            table.append(jnp.concatenate(row + row))
    w["gain"] = jnp.stack(table)
    return w


def weight_terms(left, right):
    total = None
    for a, b in zip(left, right):
        term = outer(a, b)
        total = term if total is None else total + term
    return total


def over_replicas(x):
    inner = x.shape[1:]
    x = x.reshape(-1, inner[-1])
    return lax.psum_scatter(x, "replica", scatter_dimension=0, tiled=True).reshape(inner)


def per_device(block_input, modulation, w_qkv, b_qkv, qk_gain, w_out, b_out, w_fc1, b_fc1, w_fc2, b_fc2, cotangent):
    section = lax.axis_index("section")
    first = section == 0
    sid = lax.axis_index("shard")
    core, row_pair = sid % 2, sid // 2
    count = lax.axis_size("replica")
    rid = lax.axis_index("replica")
    length = block_input.shape[2]
    padded = (length + 15) // 16 * 16
    w = prepare(w_qkv[0], b_qkv[0], qk_gain[0], w_out[0], b_out[0], w_fc1[0], b_fc1[0], w_fc2[0], b_fc2[0])

    def padding(x):
        return jnp.pad(x, ((0, 0), (0, 0), (0, padded - length), (0, 0)))

    def streams(x):
        return list(split_rows(x))

    def choose(a, b):
        return jax.tree.map(lambda p, q: jnp.where(first, p, q), a, b)

    def relay(x, pairs):
        return [lax.ppermute(t.astype(BF), "section", pairs) for t in x]

    block_input = padding(block_input)
    cotangent = padding(cotangent)
    mod = modulation[0]
    middle_mod = jnp.where(first, mod[1], mod[0])
    up_pair, down_pair = [(0, 1)], [(1, 0)]

    out0, keep0 = forward(streams(block_input[0]), mod[0], w, length)
    got = relay(out0, up_pair)
    out1, keep1 = forward(choose(streams(block_input[1]), got), middle_mod, w, length)
    got = relay(out1, up_pair)
    out2, keep2 = forward(got, mod[1], w, length)

    def zero_unless(cond, x):
        return [jnp.where(cond, t.astype(F32), 0.0) for t in x]

    grad0, mod_grad0, small0, right0 = backward(zero_unless(~first, streams(cotangent[0])), keep1, w, length)
    got = relay(grad0, down_pair)
    up = choose([t.astype(F32) for t in got], [t.astype(F32) for t in streams(cotangent[1])])
    keep_mid = choose(keep0, keep2)
    grad1, mod_grad1, small1, right1 = backward(up, keep_mid, w, length)
    got = relay(grad1, down_pair)
    last = backward_entry(zero_unless(first, got), keep1)

    def terms(left, early, late, st):
        return weight_terms((keep_mid[left][st], keep1[left][st]), (early[st], late[st])).astype(BF)

    mlp_ends = choose(last["mlp"], right0["mlp"])
    fc2 = [terms("act", right1["mlp"], mlp_ends, st) for st in range(2)]
    fc2 = jnp.stack([t.reshape(count, -1, t.shape[1]) for t in fc2], 1)
    last["mlp"], fc2 = lax.optimization_barrier((last["mlp"], fc2))
    last = backward_mlp(last, keep1, w)
    pre_ends = choose(last["pre"], right0["pre"])
    fc1 = []
    for st in range(2):
        t = terms("hidden_mlp", right1["pre"], pre_ends, st)
        fc1.append(jnp.swapaxes(t.reshape(4, count, -1, t.shape[1]), 0, 1))
    fc1 = jnp.stack(fc1, 1)
    last["mixed_grad"], fc1 = lax.optimization_barrier((last["mixed_grad"], fc1))
    fc2, fc1 = over_replicas(fc2), over_replicas(fc1)
    grad2, mod_grad2, small2, right2 = backward_attention(last, keep1, w, length)

    halves = []

    def over_far(t):
        t = t.reshape(2, -1, t.shape[1])
        sent, _ = lax.optimization_barrier((take(t, 1 - row_pair, 0), halves[-1:]))
        halves.append(far(sent))
        return (take(t, row_pair, 0).astype(F32) + halves[-1].astype(F32)).astype(BF)

    branch_ends, qkv_ends = choose(right2["branch"], right0["branch"]), choose(right2["qkv"], right0["qkv"])
    qkv, out = [], []
    for st in range(2):
        t = over_far(terms("hidden", right1["qkv"], qkv_ends, st))
        qkv.append(jnp.swapaxes(t.reshape(2, count, -1, t.shape[1]), 0, 1))
    for st in range(2):
        t = over_far(terms("attended", right1["branch"], branch_ends, st))
        out.append(t.reshape(count, -1, t.shape[1]))
    qkv, fc2, fc1 = lax.optimization_barrier((jnp.stack(qkv, 1), fc2, fc1))
    qkv = over_replicas(qkv)
    out, fc2, fc1 = lax.optimization_barrier((jnp.stack(out, 1), fc2, fc1))
    out = over_replicas(out)
    fc2 = fc2.astype(F32)
    slots = [sid ^ j for j in range(4)]
    moved = []
    for j, send in ((0, lambda x: x), (1, near), (2, far), (3, across)):
        moved.append(send(take(fc1, slots[j], 1)))
    fc1 = columns_back(jnp.stack(moved), slots)

    own, other = (take(qkv, which, 1) for which in (core, 1 - core))
    numbers = [j * 4 + h * 2 + c for c in (core, 1 - core) for j in range(3) for h in range(2)]
    qkv = columns_back(jnp.stack([own, near(other)]), numbers)
    qkv, out = lax.optimization_barrier((qkv, out))
    out = out.astype(F32)

    small = jax.tree.map(lambda a, b, c: a + b + c, small0, small1, small2)
    pieces = []
    for st in range(2):
        cores = small["qkv"][st].reshape(6, 1, -1)
        cores = jnp.where(jnp.arange(2).reshape(1, 2, 1) == core, cores, 0.0).reshape(-1)
        quarter = small["fc1"][st].reshape(1, -1)
        quarter = jnp.where(jnp.arange(4).reshape(4, 1) == sid, quarter, 0.0).reshape(-1)
        pieces.append(jnp.concatenate([cores, small["out"][st], quarter, small["fc2"][st], small["gain"][st].reshape(-1)]))
    sizes = [w_qkv.shape[3], w_out.shape[3], w_fc1.shape[3], w_fc2.shape[3], w["gain"].shape[-1]]
    summed = total_of(jnp.stack(pieces), ("shard", "replica"))
    place_id = sid * count + rid
    vectors, at = [], 0
    for size in sizes:
        vectors.append(summed[:, at : at + size])
        at += size

    def own_block(x, axis):
        size = x.shape[axis] // (4 * count)
        return lax.dynamic_slice_in_dim(x, place_id * size, size, axis)

    blocks = [own_block(v, 1)[None] for v in vectors[:4]]
    gain = own_block(vectors[4].reshape(2, 2, -1), 2)[None]

    def joined(x):
        return jnp.concatenate(x, 1)[:, :length]

    activations = jnp.stack([joined(choose(out0, out1)), joined(choose(out1, out2))]).astype(BF)
    input_grads = jnp.stack([joined(choose(grad1, grad0)), joined(choose(grad2, grad1))])
    modulation_grad = jnp.stack([choose(mod_grad1, mod_grad0), choose(mod_grad2, mod_grad1)])
    return (
        activations[None],
        input_grads[None],
        modulation_grad[None],
        qkv[None],
        blocks[0],
        gain,
        out[None],
        blocks[1],
        fc1[None],
        blocks[2],
        fc2[None],
        blocks[3],
    )


def solution(mesh):
    every = ("shard", "replica")
    return jax.shard_map(
        per_device,
        mesh=mesh,
        in_specs=(
            P(None, every, None, None),
            P("section", None, every, None, None, None),
            P("section", None, "shard", None),
            P("section", None, "shard"),
            P("section", None, None, "shard"),
            P("section", None, "shard", None),
            P("section", None, "shard"),
            P("section", None, "shard", None),
            P("section", None, "shard"),
            P("section", None, "shard", None),
            P("section", None, "shard"),
            P(None, every, None, None),
        ),
        out_specs=(
            P("section", None, every, None, None),
            P("section", None, every, None, None),
            P("section", None, every, None, None, None),
            P("section", None, every, None),
            P("section", None, every),
            P("section", None, None, every),
            P("section", None, every, None),
            P("section", None, every),
            P("section", None, every, None),
            P("section", None, every),
            P("section", None, every, None),
            P("section", None, every),
        ),
        check_vma=False,
    )
```

```python
import functools

import jax
import jax.numpy as jnp
from jax import lax
from jax.experimental import pallas as pl
from jax.experimental.pallas import tpu as pltpu
from jax.sharding import PartitionSpec as P


IMG = 64
norm_eps = 1e-06
BF = jnp.bfloat16
F32 = jnp.float32


def times(x, w):
    n, rows, d = x.shape
    y = lax.dot_general(x.reshape(n * rows, d), w, (((1,), (0,)), ((), ())), preferred_element_type=F32)
    return y.reshape(n, rows, -1)


def times_turned(x, w):
    n, rows, k = x.shape
    y = lax.dot_general(x.reshape(n * rows, k), w, (((1,), (1,)), ((), ())), preferred_element_type=F32)
    return y.reshape(n, rows, -1)


def outer(a, b):
    a, b = (t.reshape(-1, t.shape[2]) for t in (a, b))
    return lax.dot_general(a, b, (((0,), (0,)), ((), ())), preferred_element_type=F32)


def near(x):
    return lax.ppermute(x, "shard", [(i, i ^ 1) for i in range(4)])


def far(x):
    return lax.ppermute(x, "shard", [(i, i ^ 2) for i in range(4)])


def across(x):
    return lax.ppermute(x, "shard", [(i, i ^ 3) for i in range(4)])


def mate(x):
    count = lax.axis_size("replica")
    return lax.ppermute(x, "replica", [(i, i ^ 1) for i in range(count)])


def gather_two(x):
    return jnp.concatenate([x, near(x)], 0)


def gather_four(x):
    other = far(x)
    return jnp.concatenate([x, near(x), other, near(other)], 0)


def scatter_two(parts):
    own = parts.shape[0] // 2
    return parts[:own] + near(parts[own:].astype(BF)).astype(F32)


def scatter_four(parts):
    own = parts.shape[0] // 4
    away = parts[2 * own : 3 * own] + near(parts[3 * own :].astype(BF)).astype(F32)
    away = far(away.astype(BF))
    here = parts[:own] + near(parts[own : 2 * own].astype(BF)).astype(F32)
    return here + away.astype(F32)


def normalise(x):
    centred = x - jnp.mean(x, -1, keepdims=True)
    inverse = lax.rsqrt(jnp.mean(centred * centred, -1, keepdims=True) + norm_eps)
    return centred * inverse, inverse


def normalise_back(f, normed, inverse):
    return inverse * (
        f - jnp.mean(f, -1, keepdims=True) - normed * jnp.mean(f * normed, -1, keepdims=True)
    )


gelu_a = (2.0 / jnp.pi) ** 0.5
gelu_b = 0.044715


def gelu(v):
    square = v * v
    t = jnp.tanh(gelu_a * (v + gelu_b * square * v))
    half = 0.5 * (1.0 + t)
    return v * half, half + 0.5 * v * (1.0 - t * t) * gelu_a * (1.0 + 3.0 * gelu_b * square)


def total_of(x, axes):
    for axis in axes:
        count, step = lax.axis_size(axis), 1
        while step < count:
            x = x + lax.ppermute(x, axis, [(i, i ^ step) for i in range(count)])
            step *= 2
    return x


def split_rows(x):
    return (x[:, :IMG], x[:, IMG:])


def lanes_of(hd):
    return lax.broadcasted_iota(jnp.int32, (1, 2 * hd), 1) < hd


def head_sums(x, low):
    a = jnp.sum(jnp.where(low, x, 0.0), -1, keepdims=True)
    b = jnp.sum(jnp.where(low, 0.0, x), -1, keepdims=True)
    return jnp.where(low, a, b)


def rows_of(first, second, at, width):
    return jnp.concatenate([first[0, :, pl.ds(at, width)], second[0, :, pl.ds(at, width)]], 0)


def dot_rows(a, b):
    return lax.dot_general(a, b, (((1,), (1,)), ((), ())), preferred_element_type=F32)


def dot_plain(a, b):
    return lax.dot_general(a, b, (((1,), (0,)), ((), ())), preferred_element_type=F32)


def dot_turned(a, b):
    return lax.dot_general(a, b, (((0,), (0,)), ((), ())), preferred_element_type=F32)


def pair_state(ui, ut, gains, at, model, hd, low, first_rows):
    wide = 2 * hd
    q_u, k_u, v_u = (rows_of(ui, ut, j * model + at, wide) for j in range(3))
    state = []
    for j, u in enumerate((q_u, k_u)):
        g = jnp.where(first_rows, gains[j : j + 1, :], gains[j + 2 : j + 3, :])
        r = lax.rsqrt(head_sums(u * u, low) / hd + norm_eps)
        state.append((u, g, r, (u * r * g).astype(BF)))
    return state[0], state[1], v_u.astype(BF)


def head_probs(q, k, low, bias, scale):
    scores = dot_rows(jnp.where(low, q, jnp.zeros_like(q)), k) * scale + bias
    exponent = jnp.exp(scores)
    return exponent / jnp.sum(exponent, -1, keepdims=True)


def row_kinds(image, padded, length):
    first_rows = lax.broadcasted_iota(jnp.int32, (padded, 1), 0) < image
    keys = lax.broadcasted_iota(jnp.int32, (1, padded), 1)
    return first_rows, jnp.where(keys < length, 0.0, -1e30).astype(F32)


def attention_kernel(ui, ut, gains, oi, ot, *, length, hd, pairs):
    image = ui.shape[1]
    padded = image + ut.shape[1]
    model = pairs * 2 * hd
    low = lanes_of(hd)
    first_rows, bias = row_kinds(image, padded, length)
    scale = hd**-0.5

    def one(at):
        (_, _, _, q), (_, _, _, k), v = pair_state(ui, ut, gains, at, model, hd, low, first_rows)
        both = []
        for mask in (low, jnp.logical_not(low)):
            probs = head_probs(q, k, mask, bias, scale).astype(BF)
            both.append(dot_plain(probs, v))
        out = jnp.where(low, both[0], both[1]).astype(BF)
        oi[0, :, pl.ds(at, 2 * hd)] = out[:image]
        ot[0, :, pl.ds(at, 2 * hd)] = out[image:]

    def step(i, carry):
        for j in range(2):
            one(pl.multiple_of((2 * i + j) * 2 * hd, 2 * hd))
        return carry

    lax.fori_loop(0, pairs // 2, step, 0)


def attention_back_kernel(ui, ut, gi, gt, gains, pi, pt, sums, gain_sums, *, length, hd, pairs):
    image = ui.shape[1]
    padded = image + ut.shape[1]
    wide = 2 * hd
    model = pairs * wide
    low = lanes_of(hd)
    first_rows, bias = row_kinds(image, padded, length)
    scale = hd**-0.5

    def one(at):
        (q_u, q_g, q_r, q), (k_u, k_g, k_r, k), v = pair_state(ui, ut, gains, at, model, hd, low, first_rows)
        grad = rows_of(gi, gt, at, wide)
        dqs, dks, dvs = [], [], []
        for mask in (low, jnp.logical_not(low)):
            probs = head_probs(q, k, mask, bias, scale)
            prob_grad = dot_rows(jnp.where(mask, grad, jnp.zeros_like(grad)), v)
            delta = jnp.sum(prob_grad * probs, -1, keepdims=True)
            score_grad = (probs * (prob_grad - delta)).astype(BF)
            dvs.append(dot_turned(probs.astype(BF), grad))
            dqs.append(dot_plain(score_grad, k))
            dks.append(dot_turned(score_grad, q))
        gain_rows = []
        for j, (u, g, r, pair) in enumerate(((q_u, q_g, q_r, dqs), (k_u, k_g, k_r, dks), (None, None, None, dvs))):
            t = jnp.where(low, pair[0], pair[1])
            if j < 2:
                t = t * scale
                grown = t * u * r
                gain_rows.append((jnp.sum(grown[:image], 0, keepdims=True), jnp.sum(grown[image:], 0, keepdims=True)))
                gt_ = g * t
                t = r * gt_ - u * (r * r * r) * (head_sums(u * gt_, low) / hd)
            t = t.astype(BF)
            pi[0, :, pl.ds(j * model + at, wide)] = t[:image]
            pt[0, :, pl.ds(j * model + at, wide)] = t[image:]
            wide_t = t.astype(F32)
            sums[0, 0:1, pl.ds(j * model + at, wide)] = jnp.sum(wide_t[:image], 0, keepdims=True)
            sums[0, 1:2, pl.ds(j * model + at, wide)] = jnp.sum(wide_t[image:], 0, keepdims=True)
        return jnp.concatenate([gain_rows[0][0], gain_rows[1][0], gain_rows[0][1], gain_rows[1][1]], 0)

    def step(i, total):
        for j in range(2):
            total = total + one(pl.multiple_of((2 * i + j) * wide, wide))
        return total

    gain_sums[0] = lax.fori_loop(0, pairs // 2, step, jnp.zeros((4, wide), F32))


def whole_block(x):
    return pl.BlockSpec((1,) + x.shape[1:], lambda i: (i, 0, 0))


def attention(u, gains, length):
    n, image, width = u[0].shape
    text = u[1].shape[1]
    hd = gains.shape[1] // 2
    model = width // 3
    outs = [jax.ShapeDtypeStruct((n, rows, model), BF) for rows in (image, text)]
    return pl.pallas_call(
        functools.partial(attention_kernel, length=length, hd=hd, pairs=model // (2 * hd)),
        grid=(n,),
        in_specs=[whole_block(u[0]), whole_block(u[1]), pl.BlockSpec(gains.shape, lambda i: (0, 0))],
        out_specs=[whole_block(t) for t in outs],
        out_shape=outs,
        name="attention",
    )(u[0], u[1], gains)


def attention_back(grads, u, gains, length):
    n, image, width = u[0].shape
    text = u[1].shape[1]
    hd = gains.shape[1] // 2
    model = width // 3
    outs = [jax.ShapeDtypeStruct((n, rows, width), BF) for rows in (image, text)]
    outs += [jax.ShapeDtypeStruct((n, 2, width), F32), jax.ShapeDtypeStruct((n, 4, 2 * hd), F32)]
    ins = [u[0], u[1], grads[0], grads[1]]
    pi, pt, sums, gain_sums = pl.pallas_call(
        functools.partial(attention_back_kernel, length=length, hd=hd, pairs=model // (2 * hd)),
        grid=(n,),
        in_specs=[whole_block(t) for t in ins] + [pl.BlockSpec(gains.shape, lambda i: (0, 0))],
        out_specs=[whole_block(t) for t in outs],
        out_shape=outs,
        name="attention_back",
    )(*ins, gains)
    gain = jnp.sum(gain_sums, 0)
    gain = (gain[:, :hd] + gain[:, hd:]).reshape(2, 2, hd)
    sums = jnp.sum(sums, 0)
    return [pi, pt], [sums[0], sums[1]], [gain[0], gain[1]]


def forward(x, mod, w, length):
    us, mixeds, saved = [], [], {}
    keep = {"x": x, "mod": mod}
    hidden = []
    for st in range(2):
        normed, _ = normalise(x[st].astype(F32))
        h = (normed * (1.0 + mod[:, st, 1][:, None]) + mod[:, st, 0][:, None]).astype(BF)
        h = gather_two(h)
        hidden.append(h)
        p = times(h, w["qkv"][st]) + w["b_qkv"][st]
        us.append(p)
    keep["hidden"], keep["u"] = hidden, us
    attended = attention(us, w["gain"], length)
    keep["attended"] = attended
    keep["branch"], keep["mixed"], keep["hidden_mlp"], keep["slope"], keep["act"], keep["mlp"] = [], [], [], [], [], []
    outs = []
    for st in range(2):
        branch = scatter_two(times(attended[st], w["out"][st])) + w["b_out"][st]
        mixed = x[st].astype(F32) + mod[:, st, 2][:, None] * branch
        normed, _ = normalise(mixed)
        h = (normed * (1.0 + mod[:, st, 4][:, None]) + mod[:, st, 3][:, None]).astype(BF)
        h = gather_four(h)
        pre = times(h, w["fc1"][st]) + w["b_fc1"][st]
        act, slope = gelu(pre)
        act, slope = act.astype(BF), slope.astype(BF)
        mlp = scatter_four(times(act, w["fc2"][st])) + w["b_fc2"][st]
        outs.append(mixed + mod[:, st, 5][:, None] * mlp)
        for name, value in (("branch", branch), ("mixed", mixed), ("hidden_mlp", h), ("slope", slope), ("act", act), ("mlp", mlp)):
            keep[name].append(value)
    return outs, keep


def backward_entry(up, keep):
    mod = keep["mod"]
    state = {"up": up, "mlp": [], "fc2": [], "gate": []}
    for st in range(2):
        mlp_grad = (mod[:, st, 5][:, None] * up[st]).astype(BF)
        state["fc2"].append(jnp.sum(mlp_grad.astype(F32), (0, 1)))
        state["gate"].append(jnp.sum(keep["mlp"][st] * up[st], 1))
        state["mlp"].append(gather_four(mlp_grad))
    return state


def backward_mlp(state, keep, w):
    mod = keep["mod"]
    state = dict(state, mixed_grad=[], late=[], pre=[], fc1=[])
    for st in range(2):
        act_grad = times_turned(state["mlp"][st], w["fc2"][st])
        pre_grad = (act_grad * keep["slope"][st].astype(F32)).astype(BF)
        state["fc1"].append(jnp.sum(pre_grad.astype(F32), (0, 1)))
        h_grad = scatter_four(times_turned(pre_grad, w["fc1"][st]))
        normed, inverse = normalise(keep["mixed"][st])
        back = normalise_back(h_grad * (1.0 + mod[:, st, 4][:, None]), normed, inverse)
        state["mixed_grad"].append(state["up"][st] + back)
        state["late"].append((jnp.sum(h_grad, 1), jnp.sum(h_grad * normed, 1), state["gate"][st]))
        state["pre"].append(pre_grad)
    return state


def backward_attention(state, keep, w, length):
    mod = keep["mod"]
    small = {"fc2": state["fc2"], "fc1": state["fc1"], "out": []}
    right = {"mlp": state["mlp"], "pre": state["pre"], "branch": []}
    attended_grads, gates = [], []
    for st in range(2):
        mixed_grad = state["mixed_grad"][st]
        branch_grad = (mod[:, st, 2][:, None] * mixed_grad).astype(BF)
        gates.append(jnp.sum(keep["branch"][st] * mixed_grad, 1))
        small["out"].append(jnp.sum(branch_grad.astype(F32), (0, 1)))
        branch_grad = gather_two(branch_grad)
        right["branch"].append(branch_grad)
        attended_grads.append(times_turned(branch_grad, w["out"][st]).astype(BF))
    right["qkv"], small["qkv"], small["gain"] = attention_back(attended_grads, keep["u"], w["gain"], length)
    input_grads, mod_grads = [], []
    for st in range(2):
        h_grad = scatter_two(times_turned(right["qkv"][st], w["qkv"][st]))
        normed, inverse = normalise(keep["x"][st].astype(F32))
        input_grads.append(
            state["mixed_grad"][st] + normalise_back(h_grad * (1.0 + mod[:, st, 1][:, None]), normed, inverse)
        )
        mod_grads.append(jnp.stack([jnp.sum(h_grad, 1), jnp.sum(h_grad * normed, 1), gates[st], *state["late"][st]], 1))
    return input_grads, jnp.stack(mod_grads, 1), small, right


def backward(up, keep, w, length):
    return backward_attention(backward_mlp(backward_entry(up, keep), keep, w), keep, w, length)


def place(pieces, slots, count):
    whole = jnp.zeros((count,) + pieces[0].shape, pieces[0].dtype)
    for piece, slot in zip(pieces, slots):
        whole = lax.dynamic_update_index_in_dim(whole, piece, slot, 0)
    return whole


def take(x, index, axis):
    return lax.dynamic_index_in_dim(x, index, axis, keepdims=False)


def column_blocks(x, blocks, groups, width, stream=None):
    streams, rows, _ = x.shape
    streams = streams if stream is None else 1
    per = len(blocks) // groups
    numbers = list(blocks) + [0 if stream is None else stream]

    def body(blocks_ref, x_ref, out_ref):
        out_ref[0] = x_ref[...]

    grid_spec = pltpu.PrefetchScalarGridSpec(
        num_scalar_prefetch=1,
        grid=(groups, per),
        in_specs=[pl.BlockSpec((streams, rows, width), lambda g, b, blocks: (blocks[len(numbers) - 1], 0, blocks[g * per + b]))],
        out_specs=pl.BlockSpec((1, streams, rows, width), lambda g, b, blocks: (g, 0, 0, b)),
    )
    out = jax.ShapeDtypeStruct((groups, streams, rows, per * width), x.dtype)
    table = jnp.stack(numbers).astype(jnp.int32)
    return pl.pallas_call(body, grid_spec=grid_spec, out_shape=out, name="column_blocks")(table, x)


def columns_back(x, numbers):
    groups, streams, rows, columns = x.shape
    per = len(numbers) // groups
    width = columns // per

    def body(numbers_ref, x_ref, out_ref):
        out_ref[...] = x_ref[0].astype(F32)

    grid_spec = pltpu.PrefetchScalarGridSpec(
        num_scalar_prefetch=1,
        grid=(groups, per),
        in_specs=[pl.BlockSpec((1, streams, rows, width), lambda g, b, numbers: (g, 0, 0, b))],
        out_specs=pl.BlockSpec((streams, rows, width), lambda g, b, numbers: (0, 0, numbers[g * per + b])),
    )
    out = jax.ShapeDtypeStruct((streams, rows, groups * columns), F32)
    table = jnp.stack(numbers).astype(jnp.int32)
    return pl.pallas_call(body, grid_spec=grid_spec, out_shape=out, name="columns_back")(table, x)


def interleave(own, other, core, blocks):
    streams, rows, columns = own.shape
    width = columns // blocks
    per = 2

    def body(core_ref, own_ref, other_ref, out_ref):
        ahead = core_ref[0] == 0
        a, b = own_ref[...].astype(F32), other_ref[...].astype(F32)
        first, second = jnp.where(ahead, a, b), jnp.where(ahead, b, a)
        for i in range(per):
            at = slice(i * width, (i + 1) * width)
            out_ref[:, :, 2 * i * width : (2 * i + 1) * width] = first[:, :, at]
            out_ref[:, :, (2 * i + 1) * width : (2 * i + 2) * width] = second[:, :, at]

    block = pl.BlockSpec((streams, rows, per * width), lambda i, core: (0, 0, i))
    grid_spec = pltpu.PrefetchScalarGridSpec(
        num_scalar_prefetch=1,
        grid=(blocks // per,),
        in_specs=[block, block],
        out_specs=pl.BlockSpec((streams, rows, 2 * per * width), lambda i, core: (0, 0, i)),
    )
    out = jax.ShapeDtypeStruct((streams, rows, 2 * columns), F32)
    return pl.pallas_call(body, grid_spec=grid_spec, out_shape=out, name="interleave")(core[None].astype(jnp.int32), own, other)


def assemble(pieces, count, rows, parity):
    arrays = []
    for st in range(2):
        whole = None
        for piece, relayed, slot, at in pieces:
            if relayed is None:
                block = piece[st]
            else:
                block = jnp.where(parity == st, piece, relayed)
            if whole is None:
                whole = jnp.zeros((count * rows, block.shape[1]), block.dtype)
            whole = lax.dynamic_update_slice_in_dim(whole, block, slot * rows + at, 0)
        arrays.append(whole)
    return arrays


def prepare(later, w_qkv, b_qkv, gain, w_out, b_out, w_fc1, b_fc1, w_fc2, b_fc2):
    sid = lax.axis_index("shard")
    core = sid % 2
    parity = lax.axis_index("replica") % 2
    rows, width = w_qkv.shape[1], w_qkv.shape[2]
    part = width // 12
    slots = (sid, sid ^ 1, sid ^ 2, sid ^ 3)

    def of_parity(x):
        return jnp.where(parity == 0, x[0], x[1])

    direct, relayed = [], []

    def fetch(send, x):
        x, _, _ = lax.optimization_barrier((x, direct[-1:], relayed[-2:-1]))
        direct.append(send(x))
        relayed.append(mate(direct[-1]))
        return direct[-1], relayed[-1]

    numbers = [j * 4 + h * 2 + (core if g == 0 else 1 - core) for g in range(2) for j in range(3) for h in range(2)]
    first = column_blocks(w_qkv, numbers[:6], 1, part, parity)[0, 0]
    vectors = (b_qkv, b_out, b_fc2, gain.reshape(2, -1))
    w_qkv, first, vectors, later = lax.optimization_barrier((w_qkv, first, vectors, later))
    packed = jnp.concatenate(vectors, 1)[None]
    opposite = far(packed)
    w_qkv, opposite = lax.optimization_barrier((w_qkv, opposite))
    second = column_blocks(w_qkv, numbers[6:], 1, part, parity)[0, 0]
    w_qkv, second = lax.optimization_barrier((w_qkv, second))
    theirs = column_blocks(w_qkv, numbers[6:], 1, part)[0]
    mine = column_blocks(w_qkv, numbers[:6], 1, part)[0]
    got = [fetch(far, first), fetch(across, second)]
    packed, opposite, _ = lax.optimization_barrier((packed, opposite, got[0][0]))
    packed = jnp.concatenate([packed, near(packed), opposite, near(opposite)], 0)
    w_out, w_fc1, packed = lax.optimization_barrier((w_out, w_fc1, packed))
    columns = w_fc1.shape[2] // 4
    away = [column_blocks(w_fc1, [slot], 1, columns, parity)[0, 0] for slot in slots[2:]]
    pieces = [(mine, None, slots[0], 0), (near(theirs), None, slots[1], 0)]
    pieces += [(*t, slots[2 + i], 0) for i, t in enumerate(got)]
    w = {"qkv": assemble(pieces, 4, rows, parity)}

    got = fetch(far, of_parity(w_out))
    pair = sid // 2
    w["out"] = assemble([(w_out, None, pair, 0), (*got, 1 - pair, 0)], 2, rows, parity)

    w_fc1, away, _ = lax.optimization_barrier((w_fc1, away, got[0]))
    blocks = [column_blocks(w_fc1, [slot], 1, columns)[0] for slot in slots[:2]]
    pieces = [(blocks[0], None, slots[0], 0), (near(blocks[1]), None, slots[1], 0)]
    pieces += [(*fetch(send, block), slot, 0) for send, block, slot in zip((far, across), away, slots[2:])]
    w["fc1"] = assemble(pieces, 4, rows, parity)
    w["fc2"] = [w_fc2[0], w_fc2[1]]

    packed = place([packed[j] for j in range(4)], slots, 4).astype(F32)
    flat, at = [], 0
    for vector in vectors:
        piece = packed[:, :, at : at + vector.shape[1]]
        at += vector.shape[1]
        flat.append(piece)
    b_qkv, b_out, b_fc2 = (jnp.concatenate([piece[j] for j in range(4)], 1) for piece in flat[:3])
    w["b_out"], w["b_fc2"], w["b_fc1"] = b_out, b_fc2, b_fc1.astype(F32)
    columns = [b_qkv[:, i * part : (i + 1) * part] for i in range(12)]
    w["b_qkv"] = jnp.where(core == 0, jnp.concatenate(columns[0::2], 1), jnp.concatenate(columns[1::2], 1))
    quarter = gain.shape[2]
    table = []
    for st in range(2):
        for j in range(2):
            row = [flat[3][i, st, j * quarter : (j + 1) * quarter] for i in range(4)]
            table.append(jnp.concatenate(row + row))
    w["gain"] = jnp.stack(table)
    return w, later


def weight_terms(left, right):
    total = None
    for a, b in zip(left, right):
        term = outer(a, b)
        total = term if total is None else total + term
    return total


def over_replicas(x):
    inner = x.shape[1:]
    x = x.reshape(-1, inner[-1])
    return lax.psum_scatter(x, "replica", scatter_dimension=0, tiled=True).reshape(inner)


def per_device(block_input, modulation, w_qkv, b_qkv, qk_gain, w_out, b_out, w_fc1, b_fc1, w_fc2, b_fc2, cotangent):
    section = lax.axis_index("section")
    first = section == 0
    sid = lax.axis_index("shard")
    core, row_pair = sid % 2, sid // 2
    count = lax.axis_size("replica")
    rid = lax.axis_index("replica")
    length = block_input.shape[2]
    padded = (length + 15) // 16 * 16
    later = (block_input, modulation, cotangent)
    w, (block_input, modulation, cotangent) = prepare(later, w_qkv[0], b_qkv[0], qk_gain[0], w_out[0], b_out[0], w_fc1[0], b_fc1[0], w_fc2[0], b_fc2[0])

    def padding(x):
        return jnp.pad(x, ((0, 0), (0, 0), (0, padded - length), (0, 0)))

    def streams(x):
        return list(split_rows(x))

    def choose(a, b):
        return jax.tree.map(lambda p, q: jnp.where(first, p, q), a, b)

    def relay(x, pairs):
        return [lax.ppermute(t.astype(BF), "section", pairs) for t in x]

    block_input = padding(block_input)
    cotangent = padding(cotangent)
    mod = modulation[0]
    middle_mod = jnp.where(first, mod[1], mod[0])
    up_pair, down_pair = [(0, 1)], [(1, 0)]

    out0, keep0 = forward(streams(block_input[0]), mod[0], w, length)
    out0, cotangent = lax.optimization_barrier((out0, cotangent))
    got = relay(out0, up_pair)
    out1, keep1 = forward(choose(streams(block_input[1]), got), middle_mod, w, length)
    got = relay(out1, up_pair)
    out2, keep2 = forward(got, mod[1], w, length)

    def zero_unless(cond, x):
        return [jnp.where(cond, t.astype(F32), 0.0) for t in x]

    grad0, mod_grad0, small0, right0 = backward(zero_unless(~first, streams(cotangent[0])), keep1, w, length)
    got = relay(grad0, down_pair)
    up = choose([t.astype(F32) for t in got], [t.astype(F32) for t in streams(cotangent[1])])
    keep_mid = choose(keep0, keep2)
    grad1, mod_grad1, small1, right1 = backward(up, keep_mid, w, length)
    got = relay(grad1, down_pair)
    last = backward_entry(zero_unless(first, got), keep1)

    def terms(left, early, late, st):
        return weight_terms((keep_mid[left][st], keep1[left][st]), (early[st], late[st])).astype(BF)

    mlp_ends = choose(last["mlp"], right0["mlp"])
    fc2 = [terms("act", right1["mlp"], mlp_ends, st) for st in range(2)]
    fc2 = [t.reshape(count, 1, -1, t.shape[1]) for t in fc2]
    last["mlp"], fc2 = lax.optimization_barrier((last["mlp"], fc2))
    last = backward_mlp(last, keep1, w)
    pre_ends = choose(last["pre"], right0["pre"])
    fc1 = []
    for st in range(2):
        t = terms("hidden_mlp", right1["pre"], pre_ends, st)
        fc1.append(jnp.swapaxes(t.reshape(4, count, -1, t.shape[1]), 0, 1))
    fc1 = jnp.stack(fc1, 1)
    last["mixed_grad"], fc1 = lax.optimization_barrier((last["mixed_grad"], fc1))
    fc2, fc1 = [over_replicas(t) for t in fc2], over_replicas(fc1)
    grad2, mod_grad2, small2, right2 = backward_attention(last, keep1, w, length)

    halves = []

    def over_far(t):
        t = t.reshape(2, -1, t.shape[1])
        sent, _ = lax.optimization_barrier((take(t, 1 - row_pair, 0), halves[-1:]))
        halves.append(far(sent))
        return (take(t, row_pair, 0).astype(F32) + halves[-1].astype(F32)).astype(BF)

    branch_ends, qkv_ends = choose(right2["branch"], right0["branch"]), choose(right2["qkv"], right0["qkv"])
    qkv, out = [], []
    for st in range(2):
        t = over_far(terms("attended", right1["branch"], branch_ends, st))
        out.append(t.reshape(count, -1, t.shape[1]))
    for st in range(2):
        t = over_far(terms("hidden", right1["qkv"], qkv_ends, st))
        qkv.append(jnp.swapaxes(t.reshape(2, count, -1, t.shape[1]), 0, 1))
    out, fc2, fc1 = lax.optimization_barrier((jnp.stack(out, 1), fc2, fc1))
    out = over_replicas(out)
    qkv, out = lax.optimization_barrier((jnp.stack(qkv, 1), out))
    qkv = over_replicas(qkv)
    out = out.astype(F32)
    fc2 = jnp.concatenate(fc2, 0).astype(F32)
    slots = [sid ^ j for j in range(4)]
    moved = []
    for j, send in ((0, lambda x: x), (1, near), (2, far), (3, across)):
        moved.append(send(take(fc1, slots[j], 1)))
    fc1 = columns_back(jnp.stack(moved), slots)

    qkv = interleave(take(qkv, core, 1), near(take(qkv, 1 - core, 1)), core, 6)

    small = jax.tree.map(lambda a, b, c: a + b + c, small0, small1, small2)
    pieces = []
    for st in range(2):
        cores = small["qkv"][st].reshape(6, 1, -1)
        cores = jnp.where(jnp.arange(2).reshape(1, 2, 1) == core, cores, 0.0).reshape(-1)
        quarter = small["fc1"][st].reshape(1, -1)
        quarter = jnp.where(jnp.arange(4).reshape(4, 1) == sid, quarter, 0.0).reshape(-1)
        pieces.append(jnp.concatenate([cores, small["out"][st], quarter, small["fc2"][st], small["gain"][st].reshape(-1)]))
    sizes = [w_qkv.shape[3], w_out.shape[3], w_fc1.shape[3], w_fc2.shape[3], w["gain"].shape[-1]]
    summed = total_of(jnp.stack(pieces), ("shard", "replica"))
    place_id = sid * count + rid
    vectors, at = [], 0
    for size in sizes:
        vectors.append(summed[:, at : at + size])
        at += size

    def own_block(x, axis):
        size = x.shape[axis] // (4 * count)
        return lax.dynamic_slice_in_dim(x, place_id * size, size, axis)

    blocks = [own_block(v, 1)[None] for v in vectors[:4]]
    gain = own_block(vectors[4].reshape(2, 2, -1), 2)[None]

    def joined(x):
        return jnp.concatenate(x, 1)[:, :length]

    activations = jnp.stack([joined(choose(out0, out1)), joined(choose(out1, out2))]).astype(BF)
    input_grads = jnp.stack([joined(choose(grad1, grad0)), joined(choose(grad2, grad1))])
    modulation_grad = jnp.stack([choose(mod_grad1, mod_grad0), choose(mod_grad2, mod_grad1)])
    return (
        activations[None],
        input_grads[None],
        modulation_grad[None],
        qkv[None],
        blocks[0],
        gain,
        out[None],
        blocks[1],
        fc1[None],
        blocks[2],
        fc2[None],
        blocks[3],
    )


def solution(mesh):
    every = ("shard", "replica")
    return jax.shard_map(
        per_device,
        mesh=mesh,
        in_specs=(
            P(None, every, None, None),
            P("section", None, every, None, None, None),
            P("section", None, "shard", None),
            P("section", None, "shard"),
            P("section", None, None, "shard"),
            P("section", None, "shard", None),
            P("section", None, "shard"),
            P("section", None, "shard", None),
            P("section", None, "shard"),
            P("section", None, "shard", None),
            P("section", None, "shard"),
            P(None, every, None, None),
        ),
        out_specs=(
            P("section", None, every, None, None),
            P("section", None, every, None, None),
            P("section", None, every, None, None, None),
            P("section", None, every, None),
            P("section", None, every),
            P("section", None, None, every),
            P("section", None, every, None),
            P("section", None, every),
            P("section", None, every, None),
            P("section", None, every),
            P("section", None, every, None),
            P("section", None, every),
        ),
        check_vma=False,
    )
```

```python
import functools

import jax
import jax.numpy as jnp
from jax import lax
from jax.experimental import pallas as pl
from jax.experimental.pallas import tpu as pltpu
from jax.sharding import PartitionSpec as P


IMG = 64
norm_eps = 1e-06
BF = jnp.bfloat16
F32 = jnp.float32


def times(x, w):
    n, rows, d = x.shape
    y = lax.dot_general(x.reshape(n * rows, d), w, (((1,), (0,)), ((), ())), preferred_element_type=F32)
    return y.reshape(n, rows, -1)


def times_turned(x, w):
    n, rows, k = x.shape
    y = lax.dot_general(x.reshape(n * rows, k), w, (((1,), (1,)), ((), ())), preferred_element_type=F32)
    return y.reshape(n, rows, -1)


def outer(a, b):
    a, b = (t.reshape(-1, t.shape[2]) for t in (a, b))
    return lax.dot_general(a, b, (((0,), (0,)), ((), ())), preferred_element_type=F32)


def near(x):
    return lax.ppermute(x, "shard", [(i, i ^ 1) for i in range(4)])


def far(x):
    return lax.ppermute(x, "shard", [(i, i ^ 2) for i in range(4)])


def across(x):
    return lax.ppermute(x, "shard", [(i, i ^ 3) for i in range(4)])


def mate(x):
    count = lax.axis_size("replica")
    return lax.ppermute(x, "replica", [(i, i ^ 1) for i in range(count)])


def gather_two(x):
    return jnp.concatenate([x, near(x)], 0)


def gather_four(x):
    other = far(x)
    return jnp.concatenate([x, near(x), other, near(other)], 0)


def scatter_two(parts):
    own = parts.shape[0] // 2
    return parts[:own] + near(parts[own:].astype(BF)).astype(F32)


def scatter_four(parts):
    own = parts.shape[0] // 4
    away = parts[2 * own : 3 * own] + near(parts[3 * own :].astype(BF)).astype(F32)
    away = far(away.astype(BF))
    here = parts[:own] + near(parts[own : 2 * own].astype(BF)).astype(F32)
    return here + away.astype(F32)


def both_times(x, w, bias, tile):
    n, d = x[0].shape[0], x[0].shape[2]
    k = w[0].shape[1]
    flat = [t.reshape(-1, d) for t in x]

    def body(x0, x1, w0, w1, b0, b1, o0, o1):
        for t, m, b, o in ((x0, w0, b0, o0), (x1, w1, b1, o1)):
            o[...] = dot_plain(t[...], m[...]) + b[...]

    whole = [pl.BlockSpec(t.shape, lambda i: (0, 0)) for t in flat]
    out = pl.pallas_call(
        body,
        grid=(k // tile,),
        in_specs=whole + [pl.BlockSpec((d, tile), lambda i: (0, i))] * 2 + [pl.BlockSpec((1, tile), lambda i: (0, i))] * 2,
        out_specs=[pl.BlockSpec((t.shape[0], tile), lambda i: (0, i)) for t in flat],
        out_shape=[jax.ShapeDtypeStruct((t.shape[0], k), F32) for t in flat],
        name="both_times",
    )(*flat, *w, *(b.reshape(1, -1) for b in bias))
    return [t.reshape(n, -1, k) for t in out]


def both_times_turned(x, w, tile):
    n, k = x[0].shape[0], x[0].shape[2]
    d = w[0].shape[0]
    flat = [t.reshape(-1, k) for t in x]

    def body(x0, x1, w0, w1, o0, o1):
        for t, m, o in ((x0, w0, o0), (x1, w1, o1)):
            o[...] = dot_rows(t[...], m[...])

    whole = [pl.BlockSpec(t.shape, lambda i: (0, 0)) for t in flat]
    out = pl.pallas_call(
        body,
        grid=(d // tile,),
        in_specs=whole + [pl.BlockSpec((tile, k), lambda i: (i, 0))] * 2,
        out_specs=[pl.BlockSpec((t.shape[0], tile), lambda i: (0, i)) for t in flat],
        out_shape=[jax.ShapeDtypeStruct((t.shape[0], d), F32) for t in flat],
        name="both_times_turned",
    )(*flat, *w)
    return [t.reshape(n, -1, d) for t in out]


def normalise(x):
    centred = x - jnp.mean(x, -1, keepdims=True)
    inverse = lax.rsqrt(jnp.mean(centred * centred, -1, keepdims=True) + norm_eps)
    return centred * inverse, inverse


def normalise_back(f, normed, inverse):
    return inverse * (
        f - jnp.mean(f, -1, keepdims=True) - normed * jnp.mean(f * normed, -1, keepdims=True)
    )


gelu_a = (2.0 / jnp.pi) ** 0.5
gelu_b = 0.044715


def gelu(v):
    square = v * v
    t = jnp.tanh(gelu_a * (v + gelu_b * square * v))
    half = 0.5 * (1.0 + t)
    return v * half, half + 0.5 * v * (1.0 - t * t) * gelu_a * (1.0 + 3.0 * gelu_b * square)


def total_of(x, axes):
    for axis in axes:
        count, step = lax.axis_size(axis), 1
        while step < count:
            x = x + lax.ppermute(x, axis, [(i, i ^ step) for i in range(count)])
            step *= 2
    return x


def split_rows(x):
    return (x[:, :IMG], x[:, IMG:])


def lanes_of(hd):
    return lax.broadcasted_iota(jnp.int32, (1, 2 * hd), 1) < hd


def head_sums(x, low):
    a = jnp.sum(jnp.where(low, x, 0.0), -1, keepdims=True)
    b = jnp.sum(jnp.where(low, 0.0, x), -1, keepdims=True)
    return jnp.where(low, a, b)


def rows_of(first, second, at, width):
    return jnp.concatenate([first[0, :, pl.ds(at, width)], second[0, :, pl.ds(at, width)]], 0)


def dot_rows(a, b):
    return lax.dot_general(a, b, (((1,), (1,)), ((), ())), preferred_element_type=F32)


def dot_plain(a, b):
    return lax.dot_general(a, b, (((1,), (0,)), ((), ())), preferred_element_type=F32)


def dot_turned(a, b):
    return lax.dot_general(a, b, (((0,), (0,)), ((), ())), preferred_element_type=F32)


def pair_state(ui, ut, gains, at, model, hd, low, first_rows):
    wide = 2 * hd
    q_u, k_u, v_u = (rows_of(ui, ut, j * model + at, wide) for j in range(3))
    state = []
    for j, u in enumerate((q_u, k_u)):
        g = jnp.where(first_rows, gains[j : j + 1, :], gains[j + 2 : j + 3, :])
        r = lax.rsqrt(head_sums(u * u, low) / hd + norm_eps)
        state.append((u, g, r, (u * r * g).astype(BF)))
    return state[0], state[1], v_u.astype(BF)


def head_probs(q, k, low, bias):
    exponent = jnp.exp(dot_rows(jnp.where(low, q, jnp.zeros_like(q)), k) + bias)
    return exponent * (1.0 / jnp.sum(exponent, -1, keepdims=True))


def row_kinds(image, padded, length):
    first_rows = lax.broadcasted_iota(jnp.int32, (padded, 1), 0) < image
    keys = lax.broadcasted_iota(jnp.int32, (1, padded), 1)
    return first_rows, jnp.where(keys < length, 0.0, -1e30).astype(F32)


def attention_kernel(ui, ut, gains, oi, ot, *, length, hd, pairs):
    image = ui.shape[1]
    padded = image + ut.shape[1]
    model = pairs * 2 * hd
    low = lanes_of(hd)
    first_rows, bias = row_kinds(image, padded, length)
    scale = hd**-0.5

    def one(at):
        (_, _, _, q), (_, _, _, k), v = pair_state(ui, ut, gains, at, model, hd, low, first_rows)
        both = []
        q = q * jnp.asarray(scale, BF)
        for mask in (low, jnp.logical_not(low)):
            probs = head_probs(q, k, mask, bias).astype(BF)
            both.append(dot_plain(probs, v))
        out = jnp.where(low, both[0], both[1]).astype(BF)
        oi[0, :, pl.ds(at, 2 * hd)] = out[:image]
        ot[0, :, pl.ds(at, 2 * hd)] = out[image:]

    def step(i, carry):
        for j in range(2):
            one(pl.multiple_of((2 * i + j) * 2 * hd, 2 * hd))
        return carry

    lax.fori_loop(0, pairs // 2, step, 0)


def attention_back_kernel(ui, ut, gi, gt, gains, pi, pt, sums, gain_sums, *, length, hd, pairs):
    image = ui.shape[1]
    padded = image + ut.shape[1]
    wide = 2 * hd
    model = pairs * wide
    low = lanes_of(hd)
    first_rows, bias = row_kinds(image, padded, length)
    scale = hd**-0.5

    def one(at):
        (q_u, q_g, q_r, q), (k_u, k_g, k_r, k), v = pair_state(ui, ut, gains, at, model, hd, low, first_rows)
        grad = rows_of(gi, gt, at, wide)
        dqs, dks, dvs = [], [], []
        scaled = q * jnp.asarray(scale, BF)
        for mask in (low, jnp.logical_not(low)):
            probs = head_probs(scaled, k, mask, bias)
            prob_grad = dot_rows(jnp.where(mask, grad, jnp.zeros_like(grad)), v)
            delta = jnp.sum(prob_grad * probs, -1, keepdims=True)
            score_grad = (probs * (prob_grad - delta)).astype(BF)
            dvs.append(dot_turned(probs.astype(BF), grad))
            dqs.append(dot_plain(score_grad, k))
            dks.append(dot_turned(score_grad, q))
        gain_rows = []
        for j, (u, g, r, pair) in enumerate(((q_u, q_g, q_r, dqs), (k_u, k_g, k_r, dks), (None, None, None, dvs))):
            t = jnp.where(low, pair[0], pair[1])
            if j < 2:
                t = t * scale
                grown = t * u * r
                gain_rows.append((jnp.sum(grown[:image], 0, keepdims=True), jnp.sum(grown[image:], 0, keepdims=True)))
                gt_ = g * t
                t = r * gt_ - u * (r * r * r) * (head_sums(u * gt_, low) / hd)
            t = t.astype(BF)
            pi[0, :, pl.ds(j * model + at, wide)] = t[:image]
            pt[0, :, pl.ds(j * model + at, wide)] = t[image:]
            wide_t = t.astype(F32)
            sums[0, 0:1, pl.ds(j * model + at, wide)] = jnp.sum(wide_t[:image], 0, keepdims=True)
            sums[0, 1:2, pl.ds(j * model + at, wide)] = jnp.sum(wide_t[image:], 0, keepdims=True)
        return jnp.concatenate([gain_rows[0][0], gain_rows[1][0], gain_rows[0][1], gain_rows[1][1]], 0)

    def step(i, total):
        for j in range(2):
            total = total + one(pl.multiple_of((2 * i + j) * wide, wide))
        return total

    gain_sums[0] = lax.fori_loop(0, pairs // 2, step, jnp.zeros((4, wide), F32))


def whole_block(x):
    return pl.BlockSpec((1,) + x.shape[1:], lambda i: (i, 0, 0))


def attention(u, gains, length):
    n, image, width = u[0].shape
    text = u[1].shape[1]
    hd = gains.shape[1] // 2
    model = width // 3
    outs = [jax.ShapeDtypeStruct((n, rows, model), BF) for rows in (image, text)]
    return pl.pallas_call(
        functools.partial(attention_kernel, length=length, hd=hd, pairs=model // (2 * hd)),
        grid=(n,),
        in_specs=[whole_block(u[0]), whole_block(u[1]), pl.BlockSpec(gains.shape, lambda i: (0, 0))],
        out_specs=[whole_block(t) for t in outs],
        out_shape=outs,
        name="attention",
    )(u[0], u[1], gains)


def attention_back(grads, u, gains, length):
    n, image, width = u[0].shape
    text = u[1].shape[1]
    hd = gains.shape[1] // 2
    model = width // 3
    outs = [jax.ShapeDtypeStruct((n, rows, width), BF) for rows in (image, text)]
    outs += [jax.ShapeDtypeStruct((n, 2, width), F32), jax.ShapeDtypeStruct((n, 4, 2 * hd), F32)]
    ins = [u[0], u[1], grads[0], grads[1]]
    pi, pt, sums, gain_sums = pl.pallas_call(
        functools.partial(attention_back_kernel, length=length, hd=hd, pairs=model // (2 * hd)),
        grid=(n,),
        in_specs=[whole_block(t) for t in ins] + [pl.BlockSpec(gains.shape, lambda i: (0, 0))],
        out_specs=[whole_block(t) for t in outs],
        out_shape=outs,
        name="attention_back",
    )(*ins, gains)
    gain = jnp.sum(gain_sums, 0)
    gain = (gain[:, :hd] + gain[:, hd:]).reshape(2, 2, hd)
    sums = jnp.sum(sums, 0)
    return [pi, pt], [sums[0], sums[1]], [gain[0], gain[1]]


def forward(x, mod, w, length):
    keep = {"x": x, "mod": mod}
    hidden = []
    for st in range(2):
        normed, _ = normalise(x[st].astype(F32))
        h = (normed * (1.0 + mod[:, st, 1][:, None]) + mod[:, st, 0][:, None]).astype(BF)
        h = gather_two(h)
        hidden.append(h)
    us = both_times(hidden, w["qkv"], w["b_qkv"], w["qkv"][0].shape[1] // 6)
    keep["hidden"], keep["u"] = hidden, us
    attended = attention(us, w["gain"], length)
    keep["attended"] = attended
    keep["branch"], keep["mixed"], keep["hidden_mlp"], keep["slope"], keep["act"], keep["mlp"] = [], [], [], [], [], []
    outs = []
    for st in range(2):
        branch = scatter_two(times(attended[st], w["out"][st])) + w["b_out"][st]
        mixed = x[st].astype(F32) + mod[:, st, 2][:, None] * branch
        normed, _ = normalise(mixed)
        h = (normed * (1.0 + mod[:, st, 4][:, None]) + mod[:, st, 3][:, None]).astype(BF)
        h = gather_four(h)
        pre = times(h, w["fc1"][st]) + w["b_fc1"][st]
        act, slope = gelu(pre)
        act, slope = act.astype(BF), slope.astype(BF)
        mlp = scatter_four(times(act, w["fc2"][st])) + w["b_fc2"][st]
        outs.append(mixed + mod[:, st, 5][:, None] * mlp)
        for name, value in (("branch", branch), ("mixed", mixed), ("hidden_mlp", h), ("slope", slope), ("act", act), ("mlp", mlp)):
            keep[name].append(value)
    return outs, keep


def backward_entry(up, keep):
    mod = keep["mod"]
    state = {"up": up, "mlp": [], "fc2": [], "gate": []}
    for st in range(2):
        mlp_grad = (mod[:, st, 5][:, None] * up[st]).astype(BF)
        state["fc2"].append(jnp.sum(mlp_grad.astype(F32), (0, 1)))
        state["gate"].append(jnp.sum(keep["mlp"][st] * up[st], 1))
        state["mlp"].append(gather_four(mlp_grad))
    return state


def backward_mlp(state, keep, w):
    mod = keep["mod"]
    state = dict(state, mixed_grad=[], late=[], pre=[], fc1=[])
    for st in range(2):
        act_grad = times_turned(state["mlp"][st], w["fc2"][st])
        pre_grad = (act_grad * keep["slope"][st].astype(F32)).astype(BF)
        state["fc1"].append(jnp.sum(pre_grad.astype(F32), (0, 1)))
        h_grad = scatter_four(times_turned(pre_grad, w["fc1"][st]))
        normed, inverse = normalise(keep["mixed"][st])
        back = normalise_back(h_grad * (1.0 + mod[:, st, 4][:, None]), normed, inverse)
        state["mixed_grad"].append(state["up"][st] + back)
        state["late"].append((jnp.sum(h_grad, 1), jnp.sum(h_grad * normed, 1), state["gate"][st]))
        state["pre"].append(pre_grad)
    return state


def backward_attention(state, keep, w, length):
    mod = keep["mod"]
    small = {"fc2": state["fc2"], "fc1": state["fc1"], "out": []}
    right = {"mlp": state["mlp"], "pre": state["pre"], "branch": []}
    attended_grads, gates = [], []
    for st in range(2):
        mixed_grad = state["mixed_grad"][st]
        branch_grad = (mod[:, st, 2][:, None] * mixed_grad).astype(BF)
        gates.append(jnp.sum(keep["branch"][st] * mixed_grad, 1))
        small["out"].append(jnp.sum(branch_grad.astype(F32), (0, 1)))
        branch_grad = gather_two(branch_grad)
        right["branch"].append(branch_grad)
        attended_grads.append(times_turned(branch_grad, w["out"][st]).astype(BF))
    right["qkv"], small["qkv"], small["gain"] = attention_back(attended_grads, keep["u"], w["gain"], length)
    input_grads, mod_grads = [], []
    h_grads = both_times_turned(right["qkv"], w["qkv"], w["qkv"][0].shape[0] // 6)
    for st in range(2):
        h_grad = scatter_two(h_grads[st])
        normed, inverse = normalise(keep["x"][st].astype(F32))
        input_grads.append(
            state["mixed_grad"][st] + normalise_back(h_grad * (1.0 + mod[:, st, 1][:, None]), normed, inverse)
        )
        mod_grads.append(jnp.stack([jnp.sum(h_grad, 1), jnp.sum(h_grad * normed, 1), gates[st], *state["late"][st]], 1))
    return input_grads, jnp.stack(mod_grads, 1), small, right


def backward(up, keep, w, length):
    return backward_attention(backward_mlp(backward_entry(up, keep), keep, w), keep, w, length)


def place(pieces, slots, count):
    whole = jnp.zeros((count,) + pieces[0].shape, pieces[0].dtype)
    for piece, slot in zip(pieces, slots):
        whole = lax.dynamic_update_index_in_dim(whole, piece, slot, 0)
    return whole


def take(x, index, axis):
    return lax.dynamic_index_in_dim(x, index, axis, keepdims=False)


def column_blocks(x, blocks, groups, width, stream=None):
    streams, rows, _ = x.shape
    streams = streams if stream is None else 1
    per = len(blocks) // groups
    numbers = list(blocks) + [0 if stream is None else stream]

    def body(blocks_ref, x_ref, out_ref):
        out_ref[0] = x_ref[...]

    grid_spec = pltpu.PrefetchScalarGridSpec(
        num_scalar_prefetch=1,
        grid=(groups, per),
        in_specs=[pl.BlockSpec((streams, rows, width), lambda g, b, blocks: (blocks[len(numbers) - 1], 0, blocks[g * per + b]))],
        out_specs=pl.BlockSpec((1, streams, rows, width), lambda g, b, blocks: (g, 0, 0, b)),
    )
    out = jax.ShapeDtypeStruct((groups, streams, rows, per * width), x.dtype)
    table = jnp.stack(numbers).astype(jnp.int32)
    return pl.pallas_call(body, grid_spec=grid_spec, out_shape=out, name="column_blocks")(table, x)


def columns_back(x, numbers):
    groups, streams, rows, columns = x.shape
    per = len(numbers) // groups
    width = columns // per

    def body(numbers_ref, x_ref, out_ref):
        out_ref[...] = x_ref[0].astype(F32)

    grid_spec = pltpu.PrefetchScalarGridSpec(
        num_scalar_prefetch=1,
        grid=(groups, per),
        in_specs=[pl.BlockSpec((1, streams, rows, width), lambda g, b, numbers: (g, 0, 0, b))],
        out_specs=pl.BlockSpec((streams, rows, width), lambda g, b, numbers: (0, 0, numbers[g * per + b])),
    )
    out = jax.ShapeDtypeStruct((streams, rows, groups * columns), F32)
    table = jnp.stack(numbers).astype(jnp.int32)
    return pl.pallas_call(body, grid_spec=grid_spec, out_shape=out, name="columns_back")(table, x)


def interleave(own, other, core, blocks):
    streams, rows, columns = own.shape
    width = columns // blocks
    per = 2

    def body(core_ref, own_ref, other_ref, out_ref):
        ahead = core_ref[0] == 0
        a, b = own_ref[...].astype(F32), other_ref[...].astype(F32)
        first, second = jnp.where(ahead, a, b), jnp.where(ahead, b, a)
        for i in range(per):
            at = slice(i * width, (i + 1) * width)
            out_ref[:, :, 2 * i * width : (2 * i + 1) * width] = first[:, :, at]
            out_ref[:, :, (2 * i + 1) * width : (2 * i + 2) * width] = second[:, :, at]

    block = pl.BlockSpec((streams, rows, per * width), lambda i, core: (0, 0, i))
    grid_spec = pltpu.PrefetchScalarGridSpec(
        num_scalar_prefetch=1,
        grid=(blocks // per,),
        in_specs=[block, block],
        out_specs=pl.BlockSpec((streams, rows, 2 * per * width), lambda i, core: (0, 0, i)),
    )
    out = jax.ShapeDtypeStruct((streams, rows, 2 * columns), F32)
    return pl.pallas_call(body, grid_spec=grid_spec, out_shape=out, name="interleave")(core[None].astype(jnp.int32), own, other)


def assemble(pieces, count, rows, parity):
    arrays = []
    for st in range(2):
        whole = None
        for piece, relayed, slot, at in pieces:
            if relayed is None:
                block = piece[st]
            else:
                block = jnp.where(parity == st, piece, relayed)
            if whole is None:
                whole = jnp.zeros((count * rows, block.shape[1]), block.dtype)
            whole = lax.dynamic_update_slice_in_dim(whole, block, slot * rows + at, 0)
        arrays.append(whole)
    return arrays


def prepare(later, w_qkv, b_qkv, gain, w_out, b_out, w_fc1, b_fc1, w_fc2, b_fc2):
    sid = lax.axis_index("shard")
    core = sid % 2
    parity = lax.axis_index("replica") % 2
    rows, width = w_qkv.shape[1], w_qkv.shape[2]
    part = width // 12
    slots = (sid, sid ^ 1, sid ^ 2, sid ^ 3)

    def of_parity(x):
        return jnp.where(parity == 0, x[0], x[1])

    direct, relayed = [], []

    def fetch(send, x):
        x, _, _ = lax.optimization_barrier((x, direct[-1:], relayed[-3:-2]))
        direct.append(send(x))
        relayed.append(mate(direct[-1]))
        return direct[-1], relayed[-1]

    numbers = [j * 4 + h * 2 + (core if g == 0 else 1 - core) for g in range(2) for j in range(3) for h in range(2)]
    first = column_blocks(w_qkv, numbers[:6], 1, part, parity)[0, 0]
    vectors = (b_qkv, b_out, b_fc2, gain.reshape(2, -1))
    w_qkv, first, vectors, later = lax.optimization_barrier((w_qkv, first, vectors, later))
    packed = jnp.concatenate(vectors, 1)[None]
    opposite = far(packed)
    w_qkv, opposite = lax.optimization_barrier((w_qkv, opposite))
    second = column_blocks(w_qkv, numbers[6:], 1, part, parity)[0, 0]
    w_qkv, second = lax.optimization_barrier((w_qkv, second))
    theirs = column_blocks(w_qkv, numbers[6:], 1, part)[0]
    mine = column_blocks(w_qkv, numbers[:6], 1, part)[0]
    got = [fetch(far, first), fetch(across, second)]
    packed, opposite, _ = lax.optimization_barrier((packed, opposite, got[0][0]))
    packed = jnp.concatenate([packed, near(packed), opposite, near(opposite)], 0)
    w_out, w_fc1, packed = lax.optimization_barrier((w_out, w_fc1, packed))
    columns = w_fc1.shape[2] // 4
    away = [column_blocks(w_fc1, [slot], 1, columns, parity)[0, 0] for slot in slots[2:]]
    pieces = [(mine, None, slots[0], 0), (near(theirs), None, slots[1], 0)]
    pieces += [(*t, slots[2 + i], 0) for i, t in enumerate(got)]
    w = {"qkv": assemble(pieces, 4, rows, parity)}

    got = fetch(far, of_parity(w_out))
    pair = sid // 2
    w["out"] = assemble([(w_out, None, pair, 0), (*got, 1 - pair, 0)], 2, rows, parity)

    w_fc1, away, _ = lax.optimization_barrier((w_fc1, away, got[0]))
    blocks = [column_blocks(w_fc1, [slot], 1, columns)[0] for slot in slots[:2]]
    pieces = [(blocks[0], None, slots[0], 0), (near(blocks[1]), None, slots[1], 0)]
    pieces += [(*fetch(send, block), slot, 0) for send, block, slot in zip((far, across), away, slots[2:])]
    w["fc1"] = assemble(pieces, 4, rows, parity)
    w["fc2"] = [w_fc2[0], w_fc2[1]]

    packed = place([packed[j] for j in range(4)], slots, 4).astype(F32)
    flat, at = [], 0
    for vector in vectors:
        piece = packed[:, :, at : at + vector.shape[1]]
        at += vector.shape[1]
        flat.append(piece)
    b_qkv, b_out, b_fc2 = (jnp.concatenate([piece[j] for j in range(4)], 1) for piece in flat[:3])
    w["b_out"], w["b_fc2"], w["b_fc1"] = b_out, b_fc2, b_fc1.astype(F32)
    columns = [b_qkv[:, i * part : (i + 1) * part] for i in range(12)]
    w["b_qkv"] = jnp.where(core == 0, jnp.concatenate(columns[0::2], 1), jnp.concatenate(columns[1::2], 1))
    quarter = gain.shape[2]
    table = []
    for st in range(2):
        for j in range(2):
            row = [flat[3][i, st, j * quarter : (j + 1) * quarter] for i in range(4)]
            table.append(jnp.concatenate(row + row))
    w["gain"] = jnp.stack(table)
    return w, later


def weight_terms(left, right):
    total = None
    for a, b in zip(left, right):
        term = outer(a, b)
        total = term if total is None else total + term
    return total


def over_replicas(x, inner):
    return lax.psum_scatter(x, "replica", scatter_dimension=0, tiled=True).reshape(inner)


def rows_only(x):
    return x.reshape(-1, x.shape[-1])


def per_device(block_input, modulation, w_qkv, b_qkv, qk_gain, w_out, b_out, w_fc1, b_fc1, w_fc2, b_fc2, cotangent):
    section = lax.axis_index("section")
    first = section == 0
    sid = lax.axis_index("shard")
    core, row_pair = sid % 2, sid // 2
    count = lax.axis_size("replica")
    rid = lax.axis_index("replica")
    length = block_input.shape[2]
    padded = (length + 15) // 16 * 16
    later = (block_input, modulation, cotangent)
    w, (block_input, modulation, cotangent) = prepare(later, w_qkv[0], b_qkv[0], qk_gain[0], w_out[0], b_out[0], w_fc1[0], b_fc1[0], w_fc2[0], b_fc2[0])

    def padding(x):
        return jnp.pad(x, ((0, 0), (0, 0), (0, padded - length), (0, 0)))

    def streams(x):
        return list(split_rows(x))

    def choose(a, b):
        return jax.tree.map(lambda p, q: jnp.where(first, p, q), a, b)

    def relay(x, pairs):
        return [lax.ppermute(t.astype(BF), "section", pairs) for t in x]

    block_input = padding(block_input)
    cotangent = padding(cotangent)
    mod = modulation[0]
    middle_mod = jnp.where(first, mod[1], mod[0])
    up_pair, down_pair = [(0, 1)], [(1, 0)]

    out0, keep0 = forward(streams(block_input[0]), mod[0], w, length)
    out0, cotangent = lax.optimization_barrier((out0, cotangent))
    got = relay(out0, up_pair)
    out1, keep1 = forward(choose(streams(block_input[1]), got), middle_mod, w, length)
    got = relay(out1, up_pair)
    out2, keep2 = forward(got, mod[1], w, length)

    def zero_unless(cond, x):
        return [jnp.where(cond, t.astype(F32), 0.0) for t in x]

    grad0, mod_grad0, small0, right0 = backward(zero_unless(~first, streams(cotangent[0])), keep1, w, length)
    got = relay(grad0, down_pair)
    up = choose([t.astype(F32) for t in got], [t.astype(F32) for t in streams(cotangent[1])])
    keep_mid = choose(keep0, keep2)
    keep_mid["slope"] = lax.optimization_barrier(keep_mid["slope"])
    grad1, mod_grad1, small1, right1 = backward(up, keep_mid, w, length)
    got = relay(grad1, down_pair)
    last = backward_entry(zero_unless(first, got), keep1)

    def terms(left, early, late, st):
        return weight_terms((keep_mid[left][st], keep1[left][st]), (early[st], late[st])).astype(BF)

    mlp_ends = choose(last["mlp"], right0["mlp"])
    fc2 = [terms("act", right1["mlp"], mlp_ends, st) for st in range(2)]
    last["mlp"], fc2 = lax.optimization_barrier((last["mlp"], fc2))
    last = backward_mlp(last, keep1, w)
    pre_ends = choose(last["pre"], right0["pre"])
    fc1 = []
    for st in range(2):
        t = terms("hidden_mlp", right1["pre"], pre_ends, st)
        fc1.append(jnp.swapaxes(t.reshape(4, count, -1, t.shape[1]), 0, 1))
    fc1 = jnp.stack(fc1, 1)
    fc1_inner, fc1 = fc1.shape[1:], rows_only(fc1)
    last["mixed_grad"], fc1 = lax.optimization_barrier((last["mixed_grad"], fc1))
    fc2, fc1 = [over_replicas(t, (1, -1, t.shape[1])) for t in fc2], over_replicas(fc1, fc1_inner)
    grad2, mod_grad2, small2, right2 = backward_attention(last, keep1, w, length)

    halves = []

    def over_far(t):
        t = t.reshape(2, -1, t.shape[1])
        sent, _ = lax.optimization_barrier((take(t, 1 - row_pair, 0), halves[-1:]))
        halves.append(far(sent))
        return (take(t, row_pair, 0).astype(F32) + halves[-1].astype(F32)).astype(BF)

    branch_ends, qkv_ends = choose(right2["branch"], right0["branch"]), choose(right2["qkv"], right0["qkv"])
    qkv, out = [], []
    for st in range(2):
        t = over_far(terms("attended", right1["branch"], branch_ends, st))
        out.append(t.reshape(count, -1, t.shape[1]))
    for st in range(2):
        t = over_far(terms("hidden", right1["qkv"], qkv_ends, st))
        qkv.append(jnp.swapaxes(t.reshape(2, count, -1, t.shape[1]), 0, 1))
    out, qkv = jnp.stack(out, 1), jnp.stack(qkv, 1)
    out_inner, qkv_inner = out.shape[1:], qkv.shape[1:]
    out, fc2, fc1 = lax.optimization_barrier((rows_only(out), fc2, fc1))
    out = over_replicas(out, out_inner)
    qkv, out = lax.optimization_barrier((rows_only(qkv), out))
    qkv = over_replicas(qkv, qkv_inner)
    out = out.astype(F32)
    fc2 = jnp.concatenate(fc2, 0).astype(F32)
    slots = [sid ^ j for j in range(4)]
    moved = []
    for j, send in ((0, lambda x: x), (1, near), (2, far), (3, across)):
        moved.append(send(take(fc1, slots[j], 1)))
    fc1 = columns_back(jnp.stack(moved), slots)

    small = jax.tree.map(lambda a, b, c: a + b + c, small0, small1, small2)
    pieces = []
    for st in range(2):
        cores = small["qkv"][st].reshape(6, 1, -1)
        cores = jnp.where(jnp.arange(2).reshape(1, 2, 1) == core, cores, 0.0).reshape(-1)
        quarter = small["fc1"][st].reshape(1, -1)
        quarter = jnp.where(jnp.arange(4).reshape(4, 1) == sid, quarter, 0.0).reshape(-1)
        pieces.append(jnp.concatenate([cores, small["out"][st], quarter, small["fc2"][st], small["gain"][st].reshape(-1)]))
    sizes = [w_qkv.shape[3], w_out.shape[3], w_fc1.shape[3], w_fc2.shape[3], w["gain"].shape[-1]]
    summed = total_of(jnp.stack(pieces), ("shard", "replica"))
    place_id = sid * count + rid
    vectors, at = [], 0
    for size in sizes:
        vectors.append(summed[:, at : at + size])
        at += size

    def own_block(x, axis):
        size = x.shape[axis] // (4 * count)
        return lax.dynamic_slice_in_dim(x, place_id * size, size, axis)

    blocks = [own_block(v, 1)[None] for v in vectors[:4]]
    gain = own_block(vectors[4].reshape(2, 2, -1), 2)[None]

    def joined(x):
        return jnp.concatenate(x, 1)[:, :length]

    activations = jnp.stack([joined(choose(out0, out1)), joined(choose(out1, out2))]).astype(BF)
    input_grads = jnp.stack([joined(choose(grad1, grad0)), joined(choose(grad2, grad1))])
    modulation_grad = jnp.stack([choose(mod_grad1, mod_grad0), choose(mod_grad2, mod_grad1)])
    others = (activations, input_grads, modulation_grad, blocks, gain, out, fc1, fc2)
    others, qkv = lax.optimization_barrier((others, qkv))
    activations, input_grads, modulation_grad, blocks, gain, out, fc1, fc2 = others
    qkv = interleave(take(qkv, core, 1), near(take(qkv, 1 - core, 1)), core, 6)
    return (
        activations[None],
        input_grads[None],
        modulation_grad[None],
        qkv[None],
        blocks[0],
        gain,
        out[None],
        blocks[1],
        fc1[None],
        blocks[2],
        fc2[None],
        blocks[3],
    )


def solution(mesh):
    every = ("shard", "replica")
    return jax.shard_map(
        per_device,
        mesh=mesh,
        in_specs=(
            P(None, every, None, None),
            P("section", None, every, None, None, None),
            P("section", None, "shard", None),
            P("section", None, "shard"),
            P("section", None, None, "shard"),
            P("section", None, "shard", None),
            P("section", None, "shard"),
            P("section", None, "shard", None),
            P("section", None, "shard"),
            P("section", None, "shard", None),
            P("section", None, "shard"),
            P(None, every, None, None),
        ),
        out_specs=(
            P("section", None, every, None, None),
            P("section", None, every, None, None),
            P("section", None, every, None, None, None),
            P("section", None, every, None),
            P("section", None, every),
            P("section", None, None, every),
            P("section", None, every, None),
            P("section", None, every),
            P("section", None, every, None),
            P("section", None, every),
            P("section", None, every, None),
            P("section", None, every),
        ),
        check_vma=False,
    )
```

```python
import functools

import jax
import jax.numpy as jnp
from jax import lax
from jax.experimental import pallas as pl
from jax.experimental.pallas import tpu as pltpu
from jax.sharding import PartitionSpec as P


IMG = 64
norm_eps = 1e-06
BF = jnp.bfloat16
F32 = jnp.float32


def times(x, w):
    n, rows, d = x.shape
    y = lax.dot_general(x.reshape(n * rows, d), w, (((1,), (0,)), ((), ())), preferred_element_type=F32)
    return y.reshape(n, rows, -1)


def times_turned(x, w):
    n, rows, k = x.shape
    y = lax.dot_general(x.reshape(n * rows, k), w, (((1,), (1,)), ((), ())), preferred_element_type=F32)
    return y.reshape(n, rows, -1)


def outer(a, b):
    a, b = (t.reshape(-1, t.shape[2]) for t in (a, b))
    return lax.dot_general(a, b, (((0,), (0,)), ((), ())), preferred_element_type=F32)


def near(x):
    return lax.ppermute(x, "shard", [(i, i ^ 1) for i in range(4)])


def far(x):
    return lax.ppermute(x, "shard", [(i, i ^ 2) for i in range(4)])


def across(x):
    return lax.ppermute(x, "shard", [(i, i ^ 3) for i in range(4)])


def mate(x):
    count = lax.axis_size("replica")
    return lax.ppermute(x, "replica", [(i, i ^ 1) for i in range(count)])


def gather_two(x):
    return jnp.concatenate([x, near(x)], 0)


def gather_four(x):
    other = far(x)
    return jnp.concatenate([x, near(x), other, near(other)], 0)


def scatter_two(parts):
    own = parts.shape[0] // 2
    return parts[:own] + near(parts[own:].astype(BF)).astype(F32)


def scatter_four(parts):
    own = parts.shape[0] // 4
    away = parts[2 * own : 3 * own] + near(parts[3 * own :].astype(BF)).astype(F32)
    away = far(away.astype(BF))
    here = parts[:own] + near(parts[own : 2 * own].astype(BF)).astype(F32)
    return here + away.astype(F32)


def normalise(x):
    centred = x - jnp.mean(x, -1, keepdims=True)
    inverse = lax.rsqrt(jnp.mean(centred * centred, -1, keepdims=True) + norm_eps)
    return centred * inverse, inverse


def normalise_back(f, normed, inverse):
    return inverse * (
        f - jnp.mean(f, -1, keepdims=True) - normed * jnp.mean(f * normed, -1, keepdims=True)
    )


gelu_a = (2.0 / jnp.pi) ** 0.5
gelu_b = 0.044715


def gelu(v):
    square = v * v
    t = jnp.tanh(gelu_a * (v + gelu_b * square * v))
    half = 0.5 * (1.0 + t)
    return v * half, half + 0.5 * v * (1.0 - t * t) * gelu_a * (1.0 + 3.0 * gelu_b * square)


def total_of(x, axes):
    for axis in axes:
        count, step = lax.axis_size(axis), 1
        while step < count:
            x = x + lax.ppermute(x, axis, [(i, i ^ step) for i in range(count)])
            step *= 2
    return x


def split_rows(x):
    return (x[:, :IMG], x[:, IMG:])


def lanes_of(hd):
    return lax.broadcasted_iota(jnp.int32, (1, 2 * hd), 1) < hd


def head_sums(x, low):
    a = jnp.sum(jnp.where(low, x, 0.0), -1, keepdims=True)
    b = jnp.sum(jnp.where(low, 0.0, x), -1, keepdims=True)
    return jnp.where(low, a, b)


def rows_of(first, second, at, width):
    return jnp.concatenate([first[0, :, pl.ds(at, width)], second[0, :, pl.ds(at, width)]], 0)


def dot_rows(a, b):
    return lax.dot_general(a, b, (((1,), (1,)), ((), ())), preferred_element_type=F32)


def dot_plain(a, b):
    return lax.dot_general(a, b, (((1,), (0,)), ((), ())), preferred_element_type=F32)


def dot_turned(a, b):
    return lax.dot_general(a, b, (((0,), (0,)), ((), ())), preferred_element_type=F32)


def pair_state(ui, ut, gains, at, model, hd, low, first_rows):
    wide = 2 * hd
    q_u, k_u, v_u = (rows_of(ui, ut, j * model + at, wide) for j in range(3))
    state = []
    for j, u in enumerate((q_u, k_u)):
        g = jnp.where(first_rows, gains[j : j + 1, :], gains[j + 2 : j + 3, :])
        r = lax.rsqrt(head_sums(u * u, low) / hd + norm_eps)
        state.append((u, g, r, (u * r * g).astype(BF)))
    return state[0], state[1], v_u.astype(BF)


def head_probs(q, k, low, bias):
    exponent = jnp.exp(dot_rows(jnp.where(low, q, jnp.zeros_like(q)), k) + bias)
    return exponent * (1.0 / jnp.sum(exponent, -1, keepdims=True))


def row_kinds(image, padded, length):
    first_rows = lax.broadcasted_iota(jnp.int32, (padded, 1), 0) < image
    keys = lax.broadcasted_iota(jnp.int32, (1, padded), 1)
    return first_rows, jnp.where(keys < length, 0.0, -1e30).astype(F32)


def attention_kernel(ui, ut, gains, oi, ot, *, length, hd, pairs):
    image = ui.shape[1]
    padded = image + ut.shape[1]
    model = pairs * 2 * hd
    low = lanes_of(hd)
    first_rows, bias = row_kinds(image, padded, length)
    scale = hd**-0.5

    def one(at):
        (_, _, _, q), (_, _, _, k), v = pair_state(ui, ut, gains, at, model, hd, low, first_rows)
        both = []
        q = q * jnp.asarray(scale, BF)
        for mask in (low, jnp.logical_not(low)):
            probs = head_probs(q, k, mask, bias).astype(BF)
            both.append(dot_plain(probs, v))
        out = jnp.where(low, both[0], both[1]).astype(BF)
        oi[0, :, pl.ds(at, 2 * hd)] = out[:image]
        ot[0, :, pl.ds(at, 2 * hd)] = out[image:]

    def step(i, carry):
        for j in range(2):
            one(pl.multiple_of((2 * i + j) * 2 * hd, 2 * hd))
        return carry

    lax.fori_loop(0, pairs // 2, step, 0)


def attention_back_kernel(ui, ut, gi, gt, gains, pi, pt, sums, gain_sums, *, length, hd, pairs):
    image = ui.shape[1]
    padded = image + ut.shape[1]
    wide = 2 * hd
    model = pairs * wide
    low = lanes_of(hd)
    first_rows, bias = row_kinds(image, padded, length)
    scale = hd**-0.5

    def one(at):
        (q_u, q_g, q_r, q), (k_u, k_g, k_r, k), v = pair_state(ui, ut, gains, at, model, hd, low, first_rows)
        grad = rows_of(gi, gt, at, wide)
        dqs, dks, dvs = [], [], []
        scaled = q * jnp.asarray(scale, BF)
        for mask in (low, jnp.logical_not(low)):
            probs = head_probs(scaled, k, mask, bias)
            prob_grad = dot_rows(jnp.where(mask, grad, jnp.zeros_like(grad)), v)
            delta = jnp.sum(prob_grad * probs, -1, keepdims=True)
            score_grad = (probs * (prob_grad - delta)).astype(BF)
            dvs.append(dot_turned(probs.astype(BF), grad))
            dqs.append(dot_plain(score_grad, k))
            dks.append(dot_turned(score_grad, q))
        gain_rows = []
        for j, (u, g, r, pair) in enumerate(((q_u, q_g, q_r, dqs), (k_u, k_g, k_r, dks), (None, None, None, dvs))):
            t = jnp.where(low, pair[0], pair[1])
            if j < 2:
                t = t * scale
                grown = t * u * r
                gain_rows.append((jnp.sum(grown[:image], 0, keepdims=True), jnp.sum(grown[image:], 0, keepdims=True)))
                gt_ = g * t
                t = r * gt_ - u * (r * r * r) * (head_sums(u * gt_, low) / hd)
            t = t.astype(BF)
            pi[0, :, pl.ds(j * model + at, wide)] = t[:image]
            pt[0, :, pl.ds(j * model + at, wide)] = t[image:]
            wide_t = t.astype(F32)
            sums[0, 0:1, pl.ds(j * model + at, wide)] = jnp.sum(wide_t[:image], 0, keepdims=True)
            sums[0, 1:2, pl.ds(j * model + at, wide)] = jnp.sum(wide_t[image:], 0, keepdims=True)
        return jnp.concatenate([gain_rows[0][0], gain_rows[1][0], gain_rows[0][1], gain_rows[1][1]], 0)

    def step(i, total):
        for j in range(2):
            total = total + one(pl.multiple_of((2 * i + j) * wide, wide))
        return total

    gain_sums[0] = lax.fori_loop(0, pairs // 2, step, jnp.zeros((4, wide), F32))


def whole_block(x):
    return pl.BlockSpec((1,) + x.shape[1:], lambda i: (i, 0, 0))


def attention(u, gains, length):
    n, image, width = u[0].shape
    text = u[1].shape[1]
    hd = gains.shape[1] // 2
    model = width // 3
    outs = [jax.ShapeDtypeStruct((n, rows, model), BF) for rows in (image, text)]
    return pl.pallas_call(
        functools.partial(attention_kernel, length=length, hd=hd, pairs=model // (2 * hd)),
        grid=(n,),
        in_specs=[whole_block(u[0]), whole_block(u[1]), pl.BlockSpec(gains.shape, lambda i: (0, 0))],
        out_specs=[whole_block(t) for t in outs],
        out_shape=outs,
        name="attention",
    )(u[0], u[1], gains)


def attention_back(grads, u, gains, length):
    n, image, width = u[0].shape
    text = u[1].shape[1]
    hd = gains.shape[1] // 2
    model = width // 3
    outs = [jax.ShapeDtypeStruct((n, rows, width), BF) for rows in (image, text)]
    outs += [jax.ShapeDtypeStruct((n, 2, width), F32), jax.ShapeDtypeStruct((n, 4, 2 * hd), F32)]
    ins = [u[0], u[1], grads[0], grads[1]]
    pi, pt, sums, gain_sums = pl.pallas_call(
        functools.partial(attention_back_kernel, length=length, hd=hd, pairs=model // (2 * hd)),
        grid=(n,),
        in_specs=[whole_block(t) for t in ins] + [pl.BlockSpec(gains.shape, lambda i: (0, 0))],
        out_specs=[whole_block(t) for t in outs],
        out_shape=outs,
        name="attention_back",
    )(*ins, gains)
    gain = jnp.sum(gain_sums, 0)
    gain = (gain[:, :hd] + gain[:, hd:]).reshape(2, 2, hd)
    sums = jnp.sum(sums, 0)
    return [pi, pt], [sums[0], sums[1]], [gain[0], gain[1]]


def forward(x, mod, w, length):
    keep = {"x": x, "mod": mod}
    hidden, us = [], []
    for st in range(2):
        normed, _ = normalise(x[st].astype(F32))
        h = (normed * (1.0 + mod[:, st, 1][:, None]) + mod[:, st, 0][:, None]).astype(BF)
        h = gather_two(h)
        hidden.append(h)
        us.append(times(h, w["qkv"][st]) + w["b_qkv"][st])
    keep["hidden"], keep["u"] = hidden, us
    attended = attention(us, w["gain"], length)
    keep["attended"] = attended
    keep["branch"], keep["mixed"], keep["hidden_mlp"], keep["slope"], keep["act"], keep["mlp"] = [], [], [], [], [], []
    outs = []
    for st in range(2):
        branch = scatter_two(times(attended[st], w["out"][st])) + w["b_out"][st]
        mixed = x[st].astype(F32) + mod[:, st, 2][:, None] * branch
        normed, _ = normalise(mixed)
        h = (normed * (1.0 + mod[:, st, 4][:, None]) + mod[:, st, 3][:, None]).astype(BF)
        h = gather_four(h)
        pre = times(h, w["fc1"][st]) + w["b_fc1"][st]
        act, slope = gelu(pre)
        act, slope = act.astype(BF), slope.astype(BF)
        mlp = scatter_four(times(act, w["fc2"][st])) + w["b_fc2"][st]
        outs.append(mixed + mod[:, st, 5][:, None] * mlp)
        for name, value in (("branch", branch), ("mixed", mixed), ("hidden_mlp", h), ("slope", slope), ("act", act), ("mlp", mlp)):
            keep[name].append(value)
    return outs, keep


def backward_entry(up, keep):
    mod = keep["mod"]
    state = {"up": up, "mlp": [], "fc2": [], "gate": []}
    for st in range(2):
        mlp_grad = (mod[:, st, 5][:, None] * up[st]).astype(BF)
        state["fc2"].append(jnp.sum(mlp_grad.astype(F32), (0, 1)))
        state["gate"].append(jnp.sum(keep["mlp"][st] * up[st], 1))
        state["mlp"].append(gather_four(mlp_grad))
    return state


def backward_mlp(state, keep, w):
    mod = keep["mod"]
    state = dict(state, mixed_grad=[], late=[], pre=[], fc1=[])
    for st in range(2):
        act_grad = times_turned(state["mlp"][st], w["fc2"][st])
        pre_grad = (act_grad * keep["slope"][st].astype(F32)).astype(BF)
        state["fc1"].append(jnp.sum(pre_grad.astype(F32), (0, 1)))
        h_grad = scatter_four(times_turned(pre_grad, w["fc1"][st]))
        normed, inverse = normalise(keep["mixed"][st])
        back = normalise_back(h_grad * (1.0 + mod[:, st, 4][:, None]), normed, inverse)
        state["mixed_grad"].append(state["up"][st] + back)
        state["late"].append((jnp.sum(h_grad, 1), jnp.sum(h_grad * normed, 1), state["gate"][st]))
        state["pre"].append(pre_grad)
    return state


def backward_attention(state, keep, w, length):
    mod = keep["mod"]
    small = {"fc2": state["fc2"], "fc1": state["fc1"], "out": []}
    right = {"mlp": state["mlp"], "pre": state["pre"], "branch": []}
    attended_grads, gates = [], []
    for st in range(2):
        mixed_grad = state["mixed_grad"][st]
        branch_grad = (mod[:, st, 2][:, None] * mixed_grad).astype(BF)
        gates.append(jnp.sum(keep["branch"][st] * mixed_grad, 1))
        small["out"].append(jnp.sum(branch_grad.astype(F32), (0, 1)))
        branch_grad = gather_two(branch_grad)
        right["branch"].append(branch_grad)
        attended_grads.append(times_turned(branch_grad, w["out"][st]).astype(BF))
    right["qkv"], small["qkv"], small["gain"] = attention_back(attended_grads, keep["u"], w["gain"], length)
    input_grads, mod_grads = [], []
    for st in range(2):
        h_grad = scatter_two(times_turned(right["qkv"][st], w["qkv"][st]))
        normed, inverse = normalise(keep["x"][st].astype(F32))
        input_grads.append(
            state["mixed_grad"][st] + normalise_back(h_grad * (1.0 + mod[:, st, 1][:, None]), normed, inverse)
        )
        mod_grads.append(jnp.stack([jnp.sum(h_grad, 1), jnp.sum(h_grad * normed, 1), gates[st], *state["late"][st]], 1))
    return input_grads, jnp.stack(mod_grads, 1), small, right


def backward(up, keep, w, length):
    return backward_attention(backward_mlp(backward_entry(up, keep), keep, w), keep, w, length)


def place(pieces, slots, count):
    whole = jnp.zeros((count,) + pieces[0].shape, pieces[0].dtype)
    for piece, slot in zip(pieces, slots):
        whole = lax.dynamic_update_index_in_dim(whole, piece, slot, 0)
    return whole


def take(x, index, axis):
    return lax.dynamic_index_in_dim(x, index, axis, keepdims=False)


def column_blocks(x, blocks, groups, width, stream=None):
    streams, rows, _ = x.shape
    streams = streams if stream is None else 1
    per = len(blocks) // groups
    numbers = list(blocks) + [0 if stream is None else stream]

    def body(blocks_ref, x_ref, out_ref):
        out_ref[0] = x_ref[...]

    grid_spec = pltpu.PrefetchScalarGridSpec(
        num_scalar_prefetch=1,
        grid=(groups, per),
        in_specs=[pl.BlockSpec((streams, rows, width), lambda g, b, blocks: (blocks[len(numbers) - 1], 0, blocks[g * per + b]))],
        out_specs=pl.BlockSpec((1, streams, rows, width), lambda g, b, blocks: (g, 0, 0, b)),
    )
    out = jax.ShapeDtypeStruct((groups, streams, rows, per * width), x.dtype)
    table = jnp.stack(numbers).astype(jnp.int32)
    return pl.pallas_call(body, grid_spec=grid_spec, out_shape=out, name="column_blocks")(table, x)


def columns_back(x, numbers):
    groups, streams, rows, columns = x.shape
    per = len(numbers) // groups
    width = columns // per

    def body(numbers_ref, x_ref, out_ref):
        out_ref[...] = x_ref[0].astype(F32)

    grid_spec = pltpu.PrefetchScalarGridSpec(
        num_scalar_prefetch=1,
        grid=(groups, per),
        in_specs=[pl.BlockSpec((1, streams, rows, width), lambda g, b, numbers: (g, 0, 0, b))],
        out_specs=pl.BlockSpec((streams, rows, width), lambda g, b, numbers: (0, 0, numbers[g * per + b])),
    )
    out = jax.ShapeDtypeStruct((streams, rows, groups * columns), F32)
    table = jnp.stack(numbers).astype(jnp.int32)
    return pl.pallas_call(body, grid_spec=grid_spec, out_shape=out, name="columns_back")(table, x)


def interleave(own, other, core, blocks):
    streams, rows, columns = own.shape
    width = columns // blocks
    per = 2

    def body(core_ref, own_ref, other_ref, out_ref):
        ahead = core_ref[0] == 0
        a, b = own_ref[...].astype(F32), other_ref[...].astype(F32)
        first, second = jnp.where(ahead, a, b), jnp.where(ahead, b, a)
        for i in range(per):
            at = slice(i * width, (i + 1) * width)
            out_ref[:, :, 2 * i * width : (2 * i + 1) * width] = first[:, :, at]
            out_ref[:, :, (2 * i + 1) * width : (2 * i + 2) * width] = second[:, :, at]

    block = pl.BlockSpec((streams, rows, per * width), lambda i, core: (0, 0, i))
    grid_spec = pltpu.PrefetchScalarGridSpec(
        num_scalar_prefetch=1,
        grid=(blocks // per,),
        in_specs=[block, block],
        out_specs=pl.BlockSpec((streams, rows, 2 * per * width), lambda i, core: (0, 0, i)),
    )
    out = jax.ShapeDtypeStruct((streams, rows, 2 * columns), F32)
    return pl.pallas_call(body, grid_spec=grid_spec, out_shape=out, name="interleave")(core[None].astype(jnp.int32), own, other)


def assemble(pieces, count, rows, parity):
    arrays = []
    for st in range(2):
        whole = None
        for piece, relayed, slot, at in pieces:
            if relayed is None:
                block = piece[st]
            else:
                block = jnp.where(parity == st, piece, relayed)
            if whole is None:
                whole = jnp.zeros((count * rows, block.shape[1]), block.dtype)
            whole = lax.dynamic_update_slice_in_dim(whole, block, slot * rows + at, 0)
        arrays.append(whole)
    return arrays


def prepare(later, w_qkv, b_qkv, gain, w_out, b_out, w_fc1, b_fc1, w_fc2, b_fc2):
    sid = lax.axis_index("shard")
    core = sid % 2
    parity = lax.axis_index("replica") % 2
    rows, width = w_qkv.shape[1], w_qkv.shape[2]
    part = width // 12
    slots = (sid, sid ^ 1, sid ^ 2, sid ^ 3)

    def of_parity(x):
        return jnp.where(parity == 0, x[0], x[1])

    direct, relayed = [], []

    def fetch(send, x):
        x, _, _ = lax.optimization_barrier((x, direct[-1:], relayed[-3:-2]))
        direct.append(send(x))
        relayed.append(mate(direct[-1]))
        return direct[-1], relayed[-1]

    numbers = [j * 4 + h * 2 + (core if g == 0 else 1 - core) for g in range(2) for j in range(3) for h in range(2)]
    first = column_blocks(w_qkv, numbers[:6], 1, part, parity)[0, 0]
    vectors = (b_qkv, b_out, b_fc2, gain.reshape(2, -1))
    w_qkv, first, vectors, later = lax.optimization_barrier((w_qkv, first, vectors, later))
    packed = jnp.concatenate(vectors, 1)[None]
    opposite = far(packed)
    w_qkv, opposite = lax.optimization_barrier((w_qkv, opposite))
    second = column_blocks(w_qkv, numbers[6:], 1, part, parity)[0, 0]
    w_qkv, second = lax.optimization_barrier((w_qkv, second))
    theirs = column_blocks(w_qkv, numbers[6:], 1, part)[0]
    mine = column_blocks(w_qkv, numbers[:6], 1, part)[0]
    got = [fetch(far, first), fetch(across, second)]
    packed, opposite, _ = lax.optimization_barrier((packed, opposite, got[0][0]))
    packed = jnp.concatenate([packed, near(packed), opposite, near(opposite)], 0)
    w_out, w_fc1, packed = lax.optimization_barrier((w_out, w_fc1, packed))
    columns = w_fc1.shape[2] // 4
    away = [column_blocks(w_fc1, [slot], 1, columns, parity)[0, 0] for slot in slots[2:]]
    pieces = [(mine, None, slots[0], 0), (near(theirs), None, slots[1], 0)]
    pieces += [(*t, slots[2 + i], 0) for i, t in enumerate(got)]
    w = {"qkv": assemble(pieces, 4, rows, parity)}

    got = fetch(far, of_parity(w_out))
    pair = sid // 2
    w["out"] = assemble([(w_out, None, pair, 0), (*got, 1 - pair, 0)], 2, rows, parity)

    w_fc1, away, _ = lax.optimization_barrier((w_fc1, away, got[0]))
    blocks = [column_blocks(w_fc1, [slot], 1, columns)[0] for slot in slots[:2]]
    pieces = [(blocks[0], None, slots[0], 0), (near(blocks[1]), None, slots[1], 0)]
    pieces += [(*fetch(send, block), slot, 0) for send, block, slot in zip((far, across), away, slots[2:])]
    w["fc1"] = assemble(pieces, 4, rows, parity)
    w["fc2"] = [w_fc2[0], w_fc2[1]]

    packed = place([packed[j] for j in range(4)], slots, 4).astype(F32)
    flat, at = [], 0
    for vector in vectors:
        piece = packed[:, :, at : at + vector.shape[1]]
        at += vector.shape[1]
        flat.append(piece)
    b_qkv, b_out, b_fc2 = (jnp.concatenate([piece[j] for j in range(4)], 1) for piece in flat[:3])
    w["b_out"], w["b_fc2"], w["b_fc1"] = b_out, b_fc2, b_fc1.astype(F32)
    columns = [b_qkv[:, i * part : (i + 1) * part] for i in range(12)]
    w["b_qkv"] = jnp.where(core == 0, jnp.concatenate(columns[0::2], 1), jnp.concatenate(columns[1::2], 1))
    quarter = gain.shape[2]
    table = []
    for st in range(2):
        for j in range(2):
            row = [flat[3][i, st, j * quarter : (j + 1) * quarter] for i in range(4)]
            table.append(jnp.concatenate(row + row))
    w["gain"] = jnp.stack(table)
    return w, later


def weight_terms(left, right):
    total = None
    for a, b in zip(left, right):
        term = outer(a, b)
        total = term if total is None else total + term
    return total


def over_replicas(x, inner):
    return lax.psum_scatter(x, "replica", scatter_dimension=0, tiled=True).reshape(inner)


def rows_only(x):
    return x.reshape(-1, x.shape[-1])


def per_device(block_input, modulation, w_qkv, b_qkv, qk_gain, w_out, b_out, w_fc1, b_fc1, w_fc2, b_fc2, cotangent):
    section = lax.axis_index("section")
    first = section == 0
    sid = lax.axis_index("shard")
    core, row_pair = sid % 2, sid // 2
    count = lax.axis_size("replica")
    rid = lax.axis_index("replica")
    length = block_input.shape[2]
    padded = (length + 15) // 16 * 16
    later = (block_input, modulation, cotangent)
    w, (block_input, modulation, cotangent) = prepare(later, w_qkv[0], b_qkv[0], qk_gain[0], w_out[0], b_out[0], w_fc1[0], b_fc1[0], w_fc2[0], b_fc2[0])

    def padding(x):
        return jnp.pad(x, ((0, 0), (0, 0), (0, padded - length), (0, 0)))

    def streams(x):
        return list(split_rows(x))

    def choose(a, b):
        return jax.tree.map(lambda p, q: jnp.where(first, p, q), a, b)

    def relay(x, pairs):
        return [lax.ppermute(t.astype(BF), "section", pairs) for t in x]

    block_input = padding(block_input)
    cotangent = padding(cotangent)
    mod = modulation[0]
    middle_mod = jnp.where(first, mod[1], mod[0])
    up_pair, down_pair = [(0, 1)], [(1, 0)]

    out0, keep0 = forward(streams(block_input[0]), mod[0], w, length)
    out0, cotangent = lax.optimization_barrier((out0, cotangent))
    got = relay(out0, up_pair)
    out1, keep1 = forward(choose(streams(block_input[1]), got), middle_mod, w, length)
    got = relay(out1, up_pair)
    out2, keep2 = forward(got, mod[1], w, length)

    def zero_unless(cond, x):
        return [jnp.where(cond, t.astype(F32), 0.0) for t in x]

    grad0, mod_grad0, small0, right0 = backward(zero_unless(~first, streams(cotangent[0])), keep1, w, length)
    got = relay(grad0, down_pair)
    up = choose([t.astype(F32) for t in got], [t.astype(F32) for t in streams(cotangent[1])])
    keep_mid = choose(keep0, keep2)
    grad1, mod_grad1, small1, right1 = backward(up, keep_mid, w, length)
    got = relay(grad1, down_pair)
    last = backward_entry(zero_unless(first, got), keep1)

    def terms(left, early, late, st):
        return weight_terms((keep_mid[left][st], keep1[left][st]), (early[st], late[st])).astype(BF)

    mlp_ends = choose(last["mlp"], right0["mlp"])
    fc2 = [terms("act", right1["mlp"], mlp_ends, st) for st in range(2)]
    for st in range(2):
        last["mlp"][st], fc2[st] = lax.optimization_barrier((last["mlp"][st], fc2[st]))
    last = backward_mlp(last, keep1, w)
    pre_ends = choose(last["pre"], right0["pre"])
    fc1 = []
    for st in range(2):
        t = terms("hidden_mlp", right1["pre"], pre_ends, st)
        fc1.append(jnp.swapaxes(t.reshape(4, count, -1, t.shape[1]), 0, 1))
    fc1 = jnp.stack(fc1, 1)
    fc1_inner, fc1 = fc1.shape[1:], rows_only(fc1)
    last["mixed_grad"], fc1 = lax.optimization_barrier((last["mixed_grad"], fc1))
    fc2, fc1 = [over_replicas(t, (1, -1, t.shape[1])) for t in fc2], over_replicas(fc1, fc1_inner)
    grad2, mod_grad2, small2, right2 = backward_attention(last, keep1, w, length)
    right1["qkv"], right2["qkv"] = lax.optimization_barrier((right1["qkv"], right2["qkv"]))

    halves = []

    def over_far(t):
        t = t.reshape(2, -1, t.shape[1])
        sent, _ = lax.optimization_barrier((take(t, 1 - row_pair, 0), halves[-1:]))
        halves.append(far(sent))
        return (take(t, row_pair, 0).astype(F32) + halves[-1].astype(F32)).astype(BF)

    branch_ends, qkv_ends = choose(right2["branch"], right0["branch"]), choose(right2["qkv"], right0["qkv"])
    qkv, out = [], []
    for st in range(2):
        t = over_far(terms("attended", right1["branch"], branch_ends, st))
        out.append(t.reshape(count, -1, t.shape[1]))
    for st in range(2):
        t = over_far(terms("hidden", right1["qkv"], qkv_ends, st))
        qkv.append(jnp.swapaxes(t.reshape(2, count, -1, t.shape[1]), 0, 1))
    out, qkv = jnp.stack(out, 1), jnp.stack(qkv, 1)
    out_inner, qkv_inner = out.shape[1:], qkv.shape[1:]
    out, fc2, fc1 = lax.optimization_barrier((rows_only(out), fc2, fc1))
    out = over_replicas(out, out_inner)
    qkv, out = lax.optimization_barrier((rows_only(qkv), out))
    qkv = over_replicas(qkv, qkv_inner)
    out = out.astype(F32)
    fc2 = jnp.concatenate(fc2, 0).astype(F32)
    slots = [sid ^ j for j in range(4)]
    moved = []
    for j, send in ((0, lambda x: x), (1, near), (2, far), (3, across)):
        moved.append(send(take(fc1, slots[j], 1)))
    fc1 = columns_back(jnp.stack(moved), slots)

    small = jax.tree.map(lambda a, b, c: a + b + c, small0, small1, small2)
    pieces = []
    for st in range(2):
        cores = small["qkv"][st].reshape(6, 1, -1)
        cores = jnp.where(jnp.arange(2).reshape(1, 2, 1) == core, cores, 0.0).reshape(-1)
        quarter = small["fc1"][st].reshape(1, -1)
        quarter = jnp.where(jnp.arange(4).reshape(4, 1) == sid, quarter, 0.0).reshape(-1)
        pieces.append(jnp.concatenate([cores, small["out"][st], quarter, small["fc2"][st], small["gain"][st].reshape(-1)]))
    sizes = [w_qkv.shape[3], w_out.shape[3], w_fc1.shape[3], w_fc2.shape[3], w["gain"].shape[-1]]
    summed = total_of(jnp.stack(pieces), ("shard", "replica"))
    place_id = sid * count + rid
    vectors, at = [], 0
    for size in sizes:
        vectors.append(summed[:, at : at + size])
        at += size

    def own_block(x, axis):
        size = x.shape[axis] // (4 * count)
        return lax.dynamic_slice_in_dim(x, place_id * size, size, axis)

    blocks = [own_block(v, 1)[None] for v in vectors[:4]]
    gain = own_block(vectors[4].reshape(2, 2, -1), 2)[None]

    def joined(x):
        return jnp.concatenate(x, 1)[:, :length]

    activations = jnp.stack([joined(choose(out0, out1)), joined(choose(out1, out2))]).astype(BF)
    input_grads = jnp.stack([joined(choose(grad1, grad0)), joined(choose(grad2, grad1))])
    modulation_grad = jnp.stack([choose(mod_grad1, mod_grad0), choose(mod_grad2, mod_grad1)])
    others = (activations, input_grads, modulation_grad, blocks, gain, out, fc1, fc2)
    others, qkv = lax.optimization_barrier((others, qkv))
    activations, input_grads, modulation_grad, blocks, gain, out, fc1, fc2 = others
    qkv = interleave(take(qkv, core, 1), near(take(qkv, 1 - core, 1)), core, 6)
    return (
        activations[None],
        input_grads[None],
        modulation_grad[None],
        qkv[None],
        blocks[0],
        gain,
        out[None],
        blocks[1],
        fc1[None],
        blocks[2],
        fc2[None],
        blocks[3],
    )


def solution(mesh):
    every = ("shard", "replica")
    return jax.shard_map(
        per_device,
        mesh=mesh,
        in_specs=(
            P(None, every, None, None),
            P("section", None, every, None, None, None),
            P("section", None, "shard", None),
            P("section", None, "shard"),
            P("section", None, None, "shard"),
            P("section", None, "shard", None),
            P("section", None, "shard"),
            P("section", None, "shard", None),
            P("section", None, "shard"),
            P("section", None, "shard", None),
            P("section", None, "shard"),
            P(None, every, None, None),
        ),
        out_specs=(
            P("section", None, every, None, None),
            P("section", None, every, None, None),
            P("section", None, every, None, None, None),
            P("section", None, every, None),
            P("section", None, every),
            P("section", None, None, every),
            P("section", None, every, None),
            P("section", None, every),
            P("section", None, every, None),
            P("section", None, every),
            P("section", None, every, None),
            P("section", None, every),
        ),
        check_vma=False,
    )
```

```python
import functools

import jax
import jax.numpy as jnp
from jax import lax
from jax.experimental import pallas as pl
from jax.experimental.pallas import tpu as pltpu
from jax.sharding import PartitionSpec as P


IMG = 64
norm_eps = 1e-06
BF = jnp.bfloat16
F32 = jnp.float32


def times(x, w):
    n, rows, d = x.shape
    y = lax.dot_general(x.reshape(n * rows, d), w, (((1,), (0,)), ((), ())), preferred_element_type=F32)
    return y.reshape(n, rows, -1)


def times_turned(x, w):
    n, rows, k = x.shape
    y = lax.dot_general(x.reshape(n * rows, k), w, (((1,), (1,)), ((), ())), preferred_element_type=F32)
    return y.reshape(n, rows, -1)


def outer(a, b):
    a, b = (t.reshape(-1, t.shape[2]) for t in (a, b))
    return lax.dot_general(a, b, (((0,), (0,)), ((), ())), preferred_element_type=F32)


def near(x):
    return lax.ppermute(x, "shard", [(i, i ^ 1) for i in range(4)])


def far(x):
    return lax.ppermute(x, "shard", [(i, i ^ 2) for i in range(4)])


def across(x):
    return lax.ppermute(x, "shard", [(i, i ^ 3) for i in range(4)])


def mate(x):
    count = lax.axis_size("replica")
    return lax.ppermute(x, "replica", [(i, i ^ 1) for i in range(count)])


def gather_two(x):
    return jnp.concatenate([x, near(x)], 0)


def gather_four(x):
    other = far(x)
    return jnp.concatenate([x, near(x), other, near(other)], 0)


def scatter_two(parts):
    own = parts.shape[0] // 2
    return parts[:own] + near(parts[own:].astype(BF)).astype(F32)


def scatter_four(parts):
    own = parts.shape[0] // 4
    away = parts[2 * own : 3 * own] + near(parts[3 * own :].astype(BF)).astype(F32)
    away = far(away.astype(BF))
    here = parts[:own] + near(parts[own : 2 * own].astype(BF)).astype(F32)
    return here + away.astype(F32)


def normalise(x):
    centred = x - jnp.mean(x, -1, keepdims=True)
    inverse = lax.rsqrt(jnp.mean(centred * centred, -1, keepdims=True) + norm_eps)
    return centred * inverse, inverse


def normalise_back(f, normed, inverse):
    return inverse * (
        f - jnp.mean(f, -1, keepdims=True) - normed * jnp.mean(f * normed, -1, keepdims=True)
    )


gelu_a = (2.0 / jnp.pi) ** 0.5
gelu_b = 0.044715


def gelu(v):
    square = v * v
    t = jnp.tanh(gelu_a * (v + gelu_b * square * v))
    half = 0.5 * (1.0 + t)
    return v * half, half + 0.5 * v * (1.0 - t * t) * gelu_a * (1.0 + 3.0 * gelu_b * square)


def total_of(x, axes):
    for axis in axes:
        count, step = lax.axis_size(axis), 1
        while step < count:
            x = x + lax.ppermute(x, axis, [(i, i ^ step) for i in range(count)])
            step *= 2
    return x


def split_rows(x):
    return (x[:, :IMG], x[:, IMG:])


def lanes_of(hd):
    return lax.broadcasted_iota(jnp.int32, (1, 2 * hd), 1) < hd


def head_sums(x, low):
    a = jnp.sum(jnp.where(low, x, 0.0), -1, keepdims=True)
    b = jnp.sum(jnp.where(low, 0.0, x), -1, keepdims=True)
    return jnp.where(low, a, b)


def rows_of(first, second, at, width):
    return jnp.concatenate([first[0, :, pl.ds(at, width)], second[0, :, pl.ds(at, width)]], 0)


def dot_rows(a, b):
    return lax.dot_general(a, b, (((1,), (1,)), ((), ())), preferred_element_type=F32)


def dot_plain(a, b):
    return lax.dot_general(a, b, (((1,), (0,)), ((), ())), preferred_element_type=F32)


def dot_turned(a, b):
    return lax.dot_general(a, b, (((0,), (0,)), ((), ())), preferred_element_type=F32)


def pair_state(ui, ut, gains, at, model, hd, low, first_rows):
    wide = 2 * hd
    q_u, k_u, v_u = (rows_of(ui, ut, j * model + at, wide) for j in range(3))
    state = []
    for j, u in enumerate((q_u, k_u)):
        g = jnp.where(first_rows, gains[j : j + 1, :], gains[j + 2 : j + 3, :])
        r = lax.rsqrt(head_sums(u * u, low) / hd + norm_eps)
        state.append((u, g, r, (u * r * g).astype(BF)))
    return state[0], state[1], v_u.astype(BF)


def head_probs(q, k, low, bias):
    exponent = jnp.exp(dot_rows(jnp.where(low, q, jnp.zeros_like(q)), k) + bias)
    return exponent * (1.0 / jnp.sum(exponent, -1, keepdims=True))


def row_kinds(image, padded, length):
    first_rows = lax.broadcasted_iota(jnp.int32, (padded, 1), 0) < image
    keys = lax.broadcasted_iota(jnp.int32, (1, padded), 1)
    return first_rows, jnp.where(keys < length, 0.0, -1e30).astype(F32)


def attention_kernel(ui, ut, gains, oi, ot, *, length, hd, pairs):
    image = ui.shape[1]
    padded = image + ut.shape[1]
    model = pairs * 2 * hd
    low = lanes_of(hd)
    first_rows, bias = row_kinds(image, padded, length)
    scale = hd**-0.5

    def one(at):
        (_, _, _, q), (_, _, _, k), v = pair_state(ui, ut, gains, at, model, hd, low, first_rows)
        both = []
        q = q * jnp.asarray(scale, BF)
        for mask in (low, jnp.logical_not(low)):
            probs = head_probs(q, k, mask, bias).astype(BF)
            both.append(dot_plain(probs, v))
        out = jnp.where(low, both[0], both[1]).astype(BF)
        oi[0, :, pl.ds(at, 2 * hd)] = out[:image]
        ot[0, :, pl.ds(at, 2 * hd)] = out[image:]

    def step(i, carry):
        for j in range(2):
            one(pl.multiple_of((2 * i + j) * 2 * hd, 2 * hd))
        return carry

    lax.fori_loop(0, pairs // 2, step, 0)


def attention_back_kernel(ui, ut, gi, gt, gains, pi, pt, sums, gain_sums, *, length, hd, pairs):
    image = ui.shape[1]
    padded = image + ut.shape[1]
    wide = 2 * hd
    model = pairs * wide
    low = lanes_of(hd)
    first_rows, bias = row_kinds(image, padded, length)
    scale = hd**-0.5

    def one(at):
        (q_u, q_g, q_r, q), (k_u, k_g, k_r, k), v = pair_state(ui, ut, gains, at, model, hd, low, first_rows)
        grad = rows_of(gi, gt, at, wide)
        dqs, dks, dvs = [], [], []
        scaled = q * jnp.asarray(scale, BF)
        for mask in (low, jnp.logical_not(low)):
            probs = head_probs(scaled, k, mask, bias)
            prob_grad = dot_rows(jnp.where(mask, grad, jnp.zeros_like(grad)), v)
            delta = jnp.sum(prob_grad * probs, -1, keepdims=True)
            score_grad = (probs * (prob_grad - delta)).astype(BF)
            dvs.append(dot_turned(probs.astype(BF), grad))
            dqs.append(dot_plain(score_grad, k))
            dks.append(dot_turned(score_grad, q))
        gain_rows = []
        for j, (u, g, r, pair) in enumerate(((q_u, q_g, q_r, dqs), (k_u, k_g, k_r, dks), (None, None, None, dvs))):
            t = jnp.where(low, pair[0], pair[1])
            if j < 2:
                t = t * scale
                grown = t * u * r
                gain_rows.append((jnp.sum(grown[:image], 0, keepdims=True), jnp.sum(grown[image:], 0, keepdims=True)))
                gt_ = g * t
                t = r * gt_ - u * (r * r * r) * (head_sums(u * gt_, low) / hd)
            t = t.astype(BF)
            pi[0, :, pl.ds(j * model + at, wide)] = t[:image]
            pt[0, :, pl.ds(j * model + at, wide)] = t[image:]
            wide_t = t.astype(F32)
            sums[0, 0:1, pl.ds(j * model + at, wide)] = jnp.sum(wide_t[:image], 0, keepdims=True)
            sums[0, 1:2, pl.ds(j * model + at, wide)] = jnp.sum(wide_t[image:], 0, keepdims=True)
        return jnp.concatenate([gain_rows[0][0], gain_rows[1][0], gain_rows[0][1], gain_rows[1][1]], 0)

    def step(i, total):
        for j in range(2):
            total = total + one(pl.multiple_of((2 * i + j) * wide, wide))
        return total

    gain_sums[0] = lax.fori_loop(0, pairs // 2, step, jnp.zeros((4, wide), F32))


def whole_block(x):
    return pl.BlockSpec((1,) + x.shape[1:], lambda i: (i, 0, 0))


def attention(u, gains, length):
    n, image, width = u[0].shape
    text = u[1].shape[1]
    hd = gains.shape[1] // 2
    model = width // 3
    outs = [jax.ShapeDtypeStruct((n, rows, model), BF) for rows in (image, text)]
    return pl.pallas_call(
        functools.partial(attention_kernel, length=length, hd=hd, pairs=model // (2 * hd)),
        grid=(n,),
        in_specs=[whole_block(u[0]), whole_block(u[1]), pl.BlockSpec(gains.shape, lambda i: (0, 0))],
        out_specs=[whole_block(t) for t in outs],
        out_shape=outs,
        name="attention",
    )(u[0], u[1], gains)


def attention_back(grads, u, gains, length):
    n, image, width = u[0].shape
    text = u[1].shape[1]
    hd = gains.shape[1] // 2
    model = width // 3
    outs = [jax.ShapeDtypeStruct((n, rows, width), BF) for rows in (image, text)]
    outs += [jax.ShapeDtypeStruct((n, 2, width), F32), jax.ShapeDtypeStruct((n, 4, 2 * hd), F32)]
    ins = [u[0], u[1], grads[0], grads[1]]
    pi, pt, sums, gain_sums = pl.pallas_call(
        functools.partial(attention_back_kernel, length=length, hd=hd, pairs=model // (2 * hd)),
        grid=(n,),
        in_specs=[whole_block(t) for t in ins] + [pl.BlockSpec(gains.shape, lambda i: (0, 0))],
        out_specs=[whole_block(t) for t in outs],
        out_shape=outs,
        name="attention_back",
    )(*ins, gains)
    gain = jnp.sum(gain_sums, 0)
    gain = (gain[:, :hd] + gain[:, hd:]).reshape(2, 2, hd)
    sums = jnp.sum(sums, 0)
    return [pi, pt], [sums[0], sums[1]], [gain[0], gain[1]]


def forward(x, mod, w, length):
    keep = {"x": x, "mod": mod}
    hidden, us = [], []
    for st in range(2):
        normed, _ = normalise(x[st].astype(F32))
        h = (normed * (1.0 + mod[:, st, 1][:, None]) + mod[:, st, 0][:, None]).astype(BF)
        h = gather_two(h)
        hidden.append(h)
        us.append(times(h, w["qkv"][st]) + w["b_qkv"][st])
    keep["hidden"], keep["u"] = hidden, us
    attended = attention(us, w["gain"], length)
    keep["attended"] = attended
    keep["branch"], keep["mixed"], keep["hidden_mlp"], keep["slope"], keep["act"], keep["mlp"] = [], [], [], [], [], []
    outs = []
    for st in range(2):
        branch = scatter_two(times(attended[st], w["out"][st])) + w["b_out"][st]
        mixed = x[st].astype(F32) + mod[:, st, 2][:, None] * branch
        normed, _ = normalise(mixed)
        h = (normed * (1.0 + mod[:, st, 4][:, None]) + mod[:, st, 3][:, None]).astype(BF)
        h = gather_four(h)
        pre = times(h, w["fc1"][st]) + w["b_fc1"][st]
        act, slope = gelu(pre)
        act, slope = act.astype(BF), slope.astype(BF)
        mlp = scatter_four(times(act, w["fc2"][st])) + w["b_fc2"][st]
        outs.append(mixed + mod[:, st, 5][:, None] * mlp)
        for name, value in (("branch", branch), ("mixed", mixed), ("hidden_mlp", h), ("slope", slope), ("act", act), ("mlp", mlp)):
            keep[name].append(value)
    return outs, keep


def backward_entry(up, keep):
    mod = keep["mod"]
    state = {"up": up, "mlp": [], "fc2": [], "gate": []}
    for st in range(2):
        mlp_grad = (mod[:, st, 5][:, None] * up[st]).astype(BF)
        state["fc2"].append(jnp.sum(mlp_grad.astype(F32), (0, 1)))
        state["gate"].append(jnp.sum(keep["mlp"][st] * up[st], 1))
        state["mlp"].append(gather_four(mlp_grad))
    return state


def backward_mlp(state, keep, w):
    mod = keep["mod"]
    state = dict(state, mixed_grad=[], late=[], pre=[], fc1=[])
    for st in range(2):
        act_grad = times_turned(state["mlp"][st], w["fc2"][st])
        pre_grad = (act_grad * keep["slope"][st].astype(F32)).astype(BF)
        state["fc1"].append(jnp.sum(pre_grad.astype(F32), (0, 1)))
        h_grad = scatter_four(times_turned(pre_grad, w["fc1"][st]))
        normed, inverse = normalise(keep["mixed"][st])
        back = normalise_back(h_grad * (1.0 + mod[:, st, 4][:, None]), normed, inverse)
        state["mixed_grad"].append(state["up"][st] + back)
        state["late"].append((jnp.sum(h_grad, 1), jnp.sum(h_grad * normed, 1), state["gate"][st]))
        state["pre"].append(pre_grad)
    return state


def backward_attention(state, keep, w, length):
    mod = keep["mod"]
    small = {"fc2": state["fc2"], "fc1": state["fc1"], "out": []}
    right = {"mlp": state["mlp"], "pre": state["pre"], "branch": []}
    attended_grads, gates = [], []
    for st in range(2):
        mixed_grad = state["mixed_grad"][st]
        branch_grad = (mod[:, st, 2][:, None] * mixed_grad).astype(BF)
        gates.append(jnp.sum(keep["branch"][st] * mixed_grad, 1))
        small["out"].append(jnp.sum(branch_grad.astype(F32), (0, 1)))
        branch_grad = gather_two(branch_grad)
        right["branch"].append(branch_grad)
        attended_grads.append(times_turned(branch_grad, w["out"][st]).astype(BF))
    right["qkv"], small["qkv"], small["gain"] = attention_back(attended_grads, keep["u"], w["gain"], length)
    input_grads, mod_grads = [], []
    for st in range(2):
        h_grad = scatter_two(times_turned(right["qkv"][st], w["qkv"][st]))
        normed, inverse = normalise(keep["x"][st].astype(F32))
        input_grads.append(
            state["mixed_grad"][st] + normalise_back(h_grad * (1.0 + mod[:, st, 1][:, None]), normed, inverse)
        )
        mod_grads.append(jnp.stack([jnp.sum(h_grad, 1), jnp.sum(h_grad * normed, 1), gates[st], *state["late"][st]], 1))
    return input_grads, jnp.stack(mod_grads, 1), small, right


def backward(up, keep, w, length):
    return backward_attention(backward_mlp(backward_entry(up, keep), keep, w), keep, w, length)


def place(pieces, slots, count):
    whole = jnp.zeros((count,) + pieces[0].shape, pieces[0].dtype)
    for piece, slot in zip(pieces, slots):
        whole = lax.dynamic_update_index_in_dim(whole, piece, slot, 0)
    return whole


def take(x, index, axis):
    return lax.dynamic_index_in_dim(x, index, axis, keepdims=False)


def column_blocks(x, blocks, groups, width, stream=None):
    streams, rows, _ = x.shape
    streams = streams if stream is None else 1
    per = len(blocks) // groups
    numbers = list(blocks) + [0 if stream is None else stream]

    def body(blocks_ref, x_ref, out_ref):
        out_ref[0] = x_ref[...]

    grid_spec = pltpu.PrefetchScalarGridSpec(
        num_scalar_prefetch=1,
        grid=(groups, per),
        in_specs=[pl.BlockSpec((streams, rows, width), lambda g, b, blocks: (blocks[len(numbers) - 1], 0, blocks[g * per + b]))],
        out_specs=pl.BlockSpec((1, streams, rows, width), lambda g, b, blocks: (g, 0, 0, b)),
    )
    out = jax.ShapeDtypeStruct((groups, streams, rows, per * width), x.dtype)
    table = jnp.stack(numbers).astype(jnp.int32)
    return pl.pallas_call(body, grid_spec=grid_spec, out_shape=out, name="column_blocks")(table, x)


def columns_back(x, numbers):
    groups, streams, rows, columns = x.shape
    per = len(numbers) // groups
    width = columns // per

    def body(numbers_ref, x_ref, out_ref):
        out_ref[...] = x_ref[0].astype(F32)

    grid_spec = pltpu.PrefetchScalarGridSpec(
        num_scalar_prefetch=1,
        grid=(groups, per),
        in_specs=[pl.BlockSpec((1, streams, rows, width), lambda g, b, numbers: (g, 0, 0, b))],
        out_specs=pl.BlockSpec((streams, rows, width), lambda g, b, numbers: (0, 0, numbers[g * per + b])),
    )
    out = jax.ShapeDtypeStruct((streams, rows, groups * columns), F32)
    table = jnp.stack(numbers).astype(jnp.int32)
    return pl.pallas_call(body, grid_spec=grid_spec, out_shape=out, name="columns_back")(table, x)


def interleave(own, other, core, blocks):
    streams, rows, columns = own.shape
    width = columns // blocks
    per = 2

    def body(core_ref, own_ref, other_ref, out_ref):
        ahead = core_ref[0] == 0
        a, b = own_ref[...].astype(F32), other_ref[...].astype(F32)
        first, second = jnp.where(ahead, a, b), jnp.where(ahead, b, a)
        for i in range(per):
            at = slice(i * width, (i + 1) * width)
            out_ref[:, :, 2 * i * width : (2 * i + 1) * width] = first[:, :, at]
            out_ref[:, :, (2 * i + 1) * width : (2 * i + 2) * width] = second[:, :, at]

    block = pl.BlockSpec((streams, rows, per * width), lambda i, core: (0, 0, i))
    grid_spec = pltpu.PrefetchScalarGridSpec(
        num_scalar_prefetch=1,
        grid=(blocks // per,),
        in_specs=[block, block],
        out_specs=pl.BlockSpec((streams, rows, 2 * per * width), lambda i, core: (0, 0, i)),
    )
    out = jax.ShapeDtypeStruct((streams, rows, 2 * columns), F32)
    return pl.pallas_call(body, grid_spec=grid_spec, out_shape=out, name="interleave")(core[None].astype(jnp.int32), own, other)


def assemble(pieces, count, rows, parity):
    arrays = []
    for st in range(2):
        whole = None
        for piece, relayed, slot, at in pieces:
            if relayed is None:
                block = piece[st]
            else:
                block = jnp.where(parity == st, piece, relayed)
            if whole is None:
                whole = jnp.zeros((count * rows, block.shape[1]), block.dtype)
            whole = lax.dynamic_update_slice_in_dim(whole, block, slot * rows + at, 0)
        arrays.append(whole)
    return arrays


def prepare(later, w_qkv, b_qkv, gain, w_out, b_out, w_fc1, b_fc1, w_fc2, b_fc2):
    sid = lax.axis_index("shard")
    core = sid % 2
    parity = lax.axis_index("replica") % 2
    rows, width = w_qkv.shape[1], w_qkv.shape[2]
    part = width // 12
    slots = (sid, sid ^ 1, sid ^ 2, sid ^ 3)

    def of_parity(x):
        return jnp.where(parity == 0, x[0], x[1])

    direct, relayed = [], []

    def fetch(send, x):
        x, _, _ = lax.optimization_barrier((x, direct[-1:], relayed[-3:-2]))
        direct.append(send(x))
        relayed.append(mate(direct[-1]))
        return direct[-1], relayed[-1]

    numbers = [j * 4 + h * 2 + (core if g == 0 else 1 - core) for g in range(2) for j in range(3) for h in range(2)]
    first = column_blocks(w_qkv, numbers[:6], 1, part, parity)[0, 0]
    vectors = (b_qkv, b_out, b_fc2, gain.reshape(2, -1))
    w_qkv, first, vectors, later = lax.optimization_barrier((w_qkv, first, vectors, later))
    packed = jnp.concatenate(vectors, 1)[None]
    opposite = far(packed)
    w_qkv, opposite = lax.optimization_barrier((w_qkv, opposite))
    second = column_blocks(w_qkv, numbers[6:], 1, part, parity)[0, 0]
    w_qkv, second = lax.optimization_barrier((w_qkv, second))
    theirs = column_blocks(w_qkv, numbers[6:], 1, part)[0]
    mine = column_blocks(w_qkv, numbers[:6], 1, part)[0]
    got = [fetch(far, first), fetch(across, second)]
    packed, opposite, _ = lax.optimization_barrier((packed, opposite, got[0][0]))
    packed = jnp.concatenate([packed, near(packed), opposite, near(opposite)], 0)
    w_out, w_fc1, packed = lax.optimization_barrier((w_out, w_fc1, packed))
    columns = w_fc1.shape[2] // 4
    away = [column_blocks(w_fc1, [slots[j]], 1, columns, stream)[0, 0] for j, stream in ((2, parity), (3, parity), (3, 1 - parity))]
    pieces = [(mine, None, slots[0], 0), (near(theirs), None, slots[1], 0)]
    pieces += [(*t, slots[2 + i], 0) for i, t in enumerate(got)]
    w = {"qkv": assemble(pieces, 4, rows, parity)}

    got = fetch(far, of_parity(w_out))
    pair = sid // 2
    w["out"] = assemble([(w_out, None, pair, 0), (*got, 1 - pair, 0)], 2, rows, parity)

    w_fc1, away, _ = lax.optimization_barrier((w_fc1, away, got[0]))
    blocks = [column_blocks(w_fc1, [slot], 1, columns)[0] for slot in slots[:2]]
    pieces = [(blocks[0], None, slots[0], 0), (near(blocks[1]), None, slots[1], 0)]
    pieces.append((*fetch(far, away[0]), slots[2], 0))
    rest = lax.optimization_barrier((away[1], away[2], direct[-1]))
    pieces.append((across(rest[0]), across(rest[1]), slots[3], 0))
    w["fc1"] = assemble(pieces, 4, rows, parity)
    w["fc2"] = [w_fc2[0], w_fc2[1]]

    packed = place([packed[j] for j in range(4)], slots, 4).astype(F32)
    flat, at = [], 0
    for vector in vectors:
        piece = packed[:, :, at : at + vector.shape[1]]
        at += vector.shape[1]
        flat.append(piece)
    b_qkv, b_out, b_fc2 = (jnp.concatenate([piece[j] for j in range(4)], 1) for piece in flat[:3])
    w["b_out"], w["b_fc2"], w["b_fc1"] = b_out, b_fc2, b_fc1.astype(F32)
    columns = [b_qkv[:, i * part : (i + 1) * part] for i in range(12)]
    w["b_qkv"] = jnp.where(core == 0, jnp.concatenate(columns[0::2], 1), jnp.concatenate(columns[1::2], 1))
    quarter = gain.shape[2]
    table = []
    for st in range(2):
        for j in range(2):
            row = [flat[3][i, st, j * quarter : (j + 1) * quarter] for i in range(4)]
            table.append(jnp.concatenate(row + row))
    w["gain"] = jnp.stack(table)
    return w, later


def weight_terms(left, right):
    total = None
    for a, b in zip(left, right):
        term = outer(a, b)
        total = term if total is None else total + term
    return total


def over_replicas(x, inner):
    return lax.psum_scatter(x, "replica", scatter_dimension=0, tiled=True).reshape(inner)


def rows_only(x):
    return x.reshape(-1, x.shape[-1])


def per_device(block_input, modulation, w_qkv, b_qkv, qk_gain, w_out, b_out, w_fc1, b_fc1, w_fc2, b_fc2, cotangent):
    section = lax.axis_index("section")
    first = section == 0
    sid = lax.axis_index("shard")
    core, row_pair = sid % 2, sid // 2
    count = lax.axis_size("replica")
    rid = lax.axis_index("replica")
    length = block_input.shape[2]
    padded = (length + 15) // 16 * 16
    later = (block_input, modulation, cotangent)
    w, (block_input, modulation, cotangent) = prepare(later, w_qkv[0], b_qkv[0], qk_gain[0], w_out[0], b_out[0], w_fc1[0], b_fc1[0], w_fc2[0], b_fc2[0])

    def padding(x):
        return jnp.pad(x, ((0, 0), (0, 0), (0, padded - length), (0, 0)))

    def streams(x):
        return list(split_rows(x))

    def choose(a, b):
        return jax.tree.map(lambda p, q: jnp.where(first, p, q), a, b)

    def relay(x, pairs):
        return [lax.ppermute(t.astype(BF), "section", pairs) for t in x]

    block_input = padding(block_input)
    cotangent = padding(cotangent)
    mod = modulation[0]
    middle_mod = jnp.where(first, mod[1], mod[0])
    up_pair, down_pair = [(0, 1)], [(1, 0)]

    out0, keep0 = forward(streams(block_input[0]), mod[0], w, length)
    out0, cotangent = lax.optimization_barrier((out0, cotangent))
    got = relay(out0, up_pair)
    out1, keep1 = forward(choose(streams(block_input[1]), got), middle_mod, w, length)
    got = relay(out1, up_pair)
    out2, keep2 = forward(got, mod[1], w, length)

    def zero_unless(cond, x):
        return [jnp.where(cond, t.astype(F32), 0.0) for t in x]

    grad0, mod_grad0, small0, right0 = backward(zero_unless(~first, streams(cotangent[0])), keep1, w, length)
    got = relay(grad0, down_pair)
    up = choose([t.astype(F32) for t in got], [t.astype(F32) for t in streams(cotangent[1])])
    keep_mid = choose(keep0, keep2)
    grad1, mod_grad1, small1, right1 = backward(up, keep_mid, w, length)
    got = relay(grad1, down_pair)
    last = backward_entry(zero_unless(first, got), keep1)

    def terms(left, early, late, st):
        return weight_terms((keep_mid[left][st], keep1[left][st]), (early[st], late[st])).astype(BF)

    mlp_ends = choose(last["mlp"], right0["mlp"])
    fc2 = [terms("act", right1["mlp"], mlp_ends, st) for st in range(2)]
    for st in range(2):
        last["mlp"][st], fc2[st] = lax.optimization_barrier((last["mlp"][st], fc2[st]))
    last = backward_mlp(last, keep1, w)
    pre_ends = choose(last["pre"], right0["pre"])
    fc1 = []
    for st in range(2):
        t = terms("hidden_mlp", right1["pre"], pre_ends, st)
        fc1.append(jnp.swapaxes(t.reshape(4, count, -1, t.shape[1]), 0, 1))
    fc1 = jnp.stack(fc1, 1)
    fc1_inner, fc1 = fc1.shape[1:], rows_only(fc1)
    last["mixed_grad"], fc1 = lax.optimization_barrier((last["mixed_grad"], fc1))
    fc2, fc1 = [over_replicas(t, (1, -1, t.shape[1])) for t in fc2], over_replicas(fc1, fc1_inner)
    grad2, mod_grad2, small2, right2 = backward_attention(last, keep1, w, length)
    right1["qkv"], right2["qkv"] = lax.optimization_barrier((right1["qkv"], right2["qkv"]))

    halves = []

    def over_far(t):
        t = t.reshape(2, -1, t.shape[1])
        sent, _ = lax.optimization_barrier((take(t, 1 - row_pair, 0), halves[-1:]))
        halves.append(far(sent))
        return (take(t, row_pair, 0).astype(F32) + halves[-1].astype(F32)).astype(BF)

    branch_ends, qkv_ends = choose(right2["branch"], right0["branch"]), choose(right2["qkv"], right0["qkv"])
    qkv, out = [], []
    for st in range(2):
        t = over_far(terms("attended", right1["branch"], branch_ends, st))
        out.append(t.reshape(count, -1, t.shape[1]))
    for st in range(2):
        t = over_far(terms("hidden", right1["qkv"], qkv_ends, st))
        qkv.append(jnp.swapaxes(t.reshape(2, count, -1, t.shape[1]), 0, 1))
    out = jnp.stack(out, 1)
    out_inner, qkv_inner = out.shape[1:], (1,) + qkv[0].shape[1:]
    out, fc2, fc1 = lax.optimization_barrier((rows_only(out), fc2, fc1))
    out = over_replicas(out, out_inner)
    qkv[0], out = lax.optimization_barrier((rows_only(qkv[0]), out))
    qkv[0] = over_replicas(qkv[0], qkv_inner)
    qkv[1], qkv[0] = lax.optimization_barrier((rows_only(qkv[1]), qkv[0]))
    qkv = jnp.concatenate([qkv[0], over_replicas(qkv[1], qkv_inner)], 0)
    out = out.astype(F32)
    fc2 = jnp.concatenate(fc2, 0).astype(F32)
    slots = [sid ^ j for j in range(4)]
    moved = []
    for j, send in ((0, lambda x: x), (1, near), (2, far), (3, across)):
        moved.append(send(take(fc1, slots[j], 1)))
    fc1 = columns_back(jnp.stack(moved), slots)

    small = jax.tree.map(lambda a, b, c: a + b + c, small0, small1, small2)
    pieces = []
    for st in range(2):
        cores = small["qkv"][st].reshape(6, 1, -1)
        cores = jnp.where(jnp.arange(2).reshape(1, 2, 1) == core, cores, 0.0).reshape(-1)
        quarter = small["fc1"][st].reshape(1, -1)
        quarter = jnp.where(jnp.arange(4).reshape(4, 1) == sid, quarter, 0.0).reshape(-1)
        pieces.append(jnp.concatenate([cores, small["out"][st], quarter, small["fc2"][st], small["gain"][st].reshape(-1)]))
    sizes = [w_qkv.shape[3], w_out.shape[3], w_fc1.shape[3], w_fc2.shape[3], w["gain"].shape[-1]]
    summed = total_of(jnp.stack(pieces), ("shard", "replica"))
    place_id = sid * count + rid
    vectors, at = [], 0
    for size in sizes:
        vectors.append(summed[:, at : at + size])
        at += size

    def own_block(x, axis):
        size = x.shape[axis] // (4 * count)
        return lax.dynamic_slice_in_dim(x, place_id * size, size, axis)

    blocks = [own_block(v, 1)[None] for v in vectors[:4]]
    gain = own_block(vectors[4].reshape(2, 2, -1), 2)[None]

    def joined(x):
        return jnp.concatenate(x, 1)[:, :length]

    activations = jnp.stack([joined(choose(out0, out1)), joined(choose(out1, out2))]).astype(BF)
    input_grads = jnp.stack([joined(choose(grad1, grad0)), joined(choose(grad2, grad1))])
    modulation_grad = jnp.stack([choose(mod_grad1, mod_grad0), choose(mod_grad2, mod_grad1)])
    others = (activations, input_grads, modulation_grad, blocks, gain, out, fc1, fc2)
    others, qkv = lax.optimization_barrier((others, qkv))
    activations, input_grads, modulation_grad, blocks, gain, out, fc1, fc2 = others
    qkv = interleave(take(qkv, core, 1), near(take(qkv, 1 - core, 1)), core, 6)
    return (
        activations[None],
        input_grads[None],
        modulation_grad[None],
        qkv[None],
        blocks[0],
        gain,
        out[None],
        blocks[1],
        fc1[None],
        blocks[2],
        fc2[None],
        blocks[3],
    )


def solution(mesh):
    every = ("shard", "replica")
    return jax.shard_map(
        per_device,
        mesh=mesh,
        in_specs=(
            P(None, every, None, None),
            P("section", None, every, None, None, None),
            P("section", None, "shard", None),
            P("section", None, "shard"),
            P("section", None, None, "shard"),
            P("section", None, "shard", None),
            P("section", None, "shard"),
            P("section", None, "shard", None),
            P("section", None, "shard"),
            P("section", None, "shard", None),
            P("section", None, "shard"),
            P(None, every, None, None),
        ),
        out_specs=(
            P("section", None, every, None, None),
            P("section", None, every, None, None),
            P("section", None, every, None, None, None),
            P("section", None, every, None),
            P("section", None, every),
            P("section", None, None, every),
            P("section", None, every, None),
            P("section", None, every),
            P("section", None, every, None),
            P("section", None, every),
            P("section", None, every, None),
            P("section", None, every),
        ),
        check_vma=False,
    )
```

```python
import functools

import jax
import jax.numpy as jnp
from jax import lax
from jax.experimental import pallas as pl
from jax.experimental.pallas import tpu as pltpu
from jax.sharding import PartitionSpec as P


IMG = 64
norm_eps = 1e-06
BF = jnp.bfloat16
F32 = jnp.float32


def times(x, w):
    n, rows, d = x.shape
    y = lax.dot_general(x.reshape(n * rows, d), w, (((1,), (0,)), ((), ())), preferred_element_type=F32)
    return y.reshape(n, rows, -1)


def times_turned(x, w):
    n, rows, k = x.shape
    y = lax.dot_general(x.reshape(n * rows, k), w, (((1,), (1,)), ((), ())), preferred_element_type=F32)
    return y.reshape(n, rows, -1)


def outer(a, b):
    a, b = (t.reshape(-1, t.shape[2]) for t in (a, b))
    return lax.dot_general(a, b, (((0,), (0,)), ((), ())), preferred_element_type=F32)


def near(x):
    return lax.ppermute(x, "shard", [(i, i ^ 1) for i in range(4)])


def far(x):
    return lax.ppermute(x, "shard", [(i, i ^ 2) for i in range(4)])


def across(x):
    return lax.ppermute(x, "shard", [(i, i ^ 3) for i in range(4)])


def mate(x):
    count = lax.axis_size("replica")
    return lax.ppermute(x, "replica", [(i, i ^ 1) for i in range(count)])


def gather_two(x):
    return jnp.concatenate([x, near(x)], 0)


def gather_four(x):
    other = far(x)
    return jnp.concatenate([x, near(x), other, near(other)], 0)


def scatter_two(parts):
    own = parts.shape[0] // 2
    return parts[:own] + near(parts[own:].astype(BF)).astype(F32)


def scatter_four(parts):
    own = parts.shape[0] // 4
    away = parts[2 * own : 3 * own] + near(parts[3 * own :].astype(BF)).astype(F32)
    away = far(away.astype(BF))
    here = parts[:own] + near(parts[own : 2 * own].astype(BF)).astype(F32)
    return here + away.astype(F32)


def normalise(x):
    centred = x - jnp.mean(x, -1, keepdims=True)
    inverse = lax.rsqrt(jnp.mean(centred * centred, -1, keepdims=True) + norm_eps)
    return centred * inverse, inverse


def normalise_back(f, normed, inverse):
    return inverse * (
        f - jnp.mean(f, -1, keepdims=True) - normed * jnp.mean(f * normed, -1, keepdims=True)
    )


gelu_a = (2.0 / jnp.pi) ** 0.5
gelu_b = 0.044715


def gelu(v):
    square = v * v
    t = jnp.tanh(gelu_a * (v + gelu_b * square * v))
    half = 0.5 * (1.0 + t)
    return v * half, half + 0.5 * v * (1.0 - t * t) * gelu_a * (1.0 + 3.0 * gelu_b * square)


def total_of(x, axes):
    for axis in axes:
        count, step = lax.axis_size(axis), 1
        while step < count:
            x = x + lax.ppermute(x, axis, [(i, i ^ step) for i in range(count)])
            step *= 2
    return x


def split_rows(x):
    return (x[:, :IMG], x[:, IMG:])


def lanes_of(hd):
    return lax.broadcasted_iota(jnp.int32, (1, 2 * hd), 1) < hd


def head_sums(x, low):
    a = jnp.sum(jnp.where(low, x, 0.0), -1, keepdims=True)
    b = jnp.sum(jnp.where(low, 0.0, x), -1, keepdims=True)
    return jnp.where(low, a, b)


def rows_of(first, second, at, width):
    return jnp.concatenate([first[0, :, pl.ds(at, width)], second[0, :, pl.ds(at, width)]], 0)


def dot_rows(a, b):
    return lax.dot_general(a, b, (((1,), (1,)), ((), ())), preferred_element_type=F32)


def dot_plain(a, b):
    return lax.dot_general(a, b, (((1,), (0,)), ((), ())), preferred_element_type=F32)


def dot_turned(a, b):
    return lax.dot_general(a, b, (((0,), (0,)), ((), ())), preferred_element_type=F32)


def pair_state(ui, ut, gains, at, model, hd, low, first_rows):
    wide = 2 * hd
    q_u, k_u, v_u = (rows_of(ui, ut, j * model + at, wide) for j in range(3))
    state = []
    for j, u in enumerate((q_u, k_u)):
        g = jnp.where(first_rows, gains[j : j + 1, :], gains[j + 2 : j + 3, :])
        r = lax.rsqrt(head_sums(u * u, low) / hd + norm_eps)
        state.append((u, g, r, (u * r * g).astype(BF)))
    return state[0], state[1], v_u.astype(BF)


def head_probs(q, k, low, bias):
    exponent = jnp.exp(dot_rows(jnp.where(low, q, jnp.zeros_like(q)), k) + bias)
    return exponent * (1.0 / jnp.sum(exponent, -1, keepdims=True))


def row_kinds(image, padded, length):
    first_rows = lax.broadcasted_iota(jnp.int32, (padded, 1), 0) < image
    keys = lax.broadcasted_iota(jnp.int32, (1, padded), 1)
    return first_rows, jnp.where(keys < length, 0.0, -1e30).astype(F32)


def attention_kernel(ui, ut, gains, oi, ot, *, length, hd, pairs):
    image = ui.shape[1]
    padded = image + ut.shape[1]
    model = pairs * 2 * hd
    low = lanes_of(hd)
    first_rows, bias = row_kinds(image, padded, length)
    scale = hd**-0.5

    def one(at):
        (_, _, _, q), (_, _, _, k), v = pair_state(ui, ut, gains, at, model, hd, low, first_rows)
        both = []
        q = q * jnp.asarray(scale, BF)
        for mask in (low, jnp.logical_not(low)):
            probs = head_probs(q, k, mask, bias).astype(BF)
            both.append(dot_plain(probs, v))
        out = jnp.where(low, both[0], both[1]).astype(BF)
        oi[0, :, pl.ds(at, 2 * hd)] = out[:image]
        ot[0, :, pl.ds(at, 2 * hd)] = out[image:]

    def step(i, carry):
        for j in range(2):
            one(pl.multiple_of((2 * i + j) * 2 * hd, 2 * hd))
        return carry

    lax.fori_loop(0, pairs // 2, step, 0)


def attention_back_kernel(ui, ut, gi, gt, gains, pi, pt, sums, gain_sums, *, length, hd, pairs):
    image = ui.shape[1]
    padded = image + ut.shape[1]
    wide = 2 * hd
    model = pairs * wide
    low = lanes_of(hd)
    first_rows, bias = row_kinds(image, padded, length)
    scale = hd**-0.5

    def one(at):
        (q_u, q_g, q_r, q), (k_u, k_g, k_r, k), v = pair_state(ui, ut, gains, at, model, hd, low, first_rows)
        grad = rows_of(gi, gt, at, wide)
        dqs, dks, dvs = [], [], []
        scaled = q * jnp.asarray(scale, BF)
        for mask in (low, jnp.logical_not(low)):
            probs = head_probs(scaled, k, mask, bias)
            prob_grad = dot_rows(jnp.where(mask, grad, jnp.zeros_like(grad)), v)
            delta = jnp.sum(prob_grad * probs, -1, keepdims=True)
            score_grad = (probs * (prob_grad - delta)).astype(BF)
            dvs.append(dot_turned(probs.astype(BF), grad))
            dqs.append(dot_plain(score_grad, k))
            dks.append(dot_turned(score_grad, q))
        gain_rows = []
        for j, (u, g, r, pair) in enumerate(((q_u, q_g, q_r, dqs), (k_u, k_g, k_r, dks), (None, None, None, dvs))):
            t = jnp.where(low, pair[0], pair[1])
            if j < 2:
                t = t * scale
                grown = t * u * r
                gain_rows.append((jnp.sum(grown[:image], 0, keepdims=True), jnp.sum(grown[image:], 0, keepdims=True)))
                gt_ = g * t
                t = r * gt_ - u * (r * r * r) * (head_sums(u * gt_, low) / hd)
            t = t.astype(BF)
            pi[0, :, pl.ds(j * model + at, wide)] = t[:image]
            pt[0, :, pl.ds(j * model + at, wide)] = t[image:]
            wide_t = t.astype(F32)
            sums[0, 0:1, pl.ds(j * model + at, wide)] = jnp.sum(wide_t[:image], 0, keepdims=True)
            sums[0, 1:2, pl.ds(j * model + at, wide)] = jnp.sum(wide_t[image:], 0, keepdims=True)
        return jnp.concatenate([gain_rows[0][0], gain_rows[1][0], gain_rows[0][1], gain_rows[1][1]], 0)

    def step(i, total):
        for j in range(2):
            total = total + one(pl.multiple_of((2 * i + j) * wide, wide))
        return total

    gain_sums[0] = lax.fori_loop(0, pairs // 2, step, jnp.zeros((4, wide), F32))


def whole_block(x):
    return pl.BlockSpec((1,) + x.shape[1:], lambda i: (i, 0, 0))


def attention(u, gains, length):
    n, image, width = u[0].shape
    text = u[1].shape[1]
    hd = gains.shape[1] // 2
    model = width // 3
    outs = [jax.ShapeDtypeStruct((n, rows, model), BF) for rows in (image, text)]
    return pl.pallas_call(
        functools.partial(attention_kernel, length=length, hd=hd, pairs=model // (2 * hd)),
        grid=(n,),
        in_specs=[whole_block(u[0]), whole_block(u[1]), pl.BlockSpec(gains.shape, lambda i: (0, 0))],
        out_specs=[whole_block(t) for t in outs],
        out_shape=outs,
        name="attention",
    )(u[0], u[1], gains)


def attention_back(grads, u, gains, length):
    n, image, width = u[0].shape
    text = u[1].shape[1]
    hd = gains.shape[1] // 2
    model = width // 3
    outs = [jax.ShapeDtypeStruct((n, rows, width), BF) for rows in (image, text)]
    outs += [jax.ShapeDtypeStruct((n, 2, width), F32), jax.ShapeDtypeStruct((n, 4, 2 * hd), F32)]
    ins = [u[0], u[1], grads[0], grads[1]]
    pi, pt, sums, gain_sums = pl.pallas_call(
        functools.partial(attention_back_kernel, length=length, hd=hd, pairs=model // (2 * hd)),
        grid=(n,),
        in_specs=[whole_block(t) for t in ins] + [pl.BlockSpec(gains.shape, lambda i: (0, 0))],
        out_specs=[whole_block(t) for t in outs],
        out_shape=outs,
        name="attention_back",
    )(*ins, gains)
    gain = jnp.sum(gain_sums, 0)
    gain = (gain[:, :hd] + gain[:, hd:]).reshape(2, 2, hd)
    sums = jnp.sum(sums, 0)
    return [pi, pt], [sums[0], sums[1]], [gain[0], gain[1]]


def forward(x, mod, w, length):
    keep = {"x": x, "mod": mod}
    hidden, us = [], []
    for st in range(2):
        normed, _ = normalise(x[st].astype(F32))
        h = (normed * (1.0 + mod[:, st, 1][:, None]) + mod[:, st, 0][:, None]).astype(BF)
        h = gather_two(h)
        hidden.append(h)
        us.append(times(h, w["qkv"][st]) + w["b_qkv"][st])
    keep["hidden"], keep["u"] = hidden, us
    attended = attention(us, w["gain"], length)
    keep["attended"] = attended
    keep["branch"], keep["mixed"], keep["hidden_mlp"], keep["slope"], keep["act"], keep["mlp"] = [], [], [], [], [], []
    outs = []
    for st in range(2):
        branch = scatter_two(times(attended[st], w["out"][st])) + w["b_out"][st]
        mixed = x[st].astype(F32) + mod[:, st, 2][:, None] * branch
        normed, _ = normalise(mixed)
        h = (normed * (1.0 + mod[:, st, 4][:, None]) + mod[:, st, 3][:, None]).astype(BF)
        h = gather_four(h)
        pre = times(h, w["fc1"][st]) + w["b_fc1"][st]
        act, slope = gelu(pre)
        act, slope = act.astype(BF), slope.astype(BF)
        mlp = scatter_four(times(act, w["fc2"][st])) + w["b_fc2"][st]
        outs.append(mixed + mod[:, st, 5][:, None] * mlp)
        for name, value in (("branch", branch), ("mixed", mixed), ("hidden_mlp", h), ("slope", slope), ("act", act), ("mlp", mlp)):
            keep[name].append(value)
    return outs, keep


def backward_entry(up, keep):
    mod = keep["mod"]
    state = {"up": up, "mlp": [], "fc2": [], "gate": []}
    for st in range(2):
        mlp_grad = (mod[:, st, 5][:, None] * up[st]).astype(BF)
        state["fc2"].append(jnp.sum(mlp_grad.astype(F32), (0, 1)))
        state["gate"].append(jnp.sum(keep["mlp"][st] * up[st], 1))
        state["mlp"].append(gather_four(mlp_grad))
    return state


def backward_mlp(state, keep, w):
    mod = keep["mod"]
    state = dict(state, mixed_grad=[], late=[], pre=[], fc1=[])
    for st in range(2):
        act_grad = times_turned(state["mlp"][st], w["fc2"][st])
        pre_grad = (act_grad * keep["slope"][st].astype(F32)).astype(BF)
        state["fc1"].append(jnp.sum(pre_grad.astype(F32), (0, 1)))
        h_grad = scatter_four(times_turned(pre_grad, w["fc1"][st]))
        normed, inverse = normalise(keep["mixed"][st])
        back = normalise_back(h_grad * (1.0 + mod[:, st, 4][:, None]), normed, inverse)
        state["mixed_grad"].append(state["up"][st] + back)
        state["late"].append((jnp.sum(h_grad, 1), jnp.sum(h_grad * normed, 1), state["gate"][st]))
        state["pre"].append(pre_grad)
    return state


def backward_attention(state, keep, w, length):
    mod = keep["mod"]
    small = {"fc2": state["fc2"], "fc1": state["fc1"], "out": []}
    right = {"mlp": state["mlp"], "pre": state["pre"], "branch": []}
    attended_grads, gates = [], []
    for st in range(2):
        mixed_grad = state["mixed_grad"][st]
        branch_grad = (mod[:, st, 2][:, None] * mixed_grad).astype(BF)
        gates.append(jnp.sum(keep["branch"][st] * mixed_grad, 1))
        small["out"].append(jnp.sum(branch_grad.astype(F32), (0, 1)))
        branch_grad = gather_two(branch_grad)
        right["branch"].append(branch_grad)
        attended_grads.append(times_turned(branch_grad, w["out"][st]).astype(BF))
    right["qkv"], small["qkv"], small["gain"] = attention_back(attended_grads, keep["u"], w["gain"], length)
    input_grads, mod_grads = [], []
    for st in range(2):
        h_grad = scatter_two(times_turned(right["qkv"][st], w["qkv"][st]))
        normed, inverse = normalise(keep["x"][st].astype(F32))
        input_grads.append(
            state["mixed_grad"][st] + normalise_back(h_grad * (1.0 + mod[:, st, 1][:, None]), normed, inverse)
        )
        mod_grads.append(jnp.stack([jnp.sum(h_grad, 1), jnp.sum(h_grad * normed, 1), gates[st], *state["late"][st]], 1))
    return input_grads, jnp.stack(mod_grads, 1), small, right


def backward(up, keep, w, length):
    return backward_attention(backward_mlp(backward_entry(up, keep), keep, w), keep, w, length)


def place(pieces, slots, count):
    whole = jnp.zeros((count,) + pieces[0].shape, pieces[0].dtype)
    for piece, slot in zip(pieces, slots):
        whole = lax.dynamic_update_index_in_dim(whole, piece, slot, 0)
    return whole


def take(x, index, axis):
    return lax.dynamic_index_in_dim(x, index, axis, keepdims=False)


def column_blocks(x, blocks, groups, width, stream=None):
    streams, rows, _ = x.shape
    streams = streams if stream is None else 1
    per = len(blocks) // groups
    numbers = list(blocks) + [0 if stream is None else stream]

    def body(blocks_ref, x_ref, out_ref):
        out_ref[0] = x_ref[...]

    grid_spec = pltpu.PrefetchScalarGridSpec(
        num_scalar_prefetch=1,
        grid=(groups, per),
        in_specs=[pl.BlockSpec((streams, rows, width), lambda g, b, blocks: (blocks[len(numbers) - 1], 0, blocks[g * per + b]))],
        out_specs=pl.BlockSpec((1, streams, rows, width), lambda g, b, blocks: (g, 0, 0, b)),
    )
    out = jax.ShapeDtypeStruct((groups, streams, rows, per * width), x.dtype)
    table = jnp.stack(numbers).astype(jnp.int32)
    return pl.pallas_call(body, grid_spec=grid_spec, out_shape=out, name="column_blocks")(table, x)


def columns_back(x, numbers):
    groups, streams, rows, columns = x.shape
    per = len(numbers) // groups
    width = columns // per

    def body(numbers_ref, x_ref, out_ref):
        out_ref[...] = x_ref[0].astype(F32)

    grid_spec = pltpu.PrefetchScalarGridSpec(
        num_scalar_prefetch=1,
        grid=(groups, per),
        in_specs=[pl.BlockSpec((1, streams, rows, width), lambda g, b, numbers: (g, 0, 0, b))],
        out_specs=pl.BlockSpec((streams, rows, width), lambda g, b, numbers: (0, 0, numbers[g * per + b])),
    )
    out = jax.ShapeDtypeStruct((streams, rows, groups * columns), F32)
    table = jnp.stack(numbers).astype(jnp.int32)
    return pl.pallas_call(body, grid_spec=grid_spec, out_shape=out, name="columns_back")(table, x)


def interleave(own, other, core, blocks):
    streams, rows, columns = own.shape
    width = columns // blocks
    per = 2

    def body(core_ref, own_ref, other_ref, out_ref):
        ahead = core_ref[0] == 0
        a, b = own_ref[...].astype(F32), other_ref[...].astype(F32)
        first, second = jnp.where(ahead, a, b), jnp.where(ahead, b, a)
        for i in range(per):
            at = slice(i * width, (i + 1) * width)
            out_ref[:, :, 2 * i * width : (2 * i + 1) * width] = first[:, :, at]
            out_ref[:, :, (2 * i + 1) * width : (2 * i + 2) * width] = second[:, :, at]

    block = pl.BlockSpec((streams, rows, per * width), lambda i, core: (0, 0, i))
    grid_spec = pltpu.PrefetchScalarGridSpec(
        num_scalar_prefetch=1,
        grid=(blocks // per,),
        in_specs=[block, block],
        out_specs=pl.BlockSpec((streams, rows, 2 * per * width), lambda i, core: (0, 0, i)),
    )
    out = jax.ShapeDtypeStruct((streams, rows, 2 * columns), F32)
    return pl.pallas_call(body, grid_spec=grid_spec, out_shape=out, name="interleave")(core[None].astype(jnp.int32), own, other)


def assemble(pieces, count, rows, parity):
    arrays = []
    for st in range(2):
        whole = None
        for piece, relayed, slot, at in pieces:
            if relayed is None:
                block = piece[st]
            else:
                block = jnp.where(parity == st, piece, relayed)
            if whole is None:
                whole = jnp.zeros((count * rows, block.shape[1]), block.dtype)
            whole = lax.dynamic_update_slice_in_dim(whole, block, slot * rows + at, 0)
        arrays.append(whole)
    return arrays


def prepare(later, w_qkv, b_qkv, gain, w_out, b_out, w_fc1, b_fc1, w_fc2, b_fc2):
    sid = lax.axis_index("shard")
    core = sid % 2
    parity = lax.axis_index("replica") % 2
    rows, width = w_qkv.shape[1], w_qkv.shape[2]
    part = width // 12
    slots = (sid, sid ^ 1, sid ^ 2, sid ^ 3)

    def of_parity(x):
        return jnp.where(parity == 0, x[0], x[1])

    direct, relayed = [], []

    def fetch(send, x):
        x, _, _ = lax.optimization_barrier((x, direct[-1:], relayed[-3:-2]))
        direct.append(send(x))
        relayed.append(mate(direct[-1]))
        return direct[-1], relayed[-1]

    numbers = [j * 4 + h * 2 + (core if g == 0 else 1 - core) for g in range(2) for j in range(3) for h in range(2)]
    first = column_blocks(w_qkv, numbers[:6], 1, part, parity)[0, 0]
    vectors = (b_qkv, b_out, b_fc2, gain.reshape(2, -1))
    w_qkv, first, vectors, later = lax.optimization_barrier((w_qkv, first, vectors, later))
    packed = jnp.concatenate(vectors, 1)[None]
    opposite = far(packed)
    w_qkv, opposite = lax.optimization_barrier((w_qkv, opposite))
    second = column_blocks(w_qkv, numbers[6:], 1, part, parity)[0, 0]
    w_qkv, second = lax.optimization_barrier((w_qkv, second))
    theirs = column_blocks(w_qkv, numbers[6:], 1, part)[0]
    mine = column_blocks(w_qkv, numbers[:6], 1, part)[0]
    got = [fetch(far, first), fetch(across, second)]
    packed, opposite, _ = lax.optimization_barrier((packed, opposite, got[0][0]))
    packed = jnp.concatenate([packed, near(packed), opposite, near(opposite)], 0)
    w_out, w_fc1, packed = lax.optimization_barrier((w_out, w_fc1, packed))
    columns = w_fc1.shape[2] // 4
    away = [column_blocks(w_fc1, [slot], 1, columns, parity)[0, 0] for slot in slots[2:]]
    pieces = [(mine, None, slots[0], 0), (near(theirs), None, slots[1], 0)]
    pieces += [(*t, slots[2 + i], 0) for i, t in enumerate(got)]
    w = {"qkv": assemble(pieces, 4, rows, parity)}

    got = fetch(far, of_parity(w_out))
    pair = sid // 2
    w["out"] = assemble([(w_out, None, pair, 0), (*got, 1 - pair, 0)], 2, rows, parity)

    w_fc1, away, _ = lax.optimization_barrier((w_fc1, away, got[0]))
    blocks = [column_blocks(w_fc1, [slot], 1, columns)[0] for slot in slots[:2]]
    pieces = [(blocks[0], None, slots[0], 0), (near(blocks[1]), None, slots[1], 0)]
    pieces += [(*fetch(send, block), slot, 0) for send, block, slot in zip((far, across), away, slots[2:])]
    w["fc1"] = assemble(pieces, 4, rows, parity)
    w["fc2"] = [w_fc2[0], w_fc2[1]]

    packed = place([packed[j] for j in range(4)], slots, 4).astype(F32)
    flat, at = [], 0
    for vector in vectors:
        piece = packed[:, :, at : at + vector.shape[1]]
        at += vector.shape[1]
        flat.append(piece)
    b_qkv, b_out, b_fc2 = (jnp.concatenate([piece[j] for j in range(4)], 1) for piece in flat[:3])
    w["b_out"], w["b_fc2"], w["b_fc1"] = b_out, b_fc2, b_fc1.astype(F32)
    columns = [b_qkv[:, i * part : (i + 1) * part] for i in range(12)]
    w["b_qkv"] = jnp.where(core == 0, jnp.concatenate(columns[0::2], 1), jnp.concatenate(columns[1::2], 1))
    quarter = gain.shape[2]
    table = []
    for st in range(2):
        for j in range(2):
            row = [flat[3][i, st, j * quarter : (j + 1) * quarter] for i in range(4)]
            table.append(jnp.concatenate(row + row))
    w["gain"] = jnp.stack(table)
    return w, later


def weight_terms(left, right):
    total = None
    for a, b in zip(left, right):
        term = outer(a, b)
        total = term if total is None else total + term
    return total


def over_replicas(x, inner):
    return lax.psum_scatter(x, "replica", scatter_dimension=0, tiled=True).reshape(inner)


def rows_only(x):
    return x.reshape(-1, x.shape[-1])


def per_device(block_input, modulation, w_qkv, b_qkv, qk_gain, w_out, b_out, w_fc1, b_fc1, w_fc2, b_fc2, cotangent):
    section = lax.axis_index("section")
    first = section == 0
    sid = lax.axis_index("shard")
    core, row_pair = sid % 2, sid // 2
    count = lax.axis_size("replica")
    rid = lax.axis_index("replica")
    length = block_input.shape[2]
    padded = (length + 15) // 16 * 16
    later = (block_input, modulation, cotangent)
    w, (block_input, modulation, cotangent) = prepare(later, w_qkv[0], b_qkv[0], qk_gain[0], w_out[0], b_out[0], w_fc1[0], b_fc1[0], w_fc2[0], b_fc2[0])

    def padding(x):
        return jnp.pad(x, ((0, 0), (0, 0), (0, padded - length), (0, 0)))

    def streams(x):
        return list(split_rows(x))

    def choose(a, b):
        return jax.tree.map(lambda p, q: jnp.where(first, p, q), a, b)

    def relay(x, pairs):
        return [lax.ppermute(t.astype(BF), "section", pairs) for t in x]

    block_input = padding(block_input)
    cotangent = padding(cotangent)
    mod = modulation[0]
    middle_mod = jnp.where(first, mod[1], mod[0])
    up_pair, down_pair = [(0, 1)], [(1, 0)]

    out0, keep0 = forward(streams(block_input[0]), mod[0], w, length)
    out0, cotangent = lax.optimization_barrier((out0, cotangent))
    got = relay(out0, up_pair)
    out1, keep1 = forward(choose(streams(block_input[1]), got), middle_mod, w, length)
    got = relay(out1, up_pair)
    out2, keep2 = forward(got, mod[1], w, length)

    def zero_unless(cond, x):
        return [jnp.where(cond, t.astype(F32), 0.0) for t in x]

    grad0, mod_grad0, small0, right0 = backward(zero_unless(~first, streams(cotangent[0])), keep1, w, length)
    got = relay(grad0, down_pair)
    up = choose([t.astype(F32) for t in got], [t.astype(F32) for t in streams(cotangent[1])])
    keep_mid = choose(keep0, keep2)
    grad1, mod_grad1, small1, right1 = backward(up, keep_mid, w, length)
    got = relay(grad1, down_pair)
    last = backward_entry(zero_unless(first, got), keep1)

    def terms(left, early, late, st):
        return weight_terms((keep_mid[left][st], keep1[left][st]), (early[st], late[st])).astype(BF)

    mlp_ends = choose(last["mlp"], right0["mlp"])
    fc2 = [terms("act", right1["mlp"], mlp_ends, st) for st in range(2)]
    for st in range(2):
        last["mlp"][st], fc2[st] = lax.optimization_barrier((last["mlp"][st], fc2[st]))
    last = backward_mlp(last, keep1, w)
    pre_ends = choose(last["pre"], right0["pre"])
    fc1 = []
    for st in range(2):
        t = terms("hidden_mlp", right1["pre"], pre_ends, st)
        fc1.append(jnp.swapaxes(t.reshape(4, count, -1, t.shape[1]), 0, 1))
    fc1 = jnp.stack(fc1, 1)
    fc1_inner, fc1 = fc1.shape[1:], rows_only(fc1)
    last["mixed_grad"], fc1 = lax.optimization_barrier((last["mixed_grad"], fc1))
    fc2, fc1 = [over_replicas(t, (1, -1, t.shape[1])) for t in fc2], over_replicas(fc1, fc1_inner)
    grad2, mod_grad2, small2, right2 = backward_attention(last, keep1, w, length)
    right1["qkv"], right2["qkv"] = lax.optimization_barrier((right1["qkv"], right2["qkv"]))

    halves = []

    def over_far(t):
        t = t.reshape(2, -1, t.shape[1])
        sent, _ = lax.optimization_barrier((take(t, 1 - row_pair, 0), halves[-1:]))
        halves.append(far(sent))
        return (take(t, row_pair, 0).astype(F32) + halves[-1].astype(F32)).astype(BF)

    branch_ends, qkv_ends = choose(right2["branch"], right0["branch"]), choose(right2["qkv"], right0["qkv"])
    qkv, out = [], []
    for st in range(2):
        t = over_far(terms("attended", right1["branch"], branch_ends, st))
        out.append(t.reshape(count, -1, t.shape[1]))
        t = over_far(terms("hidden", right1["qkv"], qkv_ends, st))
        qkv.append(jnp.swapaxes(t.reshape(2, count, -1, t.shape[1]), 0, 1))
    out, qkv = jnp.stack(out, 1), jnp.stack(qkv, 1)
    out_inner, qkv_inner = out.shape[1:], qkv.shape[1:]
    out, fc2, fc1 = lax.optimization_barrier((rows_only(out), fc2, fc1))
    out = over_replicas(out, out_inner)
    qkv, out = lax.optimization_barrier((rows_only(qkv), out))
    qkv = over_replicas(qkv, qkv_inner)
    out = out.astype(F32)
    fc2 = jnp.concatenate(fc2, 0).astype(F32)
    slots = [sid ^ j for j in range(4)]
    moved = []
    for j, send in ((0, lambda x: x), (1, near), (2, far), (3, across)):
        moved.append(send(take(fc1, slots[j], 1)))
    fc1 = columns_back(jnp.stack(moved), slots)

    small = jax.tree.map(lambda a, b, c: a + b + c, small0, small1, small2)
    pieces = []
    for st in range(2):
        cores = small["qkv"][st].reshape(6, 1, -1)
        cores = jnp.where(jnp.arange(2).reshape(1, 2, 1) == core, cores, 0.0).reshape(-1)
        quarter = small["fc1"][st].reshape(1, -1)
        quarter = jnp.where(jnp.arange(4).reshape(4, 1) == sid, quarter, 0.0).reshape(-1)
        pieces.append(jnp.concatenate([cores, small["out"][st], quarter, small["fc2"][st], small["gain"][st].reshape(-1)]))
    sizes = [w_qkv.shape[3], w_out.shape[3], w_fc1.shape[3], w_fc2.shape[3], w["gain"].shape[-1]]
    summed = total_of(jnp.stack(pieces), ("shard", "replica"))
    place_id = sid * count + rid
    vectors, at = [], 0
    for size in sizes:
        vectors.append(summed[:, at : at + size])
        at += size

    def own_block(x, axis):
        size = x.shape[axis] // (4 * count)
        return lax.dynamic_slice_in_dim(x, place_id * size, size, axis)

    blocks = [own_block(v, 1)[None] for v in vectors[:4]]
    gain = own_block(vectors[4].reshape(2, 2, -1), 2)[None]

    def joined(x):
        return jnp.concatenate(x, 1)[:, :length]

    activations = jnp.stack([joined(choose(out0, out1)), joined(choose(out1, out2))]).astype(BF)
    input_grads = jnp.stack([joined(choose(grad1, grad0)), joined(choose(grad2, grad1))])
    modulation_grad = jnp.stack([choose(mod_grad1, mod_grad0), choose(mod_grad2, mod_grad1)])
    others = (activations, input_grads, modulation_grad, blocks, gain, out, fc1, fc2)
    others, qkv = lax.optimization_barrier((others, qkv))
    activations, input_grads, modulation_grad, blocks, gain, out, fc1, fc2 = others
    qkv = interleave(take(qkv, core, 1), near(take(qkv, 1 - core, 1)), core, 6)
    return (
        activations[None],
        input_grads[None],
        modulation_grad[None],
        qkv[None],
        blocks[0],
        gain,
        out[None],
        blocks[1],
        fc1[None],
        blocks[2],
        fc2[None],
        blocks[3],
    )


def solution(mesh):
    every = ("shard", "replica")
    return jax.shard_map(
        per_device,
        mesh=mesh,
        in_specs=(
            P(None, every, None, None),
            P("section", None, every, None, None, None),
            P("section", None, "shard", None),
            P("section", None, "shard"),
            P("section", None, None, "shard"),
            P("section", None, "shard", None),
            P("section", None, "shard"),
            P("section", None, "shard", None),
            P("section", None, "shard"),
            P("section", None, "shard", None),
            P("section", None, "shard"),
            P(None, every, None, None),
        ),
        out_specs=(
            P("section", None, every, None, None),
            P("section", None, every, None, None),
            P("section", None, every, None, None, None),
            P("section", None, every, None),
            P("section", None, every),
            P("section", None, None, every),
            P("section", None, every, None),
            P("section", None, every),
            P("section", None, every, None),
            P("section", None, every),
            P("section", None, every, None),
            P("section", None, every),
        ),
        check_vma=False,
    )
```
